256 devices in a mesh: radius: 16 (over z, core), polar: 4 (over x), group: 4 (over y).
Axes of the slice: x: 4, y: 4, z: 8, core: 2. Of those that a mesh axis runs over, the one named last changes fastest.
Arguments:
- density: float32 [768, 1024], P('radius', 'polar'), may hold values from 0.3 to 3
- opacity: bfloat16 [64, 768, 1024], P('group', 'radius', 'polar'), may hold values from 0.049804688 to 5
- radiation_old: float32 [64, 768, 1024], P('group', 'radius', 'polar'), may hold values from 0.5 to 2
- material_old: float32 [768, 1024], P('radius', 'polar'), may hold values from 0.5 to 2
- weights: float32 [64], P('group'), may hold values from 0.5 to 2
- stellar_flux: float32 [768], P('radius'), may hold values from 10 to 100
Outputs:
- energy: float32 [64, 768, 1024], P('group', 'radius', 'polar')
- material_now: float32 [768, 1024], P('radius', 'polar')
- column: float32 [768, 1024], P('radius', 'polar')
The draws below stay inside these ranges and needn't reach their ends.
All inputs are finite; a program needn't handle non-finite values.
Results may differ from the reference program's by a relative error of at most 0.0003.
Values sent between devices are 32-bit elements; how exact they have to be, the bound alone decides.
No kernel may reach another device: no remote copies, remote signals or barrier semaphores. Data moves between devices by JAX's collectives and lax.ppermute only.
A program may use at most 64 MiB of HBM per device.

```python
import math
import jax
import jax.numpy as jnp
from jax import lax

G = 64
ITERS = 3
SWEEPS = 2
NR = 768
NT = 1024


def block_levels(stream_key, shape, cuts, least, top_value):
    factor_of, own = 1.0, jax.random.fold_in(stream_key, 6)
    for position, blocks in cuts:
        draws = jnp.exp(jax.random.uniform(jax.random.fold_in(own, position), (blocks,), jnp.float32, least / len(cuts), top_value / len(cuts)))
        factor_of = factor_of * jnp.repeat(draws, shape[position] // blocks).reshape([-1 if axis == position else 1 for axis in range(len(shape))])
    return factor_of


def setup_inputs(seed: int = 0) -> dict:
    key_of = jax.random.split(jax.random.key(seed), 7)
    density = jnp.clip(jnp.exp(math.log(3.0) - 2.3025851 * jax.random.uniform(key_of[0], (NR, NT), jnp.float32) ** block_levels(key_of[0], (NR, NT), ((0, 16), (1, 4)), -0.2, 0.2)), 0.3, 3.0)
    opacity = jnp.clip(jnp.exp(math.log(5.0) - 4.609084 * jax.random.uniform(key_of[1], (G, NR, NT), jnp.float32) ** block_levels(key_of[1], (G, NR, NT), ((0, 4), (1, 16), (2, 4)), -0.2, 0.2)), 0.049804688, 5.0).astype(jnp.bfloat16)
    radiation_old = jnp.clip(0.5 + 1.5 * jax.random.uniform(key_of[2], (G, NR, NT), jnp.float32) ** block_levels(key_of[2], (G, NR, NT), ((0, 4), (1, 16), (2, 4)), -0.2, 0.2), 0.5, 2.0)
    material_old = jnp.clip(0.5 + 1.5 * jax.random.uniform(key_of[3], (NR, NT), jnp.float32) ** block_levels(key_of[3], (NR, NT), ((0, 16), (1, 4)), -0.2, 0.2), 0.5, 2.0)
    weights = jnp.clip(jnp.exp(math.log(2.0) - 1.3862944 * jax.random.uniform(key_of[4], (G,), jnp.float32) ** block_levels(key_of[4], (G,), ((0, 4),), -0.2, 0.2)), 0.5, 2.0)
    stellar_flux = jnp.clip(jnp.exp(math.log(100.0) - 2.3025851 * jax.random.uniform(key_of[5], (NR,), jnp.float32) ** block_levels(key_of[5], (NR,), ((0, 16),), -0.2, 0.2)), 10.0, 100.0)
    return dict(density=density, opacity=opacity, radiation_old=radiation_old, material_old=material_old, weights=weights, stellar_flux=stellar_flux)


def harmonic(lower_value, upper_value):
    return 2.0 * lower_value * upper_value / (lower_value + upper_value)

def limited_diffusion(old_field, absorb):
    padded = jnp.pad(old_field, 1)
    radial_slope = 0.5 * (padded[2:, 1:-1] - padded[:-2, 1:-1])
    polar_slope = 0.5 * (padded[1:-1, 2:] - padded[1:-1, :-2])
    ratio_value = jnp.sqrt(radial_slope * radial_slope + polar_slope * polar_slope) / (absorb * old_field)
    limiter = (2.0 + ratio_value) / (6.0 + 3.0 * ratio_value + ratio_value * ratio_value)
    return limiter / absorb

def face_terms(diffusion):
    padded = jnp.pad(diffusion, 1)
    return (harmonic(diffusion, padded[2:, 1:-1]), harmonic(padded[:-2, 1:-1], diffusion), harmonic(diffusion, padded[1:-1, 2:]), harmonic(padded[1:-1, :-2], diffusion))

def apply_operator(field, absorb, face_coeffs):
    padded = jnp.pad(field, 1)
    return (1.0 + absorb) * field + face_coeffs[0] * (field - padded[2:, 1:-1]) + face_coeffs[1] * (field - padded[:-2, 1:-1]) + face_coeffs[2] * (field - padded[1:-1, 2:]) + face_coeffs[3] * (field - padded[1:-1, :-2])

def solve_group(energy, residual, absorb, face_coeffs):
    norm_now = jnp.sum(residual * residual)
    direction = residual
    for sweep_index in range(SWEEPS):
        applied = apply_operator(direction, absorb, face_coeffs)
        step_size = norm_now / jnp.sum(direction * applied)
        energy = energy + step_size * direction
        residual = residual - step_size * applied
        if sweep_index + 1 < SWEEPS:
            norm_next = jnp.sum(residual * residual)
            direction = residual + norm_next / norm_now * direction
            norm_now = norm_next
    return (energy, residual)

def reference(density, opacity, radiation_old, material_old, weights, stellar_flux):
    column = 2.0 / NT * jnp.cumsum(density, axis=1)
    heating = stellar_flux[:, None] * density * jnp.exp(-column)

    def emission_term(running, group_item):
        opacity_row, weight = group_item
        return (running + opacity_row.astype(jnp.float32) * density * weight, None)
    emission, _ = lax.scan(emission_term, jnp.zeros_like(density), (opacity, weights))
    capacity = 16.0 * density + emission
    energy = radiation_old
    residual = radiation_old
    material_now = material_old
    material_prev = material_old
    for round_index in range(ITERS):

        def group_step(running, group_item):
            opacity_row, old_field, weight, energy_row, residual_row = group_item
            absorb = opacity_row.astype(jnp.float32) * density
            face_coeffs = face_terms(limited_diffusion(old_field, absorb))
            if round_index == 0:
                residual_row = absorb * weight * material_old + old_field - apply_operator(old_field, absorb, face_coeffs)
            else:
                residual_row = residual_row + absorb * weight * (material_now - material_prev)
            energy_row, residual_row = solve_group(energy_row, residual_row, absorb, face_coeffs)
            return (running + absorb * energy_row, (energy_row, residual_row))
        absorbed, (energy, residual) = lax.scan(group_step, jnp.zeros_like(density), (opacity, radiation_old, weights, energy, residual))
        material_next = (16.0 * density * material_old + heating + absorbed) / capacity
        material_prev = material_now
        material_now = material_next
    return (energy, material_now, column)
```

```python
import functools
import jax
import jax.numpy as jnp
from jax import lax
from jax.experimental import pallas as pl
from jax.experimental.pallas import tpu as pltpu
from jax.sharding import PartitionSpec as P

ITERS = 3
HALO = 8
LANES = 128
VMEM_LIMIT = 12 * 1024 * 1024
HIGHEST = lax.Precision.HIGHEST


def vspec():
    return pl.BlockSpec(memory_space=pltpu.VMEM)


def sspec():
    return pl.BlockSpec(memory_space=pltpu.SMEM)


def call(kernel, outs, args, specs, scratch=(), flops=1000000, nbytes=1000000, name=None):
    return pl.pallas_call(
        kernel,
        out_shape=[jax.ShapeDtypeStruct(s, jnp.float32) for s in outs],
        in_specs=specs,
        out_specs=[vspec() for _ in outs],
        scratch_shapes=list(scratch),
        compiler_params=pltpu.CompilerParams(vmem_limit_bytes=VMEM_LIMIT),
        cost_estimate=pl.CostEstimate(flops=flops, bytes_accessed=nbytes, transcendentals=0),
        name=name,
    )(*args)


def pack_rows_kernel(groups, rows, opacity, old, density, material, flux, up, down):
    for out, lo in ((up, 0), (down, rows - HALO)):
        base = (lo // 16) * 16
        dens = density[lo : lo + HALO, :]
        for g in range(groups):
            part = opacity[g, base : base + 16, :].astype(jnp.float32)
            out[g] = part[lo - base : lo - base + HALO, :] * dens
            out[groups + g] = old[g, lo : lo + HALO, :]
        out[2 * groups] = dens
        out[2 * groups + 1] = material[lo : lo + HALO, :]
        out[2 * groups + 2] = jnp.broadcast_to(flux[lo : lo + HALO, :], dens.shape)


def pack_columns_kernel(groups, rows, cols, opacity, old, density, material, top, bottom, left, right):
    full = rows + 2 * HALO
    lane = lax.broadcasted_iota(jnp.int32, (full, LANES), 1)
    for out, lo, edge in ((left, 0, 0), (right, cols - LANES, LANES - HALO)):
        hi = lo + LANES

        def tile(plane, own):
            return jnp.concatenate([top[plane, :, lo:hi], own, bottom[plane, :, lo:hi]], axis=0)

        packed_a = jnp.zeros((full, LANES), jnp.float32)
        packed_e = jnp.zeros((full, LANES), jnp.float32)
        dens = density[:, lo:hi]
        for g in range(groups):
            mine = (lane >= HALO * g) & (lane < HALO * (g + 1))
            shift = (HALO * g - edge) % LANES
            a = tile(g, opacity[g, :, lo:hi].astype(jnp.float32) * dens)
            e = tile(groups + g, old[g, :, lo:hi])
            if shift:
                a = pltpu.roll(a, shift, 1)
                e = pltpu.roll(e, shift, 1)
            packed_a = jnp.where(mine, a, packed_a)
            packed_e = jnp.where(mine, e, packed_e)
        out[0] = packed_a
        out[1] = packed_e
        d = tile(2 * groups, dens)
        m = tile(2 * groups + 1, material[:, lo:hi])
        d = pltpu.roll(d, (-edge) % LANES, 1) if edge else d
        m = pltpu.roll(m, (HALO - edge) % LANES, 1)
        out[2] = jnp.where(lane < HALO, d, jnp.where(lane < 2 * HALO, m, 0.0))


def next_row(v):
    return pltpu.roll(v, v.shape[0] - 1, 0)


def prev_row(v):
    return pltpu.roll(v, 1, 0)


def next_col(v):
    return pltpu.roll(v, v.shape[1] - 1, 1)


def prev_col(v):
    return pltpu.roll(v, 1, 1)


def flux_sum(v, face_r, face_p):
    fr = face_r * (v - next_row(v))
    fp = face_p * (v - next_col(v))
    return fr - prev_row(fr) + fp - prev_col(fp)


def harmonic(a, b):
    return 2.0 * a * b / jnp.maximum(a + b, 1e-30)


def own_sum(v, rows, cols):
    own = v[HALO : HALO + rows, :cols]
    acc = own[:, :LANES]
    for lo in range(LANES, cols, LANES):
        acc = acc + own[:, lo : lo + LANES]
    return jnp.sum(acc, axis=0, keepdims=True)


def krylov(g, groups, rows, cols, r, a, face_r, face_p, r_ref, q_ref, t_ref, mom):
    q = r + a * r + flux_sum(r, face_r, face_p)
    r_ref[g] = r
    q_ref[g] = q
    mom[pl.ds(g, 1), :] = own_sum(r * r, rows, cols)
    mom[pl.ds(groups + g, 1), :] = own_sum(r * q, rows, cols)
    mom[pl.ds(2 * groups + g, 1), :] = own_sum(q * q, rows, cols)
    t = q + a * q + flux_sum(q, face_r, face_p)
    if t_ref is not None:
        t_ref[g] = t
    mom[pl.ds(3 * groups + g, 1), :] = own_sum(q * t, rows, cols)


def broadcast_moments(mom, out):
    out[...] = lax.dot_general(
        jnp.ones((out.shape[0], LANES), jnp.float32),
        mom[...],
        (((1,), (1,)), ((), ())),
        precision=HIGHEST,
        preferred_element_type=jnp.float32,
    )


def start_kernel(
    groups, rows, cols,
    weights, opacity, old, density, material, flux, top, bottom, left, right,
    a_ref, e_ref, fr_ref, fp_ref, r_ref, q_ref, t_ref, dens_ref, mat_ref, flux_ref, emit_ref, out,
    mom,
):
    full, wide = a_ref.shape[1:]
    lane = lax.broadcasted_iota(jnp.int32, (full, LANES), 1)
    at_right = lane < HALO
    at_left = lane >= LANES - HALO

    def halo_tile(plane, shift_right, shift_left):
        from_right = pltpu.roll(right[plane], shift_right, 1)
        from_left = pltpu.roll(left[plane], shift_left, 1)
        return jnp.where(at_right, from_right, jnp.where(at_left, from_left, 0.0))

    def field(own, plane, tile):
        inner = jnp.concatenate([top[plane], own, bottom[plane]], axis=0)
        return jnp.concatenate([inner, tile], axis=1)

    dens = field(density[...], 2 * groups, halo_tile(2, 0, LANES - HALO))
    mat = field(material[...], 2 * groups + 1, halo_tile(2, LANES - HALO, LANES - 2 * HALO))
    valid = dens > 0.0
    dens_ref[...] = dens
    mat_ref[...] = mat
    flux_ref[0:HALO, :] = top[2 * groups + 2][:, :LANES]
    flux_ref[HALO : HALO + rows, :] = jnp.broadcast_to(flux[...], (rows, LANES))
    flux_ref[HALO + rows :, :] = bottom[2 * groups + 2][:, :LANES]
    partial = dens[:, :LANES]
    for lo in range(LANES, cols, LANES):
        partial = partial + dens[:, lo : lo + LANES]
    mom[4 * groups : 4 * groups + full, :] = partial

    def one(g, emit):
        shift_right = lax.rem(LANES - HALO * g, LANES)
        shift_left = lax.rem(2 * LANES - HALO - HALO * g, LANES)
        own = opacity[g].astype(jnp.float32) * density[...]
        a = field(own, g, halo_tile(0, shift_right, shift_left))
        e = field(old[g], groups + g, halo_tile(1, shift_right, shift_left))
        a = jnp.where(valid, a, 1.0)
        a_ref[g] = a
        e_ref[g] = e
        w = weights[g]
        emit = emit + a * w
        slope_r = 0.5 * (next_row(e) - prev_row(e))
        slope_p = 0.5 * (next_col(e) - prev_col(e))
        n = jnp.sqrt(slope_r * slope_r + slope_p * slope_p)
        u = a * e
        s = 2.0 * u + n
        d = jnp.where(valid, e * s / (n * n + 3.0 * u * s), 0.0)
        face_r = harmonic(d, next_row(d))
        face_p = harmonic(d, next_col(d))
        fr_ref[g] = face_r
        fp_ref[g] = face_p
        r = a * (w * mat - e) - flux_sum(e, face_r, face_p)
        krylov(g, groups, rows, cols, r, a, face_r, face_p, r_ref, q_ref, t_ref, mom)
        return emit

    emit_ref[...] = lax.fori_loop(0, groups, one, jnp.zeros((full, wide), jnp.float32))
    broadcast_moments(mom, out)


def steps(groups, gathered):
    total = jnp.sum(gathered[...], axis=0, keepdims=True)
    lane = lax.broadcasted_iota(jnp.int32, (groups, LANES), 1)
    sub = lax.broadcasted_iota(jnp.int32, (groups, LANES), 0)
    m0, m1, m2, m3 = (
        jnp.sum(jnp.where(lane == sub + k * groups, total, 0.0), axis=1, keepdims=True)
        for k in range(4)
    )
    k1, k2, k3 = m1 / m0, m2 / m0, m3 / m0
    first = 1.0 / k1
    det = k2 - k1 * k1
    beta = jnp.maximum(det, 0.0) / (k1 * k1)
    low = k1 * k3 - k2 * k2
    second = jnp.where(low > 0.0, k1 * jnp.maximum(det, 0.0) / low, 0.0)
    second = jnp.minimum(second, 1.0)
    return first + second * (1.0 + beta), first * second


def update_kernel(groups, gathered, a_ref, e_ref, r_ref, q_ref, e_out, s_out, c1_ref, c2_ref):
    c1, c2 = steps(groups, gathered)
    wide = a_ref.shape[2]
    c1_ref[...] = jnp.broadcast_to(c1, (groups, wide))
    c2_ref[...] = jnp.broadcast_to(c2, (groups, wide))

    def one(g, total):
        e = e_ref[g] + c1_ref[pl.ds(g, 1), :] * r_ref[g] - c2_ref[pl.ds(g, 1), :] * q_ref[g]
        e_out[g] = e
        return total + a_ref[g] * e

    s_out[...] = lax.fori_loop(0, groups, one, jnp.zeros(s_out.shape, jnp.float32))


def last_update_kernel(groups, rows, cols, gathered, a_ref, e_ref, r_ref, q_ref, e_out, s_out, c1_ref, c2_ref):
    c1, c2 = steps(groups, gathered)
    c1_ref[...] = jnp.broadcast_to(c1, (groups, cols))
    c2_ref[...] = jnp.broadcast_to(c2, (groups, cols))

    def one(g, total):
        here = (g, slice(HALO, HALO + rows), slice(0, cols))
        e = e_ref[here] + c1_ref[pl.ds(g, 1), :] * r_ref[here] - c2_ref[pl.ds(g, 1), :] * q_ref[here]
        e_out[g] = e
        return total + a_ref[here] * e

    s_out[...] = lax.fori_loop(0, groups, one, jnp.zeros((rows, cols), jnp.float32))


def heating_kernel(groups, rows, cols, polar_count, polar_total, place, gathered, dens_ref, flux_ref, mat_ref, column_out, fixed_out):
    full, wide = dens_ref.shape
    radius, polar = place[0], place[1]
    dens = dens_ref[...]
    count = gathered.shape[0]
    row_id = lax.broadcasted_iota(jnp.int32, (count, LANES), 0)
    ahead = (row_id >= radius * polar_count) & (row_id < radius * polar_count + polar)
    carried = jnp.sum(jnp.where(ahead, gathered[...], 0.0), axis=0, keepdims=True)
    lane = lax.broadcasted_iota(jnp.int32, (full, LANES), 1)
    sub = lax.broadcasted_iota(jnp.int32, (full, LANES), 0)
    carried = jnp.sum(jnp.where(lane == sub + 4 * groups, carried, 0.0), axis=1, keepdims=True)
    src = lax.broadcasted_iota(jnp.int32, (wide, wide), 0)
    dst = lax.broadcasted_iota(jnp.int32, (wide, wide), 1)
    middle = cols + LANES // 2
    ahead_of = (dst < middle) & (src <= dst)
    behind = (dst >= middle) & (src > dst)
    coeff = jnp.where(ahead_of, 1.0, jnp.where(behind, -1.0, 0.0))
    within = lax.dot_general(
        dens, coeff, (((1,), (0,)), ((), ())), precision=HIGHEST, preferred_element_type=jnp.float32
    )
    column = 2.0 / polar_total * (carried + within)
    column_out[...] = column[HALO : HALO + rows, :cols]
    flux = jnp.concatenate([flux_ref[...]] * (wide // LANES), axis=1)
    fixed_out[...] = 16.0 * dens * mat_ref[...] + flux * dens * jnp.exp(-column)


def next_kernel(
    groups, rows, cols, count, last,
    weights, c1_ref, c2_ref, a_ref, fr_ref, fp_ref, r_in, q_in, t_in,
    fixed, capacity, mat_ref, *rest,
):
    sums = rest[:count]
    r_ref, q_ref, t_ref, m_ref, out, delta_ref, mom = rest[count:]
    total = sums[0][...]
    for s in sums[1:]:
        total = total + s[...]
    nxt = (fixed[...] + total) / capacity[...]
    m_ref[...] = nxt
    delta_ref[...] = nxt - mat_ref[...]

    def one(g, carry):
        a = a_ref[g]
        r = (
            r_in[g]
            - c1_ref[pl.ds(g, 1), :] * q_in[g]
            + c2_ref[pl.ds(g, 1), :] * t_in[g]
            + a * (weights[g] * delta_ref[...])
        )
        krylov(g, groups, rows, cols, r, a, fr_ref[g], fp_ref[g], r_ref, q_ref, None if last else t_ref, mom)
        return carry

    mom[4 * groups :, :] = jnp.zeros((mom.shape[0] - 4 * groups, LANES), jnp.float32)
    lax.fori_loop(0, groups, one, 0)
    broadcast_moments(mom, out)


def capacity_kernel(count, dens_ref, *rest):
    sums = rest[:count]
    out = rest[count]
    total = sums[0][...]
    for s in sums[1:]:
        total = total + s[...]
    dens = dens_ref[...]
    out[...] = 16.0 * jnp.where(dens > 0.0, dens, 1.0) + total


def material_kernel(count, rows, cols, fixed, capacity, *rest):
    sums = rest[:count]
    out = rest[count]
    total = sums[0][...]
    for s in sums[1:]:
        total = total + s[...]
    here = (slice(HALO, HALO + rows), slice(0, cols))
    out[...] = (fixed[here] + total) / capacity[here]


def spread(part, axis):
    count = lax.axis_size(axis)
    return [part] + [
        lax.ppermute(part, axis, [(i, (i + s) % count) for i in range(count)]) for s in range(1, count)
    ]


def shifted(upward, downward, axis):
    count = lax.axis_size(axis)
    from_lower = lax.ppermute(downward, axis, [(i, i + 1) for i in range(count - 1)])
    from_upper = lax.ppermute(upward, axis, [(i + 1, i) for i in range(count - 1)])
    return from_lower, from_upper


def per_device(density, opacity, radiation_old, material_old, weights, stellar_flux):
    groups, rows, cols = opacity.shape
    full, wide = rows + 2 * HALO, cols + LANES
    polar_count = lax.axis_size("polar")
    group_count = lax.axis_size("group")
    devices = lax.axis_size("radius") * polar_count
    place = jnp.stack([lax.axis_index("radius"), lax.axis_index("polar")]).astype(jnp.int32)
    flux = stellar_flux[:, None]
    planes = 2 * groups + 3
    big = (groups, full, wide)
    flat = (full, wide)

    up, down = call(
        functools.partial(pack_rows_kernel, groups, rows),
        [(planes, HALO, cols)] * 2,
        (opacity, radiation_old, density, material_old, flux),
        [vspec()] * 5,
        name="pack_rows",
    )
    top, bottom = shifted(up, down, "radius")
    to_left, to_right = call(
        functools.partial(pack_columns_kernel, groups, rows, cols),
        [(3, full, LANES)] * 2,
        (opacity, radiation_old, density, material_old, top, bottom),
        [vspec()] * 6,
        name="pack_columns",
    )
    left, right = shifted(to_left, to_right, "polar")
    a, e, fr, fp, r, q, t, dens, mat, flux_rows, emit, out = call(
        functools.partial(start_kernel, groups, rows, cols),
        [big] * 7 + [flat, flat, (full, LANES), flat, (devices, LANES)],
        (weights, opacity, radiation_old, density, material_old, flux, top, bottom, left, right),
        [sspec()] + [vspec()] * 9,
        scratch=[pltpu.VMEM((LANES, LANES), jnp.float32)],
        name="start",
    )
    for turn in range(ITERS):
        gathered = lax.all_to_all(out, ("radius", "polar"), 0, 0, tiled=True)
        if turn + 1 == ITERS:
            e, part = call(
                functools.partial(last_update_kernel, groups, rows, cols),
                [(groups, rows, cols), (rows, cols)],
                (gathered, a, e, r, q),
                [vspec()] * 5,
                scratch=[pltpu.VMEM((groups, cols), jnp.float32)] * 2,
                name="last_update",
            )
            sums = spread(part, "group")
            (mat,) = call(
                functools.partial(material_kernel, group_count, rows, cols),
                [(rows, cols)],
                (fixed, capacity, *sums),
                [vspec()] * (2 + group_count),
                name="material",
            )
            break
        e, part, c1, c2 = call(
            functools.partial(update_kernel, groups),
            [big, flat, (groups, wide), (groups, wide)],
            (gathered, a, e, r, q),
            [vspec()] * 5,
            name="update",
        )
        sums = spread(part, "group")
        if turn == 0:
            emits = spread(emit, "group")
            column, fixed = call(
                functools.partial(heating_kernel, groups, rows, cols, polar_count, cols * polar_count),
                [(rows, cols), flat],
                (place, gathered, dens, flux_rows, mat),
                [sspec()] + [vspec()] * 4,
                name="heating",
            )
            (capacity,) = call(
                functools.partial(capacity_kernel, group_count),
                [flat],
                (dens, *emits),
                [vspec()] * (1 + group_count),
                name="capacity",
            )
        r, q, t, mat, out = call(
            functools.partial(next_kernel, groups, rows, cols, group_count, turn + 2 == ITERS),
            [big] * 3 + [flat, (devices, LANES)],
            (weights, c1, c2, a, fr, fp, r, q, t, fixed, capacity, mat, *sums),
            [sspec()] + [vspec()] * (11 + group_count),
            scratch=[pltpu.VMEM(flat, jnp.float32), pltpu.VMEM((LANES, LANES), jnp.float32)],
            name="next",
        )
    return (e, mat, column)


def solution(mesh):
    return jax.shard_map(
        per_device,
        mesh=mesh,
        in_specs=(
            P("radius", "polar"),
            P("group", "radius", "polar"),
            P("group", "radius", "polar"),
            P("radius", "polar"),
            P("group"),
            P("radius"),
        ),
        out_specs=(P("group", "radius", "polar"), P("radius", "polar"), P("radius", "polar")),
        check_vma=False,
    )
```

```python
import functools
import jax
import jax.numpy as jnp
from jax import lax
from jax.experimental import pallas as pl
from jax.experimental.pallas import tpu as pltpu
from jax.sharding import PartitionSpec as P


ITERS = 3
HALO = 8
LANES = 128
HALF = LANES // 2
STEP = 64
VMEM_LIMIT = 12 * 1024 * 1024
HIGHEST = lax.Precision.HIGHEST
OUTSIDE = 1.6e38


def vspec():
    return pl.BlockSpec(memory_space=pltpu.VMEM)


def sspec():
    return pl.BlockSpec(memory_space=pltpu.SMEM)


def hspec():
    return pl.BlockSpec(memory_space=pl.ANY)


def call(kernel, outs, args, specs, scratch=(), flops=1000000, nbytes=1000000, name=None):
    return pl.pallas_call(
        kernel,
        out_shape=[jax.ShapeDtypeStruct(s, jnp.float32) for s in outs],
        in_specs=specs,
        out_specs=[vspec() for _ in outs],
        scratch_shapes=list(scratch),
        compiler_params=pltpu.CompilerParams(vmem_limit_bytes=VMEM_LIMIT),
        cost_estimate=pl.CostEstimate(flops=flops, bytes_accessed=nbytes, transcendentals=0),
        name=name,
    )(*args)


def lane_of(height=1):
    return lax.broadcasted_iota(jnp.int32, (height, LANES), 1)


def pieces(tall):
    cuts = [0, HALO]
    while cuts[-1] + STEP < tall - HALO:
        cuts.append(cuts[-1] + STEP)
    cuts += [tall - HALO, tall]
    return list(zip(cuts[:-1], cuts[1:]))


def pack_rows_kernel(groups, rows, flux, opacity, old, density, material, up, down, *scratch):
    copies = []
    sems = scratch[-1]
    for side, (lo, base) in enumerate(((0, 0), (rows - HALO, rows - 2 * HALO))):
        op_buf, old_buf, dens_buf, mat_buf = scratch[4 * side : 4 * side + 4]
        pairs = (
            (opacity.at[:, pl.ds(base, 2 * HALO), :], op_buf),
            (old.at[:, pl.ds(lo, HALO), :], old_buf),
            (density.at[pl.ds(lo, HALO), :], dens_buf),
            (material.at[pl.ds(lo, HALO), :], mat_buf),
        )
        for k, (src, dst) in enumerate(pairs):
            copies.append(pltpu.make_async_copy(src, dst, sems.at[4 * side + k]))
    for c in copies:
        c.start()
    for c in copies:
        c.wait()
    lane = lane_of(HALO)
    for side, (out, lo, inside, first) in enumerate(
        ((up, 0, 0, rows + HALO), (down, rows - HALO, HALO, 0))
    ):
        op_buf, old_buf, dens_buf, mat_buf = scratch[4 * side : 4 * side + 4]
        dens = dens_buf[...]
        for g in range(groups):
            out[g] = op_buf[g].astype(jnp.float32)[inside : inside + HALO, :] * dens
            out[groups + g] = old_buf[g]
        out[2 * groups] = dens
        out[2 * groups + 1] = mat_buf[...]
        vec = jnp.zeros((HALO, LANES), jnp.float32)
        for i in range(HALO):
            vec = jnp.where(lane % HALF == first + i, flux[lo + i], vec)
        out[2 * groups + 2, :, :LANES] = vec
        for at in range(LANES, out.shape[2], LANES):
            out[2 * groups + 2, :, at : at + LANES] = vec


def turn_kernel(
    groups, rows, cols, opacity, old, density, material, top, bottom,
    a_ref, e_ref, dens_ref, mat_ref, flux_ref, to_left, to_right,
):
    pairs = groups // 2
    flux_ref[...] = top[2 * groups + 2, :, :LANES] + bottom[2 * groups + 2, :, :LANES]
    for lo in range(0, cols, LANES):
        hi = lo + LANES

        def tile(plane, own):
            return jnp.concatenate([top[plane, :, lo:hi], own, bottom[plane, :, lo:hi]], axis=0)

        d = tile(2 * groups, density[:, lo:hi])
        d = jnp.concatenate([d, d], axis=0).T
        m = tile(2 * groups + 1, material[:, lo:hi])
        m = jnp.concatenate([m, m], axis=0).T
        dens_ref[lo:hi, :] = d
        mat_ref[lo:hi, :] = m

        def one(p, carry):
            both = []
            for h in range(2):
                g = 2 * p + h
                both.append(tile(g, opacity[g, :, lo:hi].astype(jnp.float32) * density[:, lo:hi]))
            a = jnp.concatenate(both, axis=0).T
            a_ref[p, lo:hi, :] = jnp.where(dens_ref[lo:hi, :] > 0.0, a, 1.0)
            both = [tile(groups + 2 * p + h, old[2 * p + h, :, lo:hi]) for h in range(2)]
            e_ref[p, lo:hi, :] = jnp.concatenate(both, axis=0).T
            return carry

        lax.fori_loop(0, pairs, one, 0)
    for out, lo in ((to_left, 0), (to_right, cols - HALO)):
        hi = lo + HALO
        for p in range(pairs):
            out[p] = a_ref[p, lo:hi, :]
            out[pairs + p] = e_ref[p, lo:hi, :]
        out[2 * pairs] = dens_ref[lo:hi, :]
        out[2 * pairs + 1] = mat_ref[lo:hi, :]


def next_row(v):
    return pltpu.roll(v, LANES - 1, 1)


def prev_row(v):
    return pltpu.roll(v, 1, 1)


def after(ref, lead, lo, hi, here):
    if hi < ref.shape[-2]:
        return ref[(*lead, slice(lo + 1, hi + 1), slice(None))]
    return pltpu.roll(here, hi - lo - 1, 0)


def before(ref, lead, lo, hi, here):
    if lo > 0:
        return ref[(*lead, slice(lo - 1, hi - 1), slice(None))]
    return pltpu.roll(here, 1, 0)


def at(lo, hi):
    return (slice(lo, hi), slice(None))


def flux_sum(p, lo, hi, v_ref, v, fr_ref, fp_ref):
    fp = fp_ref[(p, *at(lo, hi))]
    fp_before = before(fp_ref, (p,), lo, hi, fp)
    polar = fp * (v - after(v_ref, (p,), lo, hi, v)) + fp_before * (v - before(v_ref, (p,), lo, hi, v))
    fr = fr_ref[(p, *at(lo, hi))] * (v - next_row(v))
    return polar + (fr - prev_row(fr))


def tile_sum(v):
    acc = v[:HALO]
    for lo in range(HALO, v.shape[0], HALO):
        acc = acc + v[lo : lo + HALO]
    return acc


def krylov(p, pairs, a_ref, fr_ref, fp_ref, r_ref, q_ref, t_ref, mom):
    tall = r_ref.shape[1]
    sums = [jnp.zeros((HALO, LANES), jnp.float32) for _ in range(4)]
    for lo, hi in pieces(tall):
        r = r_ref[(p, *at(lo, hi))]
        q = r + a_ref[(p, *at(lo, hi))] * r + flux_sum(p, lo, hi, r_ref, r, fr_ref, fp_ref)
        q_ref[(p, *at(lo, hi))] = q
        if lo >= HALO and hi <= tall - HALO:
            sums[0] = sums[0] + tile_sum(r * r)
            sums[1] = sums[1] + tile_sum(r * q)
            sums[2] = sums[2] + tile_sum(q * q)
    for lo, hi in pieces(tall):
        own = lo >= HALO and hi <= tall - HALO
        if not own and t_ref is None:
            continue
        q = q_ref[(p, *at(lo, hi))]
        t = q + a_ref[(p, *at(lo, hi))] * q + flux_sum(p, lo, hi, q_ref, q, fr_ref, fp_ref)
        if t_ref is not None:
            t_ref[(p, *at(lo, hi))] = t
        if own:
            sums[3] = sums[3] + tile_sum(q * t)
    for k in range(4):
        mom[pl.ds(k * pairs + p, 1), :] = jnp.sum(sums[k], axis=0, keepdims=True)


def send_moments(pairs, rows, mom, out, row_sums):
    lane = lane_of(4 * pairs)
    x = mom[...]
    first = jnp.where((lane >= HALO) & (lane < HALO + rows), x, 0.0)
    second = jnp.where((lane >= HALF + HALO) & (lane < HALF + HALO + rows), x, 0.0)
    both = jnp.concatenate([first, second, jnp.zeros((LANES - 8 * pairs, LANES), jnp.float32)], axis=0)
    line = lax.dot_general(
        jnp.ones((HALO, LANES), jnp.float32), both, (((1,), (1,)), ((), ())),
        precision=HIGHEST, preferred_element_type=jnp.float32,
    )
    if row_sums is not None:
        line = jnp.where(lane_of(HALO) < HALF, line, row_sums)
    for lo in range(0, out.shape[0], HALO):
        out[lo : lo + HALO, :] = line


def weight_of(weights, p):
    return jnp.where(lane_of(HALO) < HALF, weights[2 * p], weights[2 * p + 1])[:1]


def fold(s):
    s = s + pltpu.roll(s, HALF, 1)
    middle = s.shape[0] // 2
    return jnp.where(lane_of(middle) < HALF, s[:middle], s[middle:])


def unfold(s):
    other = pltpu.roll(s, HALF, 1)
    low = lane_of(s.shape[0]) < HALF
    return jnp.where(low, s, other), jnp.where(low, other, s)


def start_kernel(
    groups, rows, cols, weights, a_in, e_in, dens_in, mat_in, left, right,
    a_ref, e_ref, fr_ref, fp_ref, r_ref, q_ref, t_ref, dens_ref, mat_ref, emit_out, out,
    inv, emit, mom,
):
    pairs = groups // 2
    tall = cols + 2 * HALO
    dens_ref[0:HALO, :] = left[2 * pairs]
    dens_ref[HALO : HALO + cols, :] = dens_in[...]
    dens_ref[HALO + cols :, :] = right[2 * pairs]
    mat_ref[0:HALO, :] = left[2 * pairs + 1]
    mat_ref[HALO : HALO + cols, :] = mat_in[...]
    mat_ref[HALO + cols :, :] = right[2 * pairs + 1]
    emit[...] = jnp.zeros(emit.shape, jnp.float32)

    def one(p, carry):
        w = weight_of(weights, p)
        for lo, hi in pieces(tall):
            if lo < HALO:
                a, e = left[p], left[pairs + p]
            elif hi > tall - HALO:
                a, e = right[p], right[pairs + p]
            else:
                a, e = (ref[(p, *at(lo - HALO, hi - HALO))] for ref in (a_in, e_in))
            if lo < HALO or hi > tall - HALO:
                a = jnp.where(dens_ref[lo:hi, :] > 0.0, a, 1.0)
            a_ref[(p, *at(lo, hi))] = a
            e_ref[(p, *at(lo, hi))] = e
            emit[lo:hi, :] += a * w
        for lo, hi in pieces(tall):
            a, e = a_ref[(p, *at(lo, hi))], e_ref[(p, *at(lo, hi))]
            slope_r = 0.5 * (next_row(e) - prev_row(e))
            slope_p = 0.5 * (after(e_ref, (p,), lo, hi, e) - before(e_ref, (p,), lo, hi, e))
            n2 = slope_r * slope_r + slope_p * slope_p
            u = a * e
            s = 2.0 * u + jnp.sqrt(n2)
            inv[lo:hi, :] = jnp.where(dens_ref[lo:hi, :] > 0.0, (n2 + 3.0 * u * s) / (e * s), OUTSIDE)
        for lo, hi in pieces(tall):
            d = inv[lo:hi, :]
            fr_ref[(p, *at(lo, hi))] = 2.0 / (d + next_row(d))
            fp_ref[(p, *at(lo, hi))] = 2.0 / (d + after(inv, (), lo, hi, d))
        for lo, hi in pieces(tall):
            a, e = a_ref[(p, *at(lo, hi))], e_ref[(p, *at(lo, hi))]
            r_ref[(p, *at(lo, hi))] = a * (w * mat_ref[lo:hi, :] - e) - flux_sum(
                p, lo, hi, e_ref, e, fr_ref, fp_ref
            )
        krylov(p, pairs, a_ref, fr_ref, fp_ref, r_ref, q_ref, t_ref, mom)
        return carry

    lax.fori_loop(0, pairs, one, 0)
    emit_out[...] = fold(emit[...])
    row_sums = jnp.sum(tile_sum(dens_in[...]), axis=0, keepdims=True)
    send_moments(pairs, rows, mom, out, row_sums)


def steps(pairs, gathered):
    total = jnp.sum(gathered[...], axis=0, keepdims=True)
    lane = lane_of(pairs)
    sub = lax.broadcasted_iota(jnp.int32, (pairs, LANES), 0)

    def moment(k):
        first, second = (
            jnp.sum(jnp.where(lane == sub + (4 * h + k) * pairs, total, 0.0), axis=1, keepdims=True)
            for h in range(2)
        )
        return jnp.where(lane < HALF, first, second)

    m0, m1, m2, m3 = (moment(k) for k in range(4))
    k1, k2, k3 = m1 / m0, m2 / m0, m3 / m0
    first = 1.0 / k1
    det = jnp.maximum(k2 - k1 * k1, 0.0)
    beta = det / (k1 * k1)
    low = k1 * k3 - k2 * k2
    second = jnp.minimum(jnp.where(low > 0.0, k1 * det / low, 0.0), 1.0)
    return first + second * (1.0 + beta), first * second


def absorbed(pairs, c1, c2, a_ref, e_ref, r_ref, q_ref, e_out, s):
    tall = a_ref.shape[1]
    for lo, hi in pieces(tall):
        total = jnp.zeros((hi - lo, LANES), jnp.float32)
        for p in range(pairs):
            e = (
                e_ref[(p, *at(lo, hi))]
                + c1[p : p + 1, :] * r_ref[(p, *at(lo, hi))]
                - c2[p : p + 1, :] * q_ref[(p, *at(lo, hi))]
            )
            e_out[(p, *at(lo, hi))] = e
            total = total + a_ref[(p, *at(lo, hi))] * e
        s[lo:hi, :] = total


def update_kernel(pairs, gathered, a_ref, e_ref, r_ref, q_ref, *rest):
    if len(rest) == 6:
        emit, *rest = rest
    else:
        emit = None
    e_out, s_out, c1_ref, c2_ref, s = rest
    c1, c2 = steps(pairs, gathered)
    c1_ref[...] = c1
    c2_ref[...] = c2
    absorbed(pairs, c1, c2, a_ref, e_ref, r_ref, q_ref, e_out, s)
    s_out[0] = fold(s[...])
    if emit is not None:
        s_out[1] = emit[...]


def last_update_kernel(pairs, cols, gathered, a_ref, e_ref, r_ref, q_ref, e_out, s_out, s):
    c1, c2 = steps(pairs, gathered)
    absorbed(pairs, c1, c2, a_ref, e_ref, r_ref, q_ref, e_out, s)
    s_out[...] = fold(s[HALO : HALO + cols, :])


def energy_kernel(pairs, rows, cols, e_ref, out):
    def one(p, carry):
        for lo in range(0, cols, LANES):
            block = e_ref[p, HALO + lo : HALO + lo + LANES, :].T
            out[2 * p, :, lo : lo + LANES] = block[HALO : HALO + rows]
            out[2 * p + 1, :, lo : lo + LANES] = block[HALF + HALO : HALF + HALO + rows]
        return carry

    lax.fori_loop(0, pairs, one, 0)


def turned_back(v, rows):
    parts = [v[lo : lo + LANES].T[HALO : HALO + rows] for lo in range(0, v.shape[0], LANES)]
    return jnp.concatenate(parts, axis=1)


def heating_kernel(
    groups, rows, cols, polar_count, place, flux, gathered, dens_ref, mat_ref, flux_ref, column_out, fixed_out
):
    tall = dens_ref.shape[0]
    radius, polar = place[0], place[1]
    dens = dens_ref[...]
    row_id = lax.broadcasted_iota(jnp.int32, gathered.shape, 0)
    ahead = (row_id >= radius * polar_count) & (row_id < radius * polar_count + polar)
    carried = jnp.sum(jnp.where(ahead, gathered[...], 0.0), axis=0, keepdims=True)
    lane = lane_of()
    carried = jnp.where(lane < HALF, pltpu.roll(carried, HALF, 1), carried)
    dst = lax.broadcasted_iota(jnp.int32, (tall, tall), 0)
    src = lax.broadcasted_iota(jnp.int32, (tall, tall), 1)
    coeff = jnp.where(
        (src >= HALO) & (src <= dst), 1.0, jnp.where((src < HALO) & (src > dst), -1.0, 0.0)
    )
    within = lax.dot_general(
        coeff, dens, (((1,), (0,)), ((), ())), precision=HIGHEST, preferred_element_type=jnp.float32
    )
    column = 2.0 / (cols * polar_count) * (carried + within)
    vec = flux_ref[0:1, :]
    for i in range(rows):
        vec = jnp.where(lane % HALF == HALO + i, flux[i], vec)
    fixed_out[...] = 16.0 * dens * mat_ref[...] + vec * dens * jnp.exp(-column)
    column_out[...] = turned_back(column[HALO : HALO + cols], rows)


def summed(refs, lead=()):
    total = refs[0][(*lead, ...)]
    for s in refs[1:]:
        total = total + s[(*lead, ...)]
    return total


def next_kernel(groups, rows, count, turn, last, weights, c1_ref, c2_ref, a_ref, fr_ref, fp_ref, r_in, q_in, t_in, fixed, cap_in, mat_ref, *rest):
    pairs = groups // 2
    sums = rest[:count]
    rest = rest[count:]
    outs, (delta, mom) = rest[:-2], rest[-2:]
    r_ref, q_ref, out, *outs = outs
    t_ref = None if last else outs.pop(0)
    m_ref = None if last else outs.pop(0)
    half = fixed.shape[0] // 2
    folded = summed(sums, (0,))
    if turn == 0:
        cap_out = outs.pop(0)
        dens = cap_in[...]
        emits = jnp.concatenate(unfold(summed(sums, (1,))), axis=0)
        cap_out[...] = 16.0 * jnp.where(dens > 0.0, dens, 1.0) + emits
        cap_in = cap_out
    for k, total in enumerate(unfold(folded)):
        here = at(k * half, (k + 1) * half)
        nxt = (fixed[here] + total) / cap_in[here]
        delta[here] = nxt - mat_ref[here]
        if m_ref is not None:
            m_ref[here] = nxt

    def one(p, carry):
        w = weight_of(weights, p)
        c1 = c1_ref[pl.ds(p, 1), :]
        c2 = c2_ref[pl.ds(p, 1), :]
        for lo, hi in pieces(r_ref.shape[1]):
            here = (p, *at(lo, hi))
            r_ref[here] = (
                r_in[here] - c1 * q_in[here] + c2 * t_in[here] + a_ref[here] * (w * delta[lo:hi, :])
            )
        krylov(p, pairs, a_ref, fr_ref, fp_ref, r_ref, q_ref, t_ref, mom)
        return carry

    lax.fori_loop(0, pairs, one, 0)
    send_moments(pairs, rows, mom, out, None)


def material_kernel(count, rows, cols, fixed, capacity, *rest):
    sums, out = rest[:count], rest[count]
    total = jnp.concatenate(unfold(summed(sums)), axis=0)
    here = at(HALO, HALO + cols)
    out[...] = turned_back((fixed[here] + total) / capacity[here], rows)


def spread(part, axis):
    count = lax.axis_size(axis)
    return [part] + [
        lax.ppermute(part, axis, [(i, (i + s) % count) for i in range(count)]) for s in range(1, count)
    ]


def shifted(upward, downward, axis):
    count = lax.axis_size(axis)
    from_lower = lax.ppermute(downward, axis, [(i, i + 1) for i in range(count - 1)])
    from_upper = lax.ppermute(upward, axis, [(i + 1, i) for i in range(count - 1)])
    return from_lower, from_upper


def per_device(density, opacity, radiation_old, material_old, weights, stellar_flux):
    groups, rows, cols = opacity.shape
    pairs, tall = groups // 2, cols + 2 * HALO
    assert rows + 2 * HALO == HALF
    polar_count = lax.axis_size("polar")
    count = lax.axis_size("group")
    devices = lax.axis_size("radius") * polar_count
    place = jnp.stack([lax.axis_index("radius"), lax.axis_index("polar")]).astype(jnp.int32)
    planes = 2 * groups + 3
    big, flat, core = (pairs, tall, LANES), (tall, LANES), (cols, LANES)
    line = (devices, LANES)
    vmem = lambda shape: pltpu.VMEM(shape, jnp.float32)

    strips = [
        pltpu.VMEM((groups, 2 * HALO, cols), jnp.bfloat16),
        vmem((groups, HALO, cols)),
        vmem((HALO, cols)),
        vmem((HALO, cols)),
    ]
    up, down = call(
        functools.partial(pack_rows_kernel, groups, rows),
        [(planes, HALO, cols)] * 2,
        (stellar_flux, opacity, radiation_old, density, material_old),
        [sspec()] + [hspec()] * 4,
        scratch=strips * 2 + [pltpu.SemaphoreType.DMA((8,))],
        name="pack_rows",
    )
    top, bottom = shifted(up, down, "radius")
    a, e, dens, mat, flux_lanes, to_left, to_right = call(
        functools.partial(turn_kernel, groups, rows, cols),
        [(pairs, *core)] * 2 + [core, core, (HALO, LANES)] + [(2 * pairs + 2, HALO, LANES)] * 2,
        (opacity, radiation_old, density, material_old, top, bottom),
        [vspec()] * 6,
        name="turn",
    )
    left, right = shifted(to_left, to_right, "polar")
    a, e, fr, fp, r, q, t, dens, mat, emit, out = call(
        functools.partial(start_kernel, groups, rows, cols),
        [big] * 7 + [flat, flat, (tall // 2, LANES), line],
        (weights, a, e, dens, mat, left, right),
        [sspec()] + [vspec()] * 6,
        scratch=[vmem(flat), vmem(flat), vmem((4 * pairs, LANES))],
        name="start",
    )
    capacity = dens
    for turn in range(ITERS):
        gathered = lax.all_to_all(out, ("radius", "polar"), 0, 0, tiled=True)
        if turn + 1 == ITERS:
            e, part = call(
                functools.partial(last_update_kernel, pairs, cols),
                [big, (cols // 2, LANES)],
                (gathered, a, e, r, q),
                [vspec()] * 5,
                scratch=[vmem(flat)],
                name="last_update",
            )
            sums = spread(part, "group")
            (energy,) = call(
                functools.partial(energy_kernel, pairs, rows, cols),
                [(groups, rows, cols)],
                (e,),
                [vspec()],
                name="energy",
            )
            (mat,) = call(
                functools.partial(material_kernel, count, rows, cols),
                [(rows, cols)],
                (fixed, capacity, *sums),
                [vspec()] * (2 + count),
                name="material",
            )
            break
        first, last = turn == 0, turn + 2 == ITERS
        extra = [emit] if first else []
        e, part, c1, c2 = call(
            functools.partial(update_kernel, pairs),
            [big, (1 + len(extra), tall // 2, LANES), (pairs, LANES), (pairs, LANES)],
            (gathered, a, e, r, q, *extra),
            [vspec()] * (5 + len(extra)),
            scratch=[vmem(flat)],
            name="update",
        )
        sums = spread(part, "group")
        if first:
            column, fixed = call(
                functools.partial(heating_kernel, groups, rows, cols, polar_count),
                [(rows, cols), flat],
                (place, stellar_flux, gathered, dens, mat, flux_lanes),
                [sspec()] * 2 + [vspec()] * 4,
                name="heating",
            )
        r, q, out, *more = call(
            functools.partial(next_kernel, groups, rows, count, turn, last),
            [big, big, line] + ([] if last else [big, flat]) + ([flat] if first else []),
            (weights, c1, c2, a, fr, fp, r, q, t, fixed, capacity, mat, *sums),
            [sspec()] + [vspec()] * (11 + count),
            scratch=[vmem(flat), vmem((4 * pairs, LANES))],
            name="next",
        )
        if not last:
            t, mat, *more = more
        if first:
            (capacity,) = more
    return (energy, mat, column)


def solution(mesh):
    return jax.shard_map(
        per_device,
        mesh=mesh,
        in_specs=(
            P("radius", "polar"),
            P("group", "radius", "polar"),
            P("group", "radius", "polar"),
            P("radius", "polar"),
            P("group"),
            P("radius"),
        ),
        out_specs=(P("group", "radius", "polar"), P("radius", "polar"), P("radius", "polar")),
        check_vma=False,
    )
```

```python
import functools
import jax
import jax.numpy as jnp
from jax import lax
from jax.experimental import pallas as pl
from jax.experimental.pallas import tpu as pltpu
from jax.sharding import PartitionSpec as P


ITERS = 3
HALO = 8
LANES = 128
HALF = LANES // 2
STEP = 64
VMEM_LIMIT = 12 * 1024 * 1024
HIGHEST = lax.Precision.HIGHEST
OUTSIDE = 1.6e38


def vspec():
    return pl.BlockSpec(memory_space=pltpu.VMEM)


def sspec():
    return pl.BlockSpec(memory_space=pltpu.SMEM)


def hspec():
    return pl.BlockSpec(memory_space=pltpu.HBM)


def call(kernel, outs, args, specs, scratch=(), flops=1000000, nbytes=1000000, name=None, limit=VMEM_LIMIT):
    return pl.pallas_call(
        kernel,
        out_shape=[jax.ShapeDtypeStruct(s, jnp.float32) for s in outs],
        in_specs=specs,
        out_specs=[vspec() for _ in outs],
        scratch_shapes=list(scratch),
        compiler_params=pltpu.CompilerParams(vmem_limit_bytes=limit),
        cost_estimate=pl.CostEstimate(flops=flops, bytes_accessed=nbytes, transcendentals=0),
        name=name,
    )(*args)


def lane_of(height=1):
    return lax.broadcasted_iota(jnp.int32, (height, LANES), 1)


def pieces(tall):
    cuts = [0, HALO]
    while cuts[-1] + STEP < tall - HALO:
        cuts.append(cuts[-1] + STEP)
    cuts += [tall - HALO, tall]
    return list(zip(cuts[:-1], cuts[1:]))


def pack_rows_kernel(groups, rows, flux, opacity, old, density, material, up, down, *scratch):
    copies = []
    sems = scratch[-1]
    for side, (lo, base) in enumerate(((0, 0), (rows - HALO, rows - 2 * HALO))):
        op_buf, old_buf, dens_buf, mat_buf = scratch[4 * side : 4 * side + 4]
        pairs = (
            (opacity.at[:, pl.ds(base, 2 * HALO), :], op_buf),
            (old.at[:, pl.ds(lo, HALO), :], old_buf),
            (density.at[pl.ds(lo, HALO), :], dens_buf),
            (material.at[pl.ds(lo, HALO), :], mat_buf),
        )
        for k, (src, dst) in enumerate(pairs):
            copies.append(pltpu.make_async_copy(src, dst, sems.at[4 * side + k]))
    for c in copies:
        c.start()
    for c in copies:
        c.wait()
    lane = lane_of(HALO)
    for side, (out, lo, inside, first) in enumerate(
        ((up, 0, 0, rows + HALO), (down, rows - HALO, HALO, 0))
    ):
        op_buf, old_buf, dens_buf, mat_buf = scratch[4 * side : 4 * side + 4]
        dens = dens_buf[...]
        for g in range(groups):
            out[g] = op_buf[g].astype(jnp.float32)[inside : inside + HALO, :] * dens
            out[groups + g] = old_buf[g]
        out[2 * groups] = dens
        out[2 * groups + 1] = mat_buf[...]
        vec = jnp.zeros((HALO, LANES), jnp.float32)
        for i in range(HALO):
            vec = jnp.where(lane % HALF == first + i, flux[lo + i], vec)
        out[2 * groups + 2, :, :LANES] = vec
        for at in range(LANES, out.shape[2], LANES):
            out[2 * groups + 2, :, at : at + LANES] = vec


def turn_kernel(
    groups, rows, cols, opacity, old, density, material, top, bottom,
    a_ref, e_ref, dens_ref, mat_ref, flux_ref, to_left, to_right,
):
    pairs = groups // 2
    flux_ref[...] = top[2 * groups + 2, :, :LANES] + bottom[2 * groups + 2, :, :LANES]
    for lo in range(0, cols, LANES):
        hi = lo + LANES

        def tile(plane, own):
            return jnp.concatenate([top[plane, :, lo:hi], own, bottom[plane, :, lo:hi]], axis=0)

        d = tile(2 * groups, density[:, lo:hi])
        d = jnp.concatenate([d, d], axis=0).T
        m = tile(2 * groups + 1, material[:, lo:hi])
        m = jnp.concatenate([m, m], axis=0).T
        dens_ref[lo:hi, :] = d
        mat_ref[lo:hi, :] = m

        def one(p, carry):
            both = []
            for h in range(2):
                g = 2 * p + h
                both.append(tile(g, opacity[g, :, lo:hi].astype(jnp.float32) * density[:, lo:hi]))
            a = jnp.concatenate(both, axis=0).T
            a_ref[p, lo:hi, :] = jnp.where(dens_ref[lo:hi, :] > 0.0, a, 1.0)
            both = [tile(groups + 2 * p + h, old[2 * p + h, :, lo:hi]) for h in range(2)]
            e_ref[p, lo:hi, :] = jnp.concatenate(both, axis=0).T
            return carry

        lax.fori_loop(0, pairs, one, 0)
    for out, lo in ((to_left, 0), (to_right, cols - HALO)):
        hi = lo + HALO
        for p in range(pairs):
            out[p] = a_ref[p, lo:hi, :]
            out[pairs + p] = e_ref[p, lo:hi, :]
        out[2 * pairs] = dens_ref[lo:hi, :]
        out[2 * pairs + 1] = mat_ref[lo:hi, :]


def next_row(v):
    return pltpu.roll(v, LANES - 1, 1)


def prev_row(v):
    return pltpu.roll(v, 1, 1)


def after(ref, lead, lo, hi, here):
    if hi < ref.shape[-2]:
        return ref[(*lead, slice(lo + 1, hi + 1), slice(None))]
    return pltpu.roll(here, hi - lo - 1, 0)


def before(ref, lead, lo, hi, here):
    if lo > 0:
        return ref[(*lead, slice(lo - 1, hi - 1), slice(None))]
    return pltpu.roll(here, 1, 0)


def at(lo, hi):
    return (slice(lo, hi), slice(None))


def flux_sum(p, lo, hi, v_ref, v, fr_ref, fp_ref):
    fp = fp_ref[(p, *at(lo, hi))]
    fp_before = before(fp_ref, (p,), lo, hi, fp)
    polar = fp * (v - after(v_ref, (p,), lo, hi, v)) + fp_before * (v - before(v_ref, (p,), lo, hi, v))
    fr = fr_ref[(p, *at(lo, hi))] * (v - next_row(v))
    return polar + (fr - prev_row(fr))


def tile_sum(v):
    acc = v[:HALO]
    for lo in range(HALO, v.shape[0], HALO):
        acc = acc + v[lo : lo + HALO]
    return acc


def krylov(p, pairs, a_ref, fr_ref, fp_ref, r_ref, q_ref, t_ref, mom):
    tall = r_ref.shape[1]
    sums = [jnp.zeros((HALO, LANES), jnp.float32) for _ in range(4)]
    for lo, hi in pieces(tall):
        r = r_ref[(p, *at(lo, hi))]
        q = r + a_ref[(p, *at(lo, hi))] * r + flux_sum(p, lo, hi, r_ref, r, fr_ref, fp_ref)
        q_ref[(p, *at(lo, hi))] = q
        if lo >= HALO and hi <= tall - HALO:
            sums[0] = sums[0] + tile_sum(r * r)
            sums[1] = sums[1] + tile_sum(r * q)
            sums[2] = sums[2] + tile_sum(q * q)
    for lo, hi in pieces(tall):
        own = lo >= HALO and hi <= tall - HALO
        if not own and t_ref is None:
            continue
        q = q_ref[(p, *at(lo, hi))]
        t = q + a_ref[(p, *at(lo, hi))] * q + flux_sum(p, lo, hi, q_ref, q, fr_ref, fp_ref)
        if t_ref is not None:
            t_ref[(p, *at(lo, hi))] = t
        if own:
            sums[3] = sums[3] + tile_sum(q * t)
    for k in range(4):
        mom[pl.ds(k * pairs + p, 1), :] = jnp.sum(sums[k], axis=0, keepdims=True)


def send_moments(pairs, rows, mom, out, row_sums):
    lane = lane_of(4 * pairs)
    x = mom[...]
    first = jnp.where((lane >= HALO) & (lane < HALO + rows), x, 0.0)
    second = jnp.where((lane >= HALF + HALO) & (lane < HALF + HALO + rows), x, 0.0)
    both = jnp.concatenate([first, second, jnp.zeros((LANES - 8 * pairs, LANES), jnp.float32)], axis=0)
    line = lax.dot_general(
        jnp.ones((HALO, LANES), jnp.float32), both, (((1,), (1,)), ((), ())),
        precision=HIGHEST, preferred_element_type=jnp.float32,
    )
    if row_sums is not None:
        line = jnp.where(lane_of(HALO) < HALF, line, row_sums)
    for lo in range(0, out.shape[0], HALO):
        out[lo : lo + HALO, :] = line


def weight_of(weights, p):
    return jnp.where(lane_of(HALO) < HALF, weights[2 * p], weights[2 * p + 1])[:1]


def fold(s):
    s = s + pltpu.roll(s, HALF, 1)
    middle = s.shape[0] // 2
    return jnp.where(lane_of(middle) < HALF, s[:middle], s[middle:])


def unfold(s):
    other = pltpu.roll(s, HALF, 1)
    low = lane_of(s.shape[0]) < HALF
    return jnp.where(low, s, other), jnp.where(low, other, s)


def start_kernel(
    groups, rows, cols, weights, a_in, e_in, dens_in, mat_in, left, right,
    a_ref, e_ref, fr_ref, fp_ref, r_ref, q_ref, t_ref, dens_ref, mat_ref, emit_out, out,
    inv, emit, mom,
):
    pairs = groups // 2
    tall = cols + 2 * HALO
    dens_ref[0:HALO, :] = left[2 * pairs]
    dens_ref[HALO : HALO + cols, :] = dens_in[...]
    dens_ref[HALO + cols :, :] = right[2 * pairs]
    mat_ref[0:HALO, :] = left[2 * pairs + 1]
    mat_ref[HALO : HALO + cols, :] = mat_in[...]
    mat_ref[HALO + cols :, :] = right[2 * pairs + 1]
    emit[...] = jnp.zeros(emit.shape, jnp.float32)

    def one(p, carry):
        w = weight_of(weights, p)
        for lo, hi in pieces(tall):
            if lo < HALO:
                a, e = left[p], left[pairs + p]
            elif hi > tall - HALO:
                a, e = right[p], right[pairs + p]
            else:
                a, e = (ref[(p, *at(lo - HALO, hi - HALO))] for ref in (a_in, e_in))
            if lo < HALO or hi > tall - HALO:
                a = jnp.where(dens_ref[lo:hi, :] > 0.0, a, 1.0)
            a_ref[(p, *at(lo, hi))] = a
            e_ref[(p, *at(lo, hi))] = e
            emit[lo:hi, :] += a * w
        for lo, hi in pieces(tall):
            a, e = a_ref[(p, *at(lo, hi))], e_ref[(p, *at(lo, hi))]
            slope_r = 0.5 * (next_row(e) - prev_row(e))
            slope_p = 0.5 * (after(e_ref, (p,), lo, hi, e) - before(e_ref, (p,), lo, hi, e))
            n2 = slope_r * slope_r + slope_p * slope_p
            u = a * e
            s = 2.0 * u + jnp.sqrt(n2)
            inv[lo:hi, :] = jnp.where(dens_ref[lo:hi, :] > 0.0, (n2 + 3.0 * u * s) / (e * s), OUTSIDE)
        for lo, hi in pieces(tall):
            d = inv[lo:hi, :]
            fr_ref[(p, *at(lo, hi))] = 2.0 / (d + next_row(d))
            fp_ref[(p, *at(lo, hi))] = 2.0 / (d + after(inv, (), lo, hi, d))
        for lo, hi in pieces(tall):
            a, e = a_ref[(p, *at(lo, hi))], e_ref[(p, *at(lo, hi))]
            r_ref[(p, *at(lo, hi))] = a * (w * mat_ref[lo:hi, :] - e) - flux_sum(
                p, lo, hi, e_ref, e, fr_ref, fp_ref
            )
        krylov(p, pairs, a_ref, fr_ref, fp_ref, r_ref, q_ref, t_ref, mom)
        return carry

    lax.fori_loop(0, pairs, one, 0)
    emit_out[...] = fold(emit[...])
    row_sums = jnp.sum(tile_sum(dens_in[...]), axis=0, keepdims=True)
    send_moments(pairs, rows, mom, out, row_sums)


def steps(pairs, gathered):
    total = jnp.sum(gathered[...], axis=0, keepdims=True)
    lane = lane_of(pairs)
    sub = lax.broadcasted_iota(jnp.int32, (pairs, LANES), 0)

    def moment(k):
        first, second = (
            jnp.sum(jnp.where(lane == sub + (4 * h + k) * pairs, total, 0.0), axis=1, keepdims=True)
            for h in range(2)
        )
        return jnp.where(lane < HALF, first, second)

    m0, m1, m2, m3 = (moment(k) for k in range(4))
    k1, k2, k3 = m1 / m0, m2 / m0, m3 / m0
    first = 1.0 / k1
    det = jnp.maximum(k2 - k1 * k1, 0.0)
    beta = det / (k1 * k1)
    low = k1 * k3 - k2 * k2
    second = jnp.minimum(jnp.where(low > 0.0, k1 * det / low, 0.0), 1.0)
    return first + second * (1.0 + beta), first * second


def absorbed(pairs, c1, c2, a_ref, e_ref, r_ref, q_ref, e_out, s):
    tall = a_ref.shape[1]
    for lo, hi in pieces(tall):
        total = jnp.zeros((hi - lo, LANES), jnp.float32)
        for p in range(pairs):
            e = (
                e_ref[(p, *at(lo, hi))]
                + c1[p : p + 1, :] * r_ref[(p, *at(lo, hi))]
                - c2[p : p + 1, :] * q_ref[(p, *at(lo, hi))]
            )
            e_out[(p, *at(lo, hi))] = e
            total = total + a_ref[(p, *at(lo, hi))] * e
        s[lo:hi, :] = total


def update_kernel(pairs, gathered, a_ref, e_ref, r_ref, q_ref, *rest):
    if len(rest) == 6:
        emit, *rest = rest
    else:
        emit = None
    e_out, s_out, c1_ref, c2_ref, s = rest
    c1, c2 = steps(pairs, gathered)
    c1_ref[...] = c1
    c2_ref[...] = c2
    absorbed(pairs, c1, c2, a_ref, e_ref, r_ref, q_ref, e_out, s)
    s_out[0] = fold(s[...])
    if emit is not None:
        s_out[1] = emit[...]


def last_update_kernel(pairs, cols, gathered, a_ref, e_ref, r_ref, q_ref, e_out, s_out, s):
    c1, c2 = steps(pairs, gathered)
    absorbed(pairs, c1, c2, a_ref, e_ref, r_ref, q_ref, e_out, s)
    s_out[...] = fold(s[HALO : HALO + cols, :])


def energy_kernel(pairs, rows, cols, e_ref, out):
    def one(p, carry):
        for lo in range(0, cols, LANES):
            block = e_ref[p, HALO + lo : HALO + lo + LANES, :].T
            out[2 * p, :, lo : lo + LANES] = block[HALO : HALO + rows]
            out[2 * p + 1, :, lo : lo + LANES] = block[HALF + HALO : HALF + HALO + rows]
        return carry

    lax.fori_loop(0, pairs, one, 0)


def turned_back(v, rows):
    parts = [v[lo : lo + LANES].T[HALO : HALO + rows] for lo in range(0, v.shape[0], LANES)]
    return jnp.concatenate(parts, axis=1)


def heating_kernel(
    groups, rows, cols, polar_count, flux, gathered, dens_ref, mat_ref, flux_ref, column_out, fixed_out
):
    tall = dens_ref.shape[0]
    radius, polar = lax.axis_index("radius"), lax.axis_index("polar")
    dens = dens_ref[...]
    row_id = lax.broadcasted_iota(jnp.int32, gathered.shape, 0)
    ahead = (row_id >= radius * polar_count) & (row_id < radius * polar_count + polar)
    carried = jnp.sum(jnp.where(ahead, gathered[...], 0.0), axis=0, keepdims=True)
    lane = lane_of()
    carried = jnp.where(lane < HALF, pltpu.roll(carried, HALF, 1), carried)
    dst = lax.broadcasted_iota(jnp.int32, (tall, tall), 0)
    src = lax.broadcasted_iota(jnp.int32, (tall, tall), 1)
    coeff = jnp.where(
        (src >= HALO) & (src <= dst), 1.0, jnp.where((src < HALO) & (src > dst), -1.0, 0.0)
    )
    within = lax.dot_general(
        coeff, dens, (((1,), (0,)), ((), ())), precision=HIGHEST, preferred_element_type=jnp.float32
    )
    column = 2.0 / (cols * polar_count) * (carried + within)
    vec = flux_ref[0:1, :]
    for i in range(rows):
        vec = jnp.where(lane % HALF == HALO + i, flux[i], vec)
    fixed_out[...] = 16.0 * dens * mat_ref[...] + vec * dens * jnp.exp(-column)
    column_out[...] = turned_back(column[HALO : HALO + cols], rows)


def summed(refs, lead=()):
    total = refs[0][(*lead, ...)]
    for s in refs[1:]:
        total = total + s[(*lead, ...)]
    return total


def next_kernel(groups, rows, count, turn, last, weights, c1_ref, c2_ref, a_ref, fr_ref, fp_ref, r_in, q_in, t_in, fixed, cap_in, mat_ref, *rest):
    pairs = groups // 2
    sums = rest[:count]
    rest = rest[count:]
    outs, (delta, mom) = rest[:-2], rest[-2:]
    r_ref, q_ref, out, *outs = outs
    t_ref = None if last else outs.pop(0)
    m_ref = None if last else outs.pop(0)
    half = fixed.shape[0] // 2
    folded = summed(sums, (0,))
    if turn == 0:
        cap_out = outs.pop(0)
        dens = cap_in[...]
        emits = jnp.concatenate(unfold(summed(sums, (1,))), axis=0)
        cap_out[...] = 16.0 * jnp.where(dens > 0.0, dens, 1.0) + emits
        cap_in = cap_out
    for k, total in enumerate(unfold(folded)):
        here = at(k * half, (k + 1) * half)
        nxt = (fixed[here] + total) / cap_in[here]
        delta[here] = nxt - mat_ref[here]
        if m_ref is not None:
            m_ref[here] = nxt

    def one(p, carry):
        w = weight_of(weights, p)
        c1 = c1_ref[pl.ds(p, 1), :]
        c2 = c2_ref[pl.ds(p, 1), :]
        for lo, hi in pieces(r_ref.shape[1]):
            here = (p, *at(lo, hi))
            r_ref[here] = (
                r_in[here] - c1 * q_in[here] + c2 * t_in[here] + a_ref[here] * (w * delta[lo:hi, :])
            )
        krylov(p, pairs, a_ref, fr_ref, fp_ref, r_ref, q_ref, t_ref, mom)
        return carry

    lax.fori_loop(0, pairs, one, 0)
    send_moments(pairs, rows, mom, out, None)


def material_kernel(count, rows, cols, fixed, capacity, *rest):
    sums, out = rest[:count], rest[count]
    total = jnp.concatenate(unfold(summed(sums)), axis=0)
    here = at(HALO, HALO + cols)
    out[...] = turned_back((fixed[here] + total) / capacity[here], rows)


def spread(part, axis):
    count = lax.axis_size(axis)
    return [part] + [
        lax.ppermute(part, axis, [(i, (i + s) % count) for i in range(count)]) for s in range(1, count)
    ]


def shifted(upward, downward, axis):
    count = lax.axis_size(axis)
    from_lower = lax.ppermute(downward, axis, [(i, i + 1) for i in range(count - 1)])
    from_upper = lax.ppermute(upward, axis, [(i + 1, i) for i in range(count - 1)])
    return from_lower, from_upper


def per_device(density, opacity, radiation_old, material_old, weights, stellar_flux):
    groups, rows, cols = opacity.shape
    pairs, tall = groups // 2, cols + 2 * HALO
    assert rows + 2 * HALO == HALF
    polar_count = lax.axis_size("polar")
    count = lax.axis_size("group")
    devices = lax.axis_size("radius") * polar_count
    planes = 2 * groups + 3
    big, flat, core = (pairs, tall, LANES), (tall, LANES), (cols, LANES)
    line = (devices, LANES)
    vmem = lambda shape: pltpu.VMEM(shape, jnp.float32)

    strips = [
        pltpu.VMEM((groups, 2 * HALO, cols), jnp.bfloat16),
        vmem((groups, HALO, cols)),
        vmem((HALO, cols)),
        vmem((HALO, cols)),
    ]
    up, down = call(
        functools.partial(pack_rows_kernel, groups, rows),
        [(planes, HALO, cols)] * 2,
        (stellar_flux, opacity, radiation_old, density, material_old),
        [sspec()] + [hspec()] * 4,
        scratch=strips * 2 + [pltpu.SemaphoreType.DMA((8,))],
        name="pack_rows",
        limit=60 * 1024 * 1024,
    )
    top, bottom = shifted(up, down, "radius")
    a, e, dens, mat, flux_lanes, to_left, to_right = call(
        functools.partial(turn_kernel, groups, rows, cols),
        [(pairs, *core)] * 2 + [core, core, (HALO, LANES)] + [(2 * pairs + 2, HALO, LANES)] * 2,
        (opacity, radiation_old, density, material_old, top, bottom),
        [vspec()] * 6,
        name="turn",
    )
    left, right = shifted(to_left, to_right, "polar")
    a, e, fr, fp, r, q, t, dens, mat, emit, out = call(
        functools.partial(start_kernel, groups, rows, cols),
        [big] * 7 + [flat, flat, (tall // 2, LANES), line],
        (weights, a, e, dens, mat, left, right),
        [sspec()] + [vspec()] * 6,
        scratch=[vmem(flat), vmem(flat), vmem((4 * pairs, LANES))],
        name="start",
    )
    capacity = dens
    for turn in range(ITERS):
        gathered = lax.all_to_all(out, ("radius", "polar"), 0, 0, tiled=True)
        if turn + 1 == ITERS:
            e, part = call(
                functools.partial(last_update_kernel, pairs, cols),
                [big, (cols // 2, LANES)],
                (gathered, a, e, r, q),
                [vspec()] * 5,
                scratch=[vmem(flat)],
                name="last_update",
            )
            sums = spread(part, "group")
            (energy,) = call(
                functools.partial(energy_kernel, pairs, rows, cols),
                [(groups, rows, cols)],
                (e,),
                [vspec()],
                name="energy",
            )
            (mat,) = call(
                functools.partial(material_kernel, count, rows, cols),
                [(rows, cols)],
                (fixed, capacity, *sums),
                [vspec()] * (2 + count),
                name="material",
            )
            break
        first, last = turn == 0, turn + 2 == ITERS
        extra = [emit] if first else []
        e, part, c1, c2 = call(
            functools.partial(update_kernel, pairs),
            [big, (1 + len(extra), tall // 2, LANES), (pairs, LANES), (pairs, LANES)],
            (gathered, a, e, r, q, *extra),
            [vspec()] * (5 + len(extra)),
            scratch=[vmem(flat)],
            name="update",
        )
        sums = spread(part, "group")
        if first:
            column, fixed = call(
                functools.partial(heating_kernel, groups, rows, cols, polar_count),
                [(rows, cols), flat],
                (stellar_flux, gathered, dens, mat, flux_lanes),
                [sspec()] + [vspec()] * 4,
                name="heating",
            )
        r, q, out, *more = call(
            functools.partial(next_kernel, groups, rows, count, turn, last),
            [big, big, line] + ([] if last else [big, flat]) + ([flat] if first else []),
            (weights, c1, c2, a, fr, fp, r, q, t, fixed, capacity, mat, *sums),
            [sspec()] + [vspec()] * (11 + count),
            scratch=[vmem(flat), vmem((4 * pairs, LANES))],
            name="next",
        )
        if not last:
            t, mat, *more = more
        if first:
            (capacity,) = more
    return (energy, mat, column)


def solution(mesh):
    return jax.shard_map(
        per_device,
        mesh=mesh,
        in_specs=(
            P("radius", "polar"),
            P("group", "radius", "polar"),
            P("group", "radius", "polar"),
            P("radius", "polar"),
            P("group"),
            P("radius"),
        ),
        out_specs=(P("group", "radius", "polar"), P("radius", "polar"), P("radius", "polar")),
        check_vma=False,
    )
```

```python
import functools
import jax
import jax.numpy as jnp
from jax import lax
from jax.experimental import pallas as pl
from jax.experimental.pallas import tpu as pltpu
from jax.sharding import PartitionSpec as P


ITERS = 3
HALO = 8
LANES = 128
HALF = LANES // 2
STEP = 64
VMEM_LIMIT = 12 * 1024 * 1024
HIGHEST = lax.Precision.HIGHEST
OUTSIDE = 1.6e38


def vspec():
    return pl.BlockSpec(memory_space=pltpu.VMEM)


def sspec():
    return pl.BlockSpec(memory_space=pltpu.SMEM)


def hspec():
    return pl.BlockSpec(memory_space=pltpu.HBM)


def call(kernel, outs, args, specs, scratch=(), flops=1000000, nbytes=1000000, name=None, limit=VMEM_LIMIT, aliases=None):
    return pl.pallas_call(
        kernel,
        out_shape=[jax.ShapeDtypeStruct(s, jnp.float32) for s in outs],
        in_specs=specs,
        out_specs=[vspec() for _ in outs],
        scratch_shapes=list(scratch),
        compiler_params=pltpu.CompilerParams(vmem_limit_bytes=limit),
        cost_estimate=pl.CostEstimate(flops=flops, bytes_accessed=nbytes, transcendentals=0),
        name=name,
        input_output_aliases=aliases or {},
    )(*args)


def lane_of(height=1):
    return lax.broadcasted_iota(jnp.int32, (height, LANES), 1)


def pieces(tall):
    cuts = [0, HALO]
    while cuts[-1] + STEP < tall - HALO:
        cuts.append(cuts[-1] + STEP)
    cuts += [tall - HALO, tall]
    return list(zip(cuts[:-1], cuts[1:]))


def partner(axis, inner, outer):
    even = lax.rem(lax.axis_index(axis), 2) == 0
    return even, jnp.where(even, inner, outer), jnp.where(even, outer, inner)


def pack_rows_kernel(groups, rows, flux, opacity, old, density, material, first, second, *scratch):
    even, lo_first, lo_second = partner("radius", rows - HALO, 0)
    sems = scratch[-1]
    sides = ((first, lo_first, even), (second, lo_second, jnp.logical_not(even)))
    copies = []
    for side, (_, lo, at_end) in enumerate(sides):
        op_buf, old_buf, dens_buf, mat_buf = scratch[4 * side : 4 * side + 4]
        lo = pl.multiple_of(lo, HALO)
        base = pl.multiple_of(jnp.where(at_end, rows - 2 * HALO, 0), 2 * HALO)
        moves = (
            (opacity.at[:, pl.ds(base, 2 * HALO), :], op_buf),
            (old.at[:, pl.ds(lo, HALO), :], old_buf),
            (density.at[pl.ds(lo, HALO), :], dens_buf),
            (material.at[pl.ds(lo, HALO), :], mat_buf),
        )
        for k, (src, dst) in enumerate(moves):
            copies.append(pltpu.make_async_copy(src, dst, sems.at[4 * side + k]))
    for c in copies:
        c.start()
    for c in copies:
        c.wait()
    lane = lane_of(HALO) % HALF
    for side, (out, lo, at_end) in enumerate(sides):
        op_buf, old_buf, dens_buf, mat_buf = scratch[4 * side : 4 * side + 4]
        dens = dens_buf[...]
        for g in range(groups):
            part = op_buf[g].astype(jnp.float32)
            out[g] = jnp.where(at_end, part[HALO:], part[:HALO]) * dens
            out[groups + g] = old_buf[g]
        out[2 * groups] = dens
        out[2 * groups + 1] = mat_buf[...]
        place = jnp.where(at_end, 0, rows + HALO)
        vec = jnp.zeros((HALO, LANES), jnp.float32)
        for i in range(HALO):
            vec = jnp.where(lane == place + i, flux[lo + i], vec)
        for at_lane in range(0, out.shape[2], LANES):
            out[2 * groups + 2, :, at_lane : at_lane + LANES] = vec


def turn_kernel(
    groups, rows, cols, opacity, old, density, material, got_first, got_second,
    a_ref, e_ref, dens_ref, mat_ref, flux_ref, to_first, to_second,
):
    pairs = groups // 2
    plane_of_flux = 2 * groups + 2
    flux_ref[...] = got_first[plane_of_flux, :, :LANES] + got_second[plane_of_flux, :, :LANES]
    even, _, _ = partner("radius", 0, 0)
    for lo in range(0, cols, LANES):
        hi = lo + LANES

        def tile(plane, own):
            one, two = got_first[plane, :, lo:hi], got_second[plane, :, lo:hi]
            return jnp.concatenate([jnp.where(even, two, one), own, jnp.where(even, one, two)], axis=0)

        d = tile(2 * groups, density[:, lo:hi])
        d = jnp.concatenate([d, d], axis=0).T
        m = tile(2 * groups + 1, material[:, lo:hi])
        m = jnp.concatenate([m, m], axis=0).T
        dens_ref[HALO + lo : HALO + hi, :] = d
        mat_ref[HALO + lo : HALO + hi, :] = m

        def one(p, carry):
            both = []
            for h in range(2):
                g = 2 * p + h
                both.append(tile(g, opacity[g, :, lo:hi].astype(jnp.float32) * density[:, lo:hi]))
            a = jnp.concatenate(both, axis=0).T
            a_ref[p, HALO + lo : HALO + hi, :] = jnp.where(dens_ref[HALO + lo : HALO + hi, :] > 0.0, a, 1.0)
            both = [tile(groups + 2 * p + h, old[2 * p + h, :, lo:hi]) for h in range(2)]
            e_ref[p, HALO + lo : HALO + hi, :] = jnp.concatenate(both, axis=0).T
            return carry

        lax.fori_loop(0, pairs, one, 0)
    _, lo_first, lo_second = partner("polar", cols, HALO)
    for out, lo in ((to_first, lo_first), (to_second, lo_second)):
        edge = pl.ds(pl.multiple_of(lo, HALO), HALO)
        for p in range(pairs):
            out[p] = a_ref[p, edge, :]
            out[pairs + p] = e_ref[p, edge, :]
        out[2 * pairs] = dens_ref[edge, :]
        out[2 * pairs + 1] = mat_ref[edge, :]


def next_row(v):
    return pltpu.roll(v, LANES - 1, 1)


def prev_row(v):
    return pltpu.roll(v, 1, 1)


def after(ref, lead, lo, hi, here, end):
    if hi < end:
        return ref[(*lead, slice(lo + 1, hi + 1), slice(None))]
    return pltpu.roll(here, hi - lo - 1, 0)


def before(ref, lead, lo, hi, here, begin):
    if lo > begin:
        return ref[(*lead, slice(lo - 1, hi - 1), slice(None))]
    return pltpu.roll(here, 1, 0)


def at(lo, hi):
    return (slice(lo, hi), slice(None))


def flux_sum(p, lo, hi, v_ref, v, fr_ref, fp_ref, span):
    begin, end = span
    fp = fp_ref[(p, *at(lo, hi))]
    fp_before = before(fp_ref, (p,), lo, hi, fp, begin)
    polar = fp * (v - after(v_ref, (p,), lo, hi, v, end)) + fp_before * (
        v - before(v_ref, (p,), lo, hi, v, begin)
    )
    fr = fr_ref[(p, *at(lo, hi))] * (v - next_row(v))
    return polar + (fr - prev_row(fr))


def tile_sum(v):
    acc = v[:HALO]
    for lo in range(HALO, v.shape[0], HALO):
        acc = acc + v[lo : lo + HALO]
    return acc


def krylov(p, pairs, parts, span, own, a_ref, fr_ref, fp_ref, r_ref, q_ref, t_ref, mom, old_mom=None):
    sums = [jnp.zeros((HALO, LANES), jnp.float32) for _ in range(4)]
    for lo, hi in parts:
        r = r_ref[(p, *at(lo, hi))]
        q = r + a_ref[(p, *at(lo, hi))] * r + flux_sum(p, lo, hi, r_ref, r, fr_ref, fp_ref, span)
        q_ref[(p, *at(lo, hi))] = q
        if lo >= own[0] and hi <= own[1]:
            sums[0] = sums[0] + tile_sum(r * r)
            sums[1] = sums[1] + tile_sum(r * q)
            sums[2] = sums[2] + tile_sum(q * q)
    for lo, hi in parts:
        inside = lo >= own[0] and hi <= own[1]
        if not inside and t_ref is None:
            continue
        q = q_ref[(p, *at(lo, hi))]
        t = q + a_ref[(p, *at(lo, hi))] * q + flux_sum(p, lo, hi, q_ref, q, fr_ref, fp_ref, span)
        if t_ref is not None:
            t_ref[(p, *at(lo, hi))] = t
        if inside:
            sums[3] = sums[3] + tile_sum(q * t)
    for k in range(4):
        total = jnp.sum(sums[k], axis=0, keepdims=True)
        if old_mom is not None:
            total = total + old_mom[pl.ds(k * pairs + p, 1), :]
        mom[pl.ds(k * pairs + p, 1), :] = total


def send_moments(pairs, rows, mom, out, row_sums):
    lane = lane_of(4 * pairs)
    x = mom[...]
    first = jnp.where((lane >= HALO) & (lane < HALO + rows), x, 0.0)
    second = jnp.where((lane >= HALF + HALO) & (lane < HALF + HALO + rows), x, 0.0)
    both = jnp.concatenate([first, second, jnp.zeros((LANES - 8 * pairs, LANES), jnp.float32)], axis=0)
    line = lax.dot_general(
        jnp.ones((HALO, LANES), jnp.float32), both, (((1,), (1,)), ((), ())),
        precision=HIGHEST, preferred_element_type=jnp.float32,
    )
    if row_sums is not None:
        line = jnp.where(lane_of(HALO) < HALF, line, row_sums)
    for lo in range(0, out.shape[0], HALO):
        out[lo : lo + HALO, :] = line


def weight_of(weights, p):
    return jnp.where(lane_of(HALO) < HALF, weights[2 * p], weights[2 * p + 1])[:1]


def fold(s):
    s = s + pltpu.roll(s, HALF, 1)
    middle = s.shape[0] // 2
    return jnp.where(lane_of(middle) < HALF, s[:middle], s[middle:])


def unfold(s):
    other = pltpu.roll(s, HALF, 1)
    low = lane_of(s.shape[0]) < HALF
    return jnp.where(low, s, other), jnp.where(low, other, s)


def first_residual(p, w, inverse_parts, parts, span, dens_ref, mat_ref, a_ref, e_ref, fr_ref, fp_ref, r_ref, inv):
    begin, end = span
    for lo, hi in inverse_parts:
        a, e = a_ref[(p, *at(lo, hi))], e_ref[(p, *at(lo, hi))]
        slope_r = 0.5 * (next_row(e) - prev_row(e))
        slope_p = 0.5 * (after(e_ref, (p,), lo, hi, e, end) - before(e_ref, (p,), lo, hi, e, begin))
        n2 = slope_r * slope_r + slope_p * slope_p
        u = a * e
        s = 2.0 * u + jnp.sqrt(n2)
        inv[lo:hi, :] = jnp.where(dens_ref[lo:hi, :] > 0.0, (n2 + 3.0 * u * s) / (e * s), OUTSIDE)
    for lo, hi in parts:
        d = inv[lo:hi, :]
        fr_ref[(p, *at(lo, hi))] = 2.0 / (d + next_row(d))
        fp_ref[(p, *at(lo, hi))] = 2.0 / (d + after(inv, (), lo, hi, d, end))
    for lo, hi in parts:
        a, e = a_ref[(p, *at(lo, hi))], e_ref[(p, *at(lo, hi))]
        r_ref[(p, *at(lo, hi))] = a * (w * mat_ref[lo:hi, :] - e) - flux_sum(
            p, lo, hi, e_ref, e, fr_ref, fp_ref, span
        )


def inner_kernel(
    groups, cols, weights, a_ref, e_ref, dens_ref, mat_ref,
    fr_ref, fp_ref, r_ref, q_ref, t_ref, emit, mom, inv,
):
    pairs = groups // 2
    span = (HALO, HALO + cols)
    parts = [(lo + HALO, hi + HALO) for lo, hi in pieces(cols)]
    own = (2 * HALO, cols)
    emit[...] = jnp.zeros(emit.shape, jnp.float32)

    def one(p, carry):
        w = weight_of(weights, p)
        for lo, hi in parts:
            emit[lo:hi, :] += a_ref[(p, *at(lo, hi))] * w
        first_residual(p, w, parts, parts, span, dens_ref, mat_ref, a_ref, e_ref, fr_ref, fp_ref, r_ref, inv)
        krylov(p, pairs, parts, span, own, a_ref, fr_ref, fp_ref, r_ref, q_ref, t_ref, mom)
        return carry

    lax.fori_loop(0, pairs, one, 0)


def frame_kernel(groups, rows, cols, weights, got_first, got_second, emit, old_mom, *rest):
    a_ref, e_ref, fr_ref, fp_ref, r_ref, q_ref, t_ref, dens_ref, mat_ref, emit_out, out, inv, mom = rest[9:]
    pairs = groups // 2
    tall = cols + 2 * HALO
    span = (0, tall)
    even, _, _ = partner("polar", 0, 0)
    ends = ((0, HALO), (tall - HALO, tall))

    def halo(side, plane):
        one, two = got_first[plane], got_second[plane]
        return jnp.where(even, two, one) if side == 0 else jnp.where(even, one, two)

    for side, (lo, hi) in enumerate(ends):
        dens_ref[lo:hi, :] = halo(side, 2 * pairs)
        mat_ref[lo:hi, :] = halo(side, 2 * pairs + 1)
    parts = [(0, HALO), (HALO, 2 * HALO), (cols, cols + HALO), (cols + HALO, tall)]
    inverse_parts = parts[:2] + [(2 * HALO, 3 * HALO)] + parts[2:]

    def one(p, emitted):
        w = weight_of(weights, p)
        sums = []
        for side, (lo, hi) in enumerate(ends):
            a = jnp.where(dens_ref[lo:hi, :] > 0.0, halo(side, p), 1.0)
            a_ref[(p, *at(lo, hi))] = a
            e_ref[(p, *at(lo, hi))] = halo(side, pairs + p)
            sums.append(emitted[side] + a * w)
        first_residual(
            p, w, inverse_parts, parts, span, dens_ref, mat_ref, a_ref, e_ref, fr_ref, fp_ref, r_ref, inv
        )
        krylov(
            p, pairs, parts, span, (HALO, HALO + cols), a_ref, fr_ref, fp_ref, r_ref, q_ref, t_ref, mom, old_mom
        )
        return tuple(sums)

    zero = jnp.zeros((HALO, LANES), jnp.float32)
    low, high = lax.fori_loop(0, pairs, one, (zero, zero))
    emit_out[...] = fold(jnp.concatenate([low, emit[HALO : HALO + cols, :], high], axis=0))
    row_sums = jnp.sum(tile_sum(dens_ref[HALO : HALO + cols, :]), axis=0, keepdims=True)
    send_moments(pairs, rows, mom, out, row_sums)


def steps(pairs, gathered):
    total = jnp.sum(gathered[...], axis=0, keepdims=True)
    lane = lane_of(pairs)
    sub = lax.broadcasted_iota(jnp.int32, (pairs, LANES), 0)

    def moment(k):
        first, second = (
            jnp.sum(jnp.where(lane == sub + (4 * h + k) * pairs, total, 0.0), axis=1, keepdims=True)
            for h in range(2)
        )
        return jnp.where(lane < HALF, first, second)

    m0, m1, m2, m3 = (moment(k) for k in range(4))
    k1, k2, k3 = m1 / m0, m2 / m0, m3 / m0
    first = 1.0 / k1
    det = jnp.maximum(k2 - k1 * k1, 0.0)
    beta = det / (k1 * k1)
    low = k1 * k3 - k2 * k2
    second = jnp.minimum(jnp.where(low > 0.0, k1 * det / low, 0.0), 1.0)
    return first + second * (1.0 + beta), first * second


def absorbed(pairs, c1, c2, a_ref, e_ref, r_ref, q_ref, e_out, s):
    tall = a_ref.shape[1]
    for lo, hi in pieces(tall):
        total = jnp.zeros((hi - lo, LANES), jnp.float32)
        for p in range(pairs):
            e = (
                e_ref[(p, *at(lo, hi))]
                + c1[p : p + 1, :] * r_ref[(p, *at(lo, hi))]
                - c2[p : p + 1, :] * q_ref[(p, *at(lo, hi))]
            )
            e_out[(p, *at(lo, hi))] = e
            total = total + a_ref[(p, *at(lo, hi))] * e
        s[lo:hi, :] = total


def update_kernel(pairs, gathered, a_ref, e_ref, r_ref, q_ref, *rest):
    if len(rest) == 6:
        emit, *rest = rest
    else:
        emit = None
    e_out, s_out, c1_ref, c2_ref, s = rest
    c1, c2 = steps(pairs, gathered)
    c1_ref[...] = c1
    c2_ref[...] = c2
    absorbed(pairs, c1, c2, a_ref, e_ref, r_ref, q_ref, e_out, s)
    s_out[0] = fold(s[...])
    if emit is not None:
        s_out[1] = emit[...]


def last_update_kernel(pairs, cols, gathered, a_ref, e_ref, r_ref, q_ref, e_out, s_out, s):
    c1, c2 = steps(pairs, gathered)
    absorbed(pairs, c1, c2, a_ref, e_ref, r_ref, q_ref, e_out, s)
    s_out[...] = fold(s[HALO : HALO + cols, :])


def energy_kernel(pairs, rows, cols, e_ref, out):
    def one(p, carry):
        for lo in range(0, cols, LANES):
            block = e_ref[p, HALO + lo : HALO + lo + LANES, :].T
            out[2 * p, :, lo : lo + LANES] = block[HALO : HALO + rows]
            out[2 * p + 1, :, lo : lo + LANES] = block[HALF + HALO : HALF + HALO + rows]
        return carry

    lax.fori_loop(0, pairs, one, 0)


def turned_back(v, rows):
    parts = [v[lo : lo + LANES].T[HALO : HALO + rows] for lo in range(0, v.shape[0], LANES)]
    return jnp.concatenate(parts, axis=1)


def heating_kernel(
    groups, rows, cols, polar_count, flux, gathered, dens_ref, mat_ref, flux_ref, column_out, fixed_out
):
    tall = dens_ref.shape[0]
    radius, polar = lax.axis_index("radius"), lax.axis_index("polar")
    dens = dens_ref[...]
    row_id = lax.broadcasted_iota(jnp.int32, gathered.shape, 0)
    ahead = (row_id >= radius * polar_count) & (row_id < radius * polar_count + polar)
    carried = jnp.sum(jnp.where(ahead, gathered[...], 0.0), axis=0, keepdims=True)
    lane = lane_of()
    carried = jnp.where(lane < HALF, pltpu.roll(carried, HALF, 1), carried)
    dst = lax.broadcasted_iota(jnp.int32, (tall, tall), 0)
    src = lax.broadcasted_iota(jnp.int32, (tall, tall), 1)
    coeff = jnp.where(
        (src >= HALO) & (src <= dst), 1.0, jnp.where((src < HALO) & (src > dst), -1.0, 0.0)
    )
    within = lax.dot_general(
        coeff, dens, (((1,), (0,)), ((), ())), precision=HIGHEST, preferred_element_type=jnp.float32
    )
    column = 2.0 / (cols * polar_count) * (carried + within)
    vec = flux_ref[0:1, :]
    for i in range(rows):
        vec = jnp.where(lane % HALF == HALO + i, flux[i], vec)
    fixed_out[...] = 16.0 * dens * mat_ref[...] + vec * dens * jnp.exp(-column)
    column_out[...] = turned_back(column[HALO : HALO + cols], rows)


def summed(refs, lead=()):
    total = refs[0][(*lead, ...)]
    for s in refs[1:]:
        total = total + s[(*lead, ...)]
    return total


def next_kernel(groups, rows, count, turn, last, weights, c1_ref, c2_ref, a_ref, fr_ref, fp_ref, r_in, q_in, t_in, fixed, cap_in, mat_ref, *rest):
    pairs = groups // 2
    sums = rest[:count]
    rest = rest[count:]
    outs, (delta, mom) = rest[:-2], rest[-2:]
    r_ref, q_ref, out, *outs = outs
    t_ref = None if last else outs.pop(0)
    m_ref = None if last else outs.pop(0)
    tall = fixed.shape[0]
    parts = pieces(tall)
    half = tall // 2
    folded = summed(sums, (0,))
    if turn == 0:
        cap_out = outs.pop(0)
        dens = cap_in[...]
        emits = jnp.concatenate(unfold(summed(sums, (1,))), axis=0)
        cap_out[...] = 16.0 * jnp.where(dens > 0.0, dens, 1.0) + emits
        cap_in = cap_out
    for k, total in enumerate(unfold(folded)):
        here = at(k * half, (k + 1) * half)
        nxt = (fixed[here] + total) / cap_in[here]
        delta[here] = nxt - mat_ref[here]
        if m_ref is not None:
            m_ref[here] = nxt

    def one(p, carry):
        w = weight_of(weights, p)
        c1 = c1_ref[pl.ds(p, 1), :]
        c2 = c2_ref[pl.ds(p, 1), :]
        for lo, hi in parts:
            here = (p, *at(lo, hi))
            r_ref[here] = (
                r_in[here] - c1 * q_in[here] + c2 * t_in[here] + a_ref[here] * (w * delta[lo:hi, :])
            )
        krylov(p, pairs, parts, (0, tall), (HALO, tall - HALO), a_ref, fr_ref, fp_ref, r_ref, q_ref, t_ref, mom)
        return carry

    lax.fori_loop(0, pairs, one, 0)
    send_moments(pairs, rows, mom, out, None)


def material_kernel(count, rows, cols, fixed, capacity, *rest):
    sums, out = rest[:count], rest[count]
    total = jnp.concatenate(unfold(summed(sums)), axis=0)
    here = at(HALO, HALO + cols)
    out[...] = turned_back((fixed[here] + total) / capacity[here], rows)


def spread(part, axis):
    count = lax.axis_size(axis)
    return [part] + [lax.ppermute(part, axis, [(i, i ^ s) for i in range(count)]) for s in range(1, count)]


def exchanged(first, second, axis):
    count = lax.axis_size(axis)
    got_first = lax.ppermute(first, axis, [(i, i ^ 1) for i in range(count)])
    links = [(i, i + 1) for i in range(1, count - 1, 2)]
    got_second = lax.ppermute(second, axis, links + [(j, i) for i, j in links])
    return got_first, got_second


def per_device(density, opacity, radiation_old, material_old, weights, stellar_flux):
    groups, rows, cols = opacity.shape
    pairs, tall = groups // 2, cols + 2 * HALO
    assert rows + 2 * HALO == HALF
    polar_count = lax.axis_size("polar")
    count = lax.axis_size("group")
    devices = lax.axis_size("radius") * polar_count
    planes = 2 * groups + 3
    big, flat, core = (pairs, tall, LANES), (tall, LANES), (cols, LANES)
    line = (devices, LANES)
    vmem = lambda shape: pltpu.VMEM(shape, jnp.float32)

    strips = [
        pltpu.VMEM((groups, 2 * HALO, cols), jnp.bfloat16),
        vmem((groups, HALO, cols)),
        vmem((HALO, cols)),
        vmem((HALO, cols)),
    ]
    first, second = call(
        functools.partial(pack_rows_kernel, groups, rows),
        [(planes, HALO, cols)] * 2,
        (stellar_flux, opacity, radiation_old, density, material_old),
        [sspec()] + [hspec()] * 4,
        scratch=strips * 2 + [pltpu.SemaphoreType.DMA((8,))],
        name="pack_rows",
        limit=60 * 1024 * 1024,
    )
    first, second = exchanged(first, second, "radius")
    a, e, dens, mat, flux_lanes, first, second = call(
        functools.partial(turn_kernel, groups, rows, cols),
        [big] * 2 + [flat, flat, (HALO, LANES)] + [(2 * pairs + 2, HALO, LANES)] * 2,
        (opacity, radiation_old, density, material_old, first, second),
        [vspec()] * 6,
        name="turn",
    )
    first, second = exchanged(first, second, "polar")
    fr, fp, r, q, t, emit, mom = call(
        functools.partial(inner_kernel, groups, cols),
        [big] * 5 + [flat, (4 * pairs, LANES)],
        (weights, a, e, dens, mat),
        [sspec()] + [vspec()] * 4,
        scratch=[vmem(flat)],
        name="inner",
    )
    a, e, fr, fp, r, q, t, dens, mat, emit, out = call(
        functools.partial(frame_kernel, groups, rows, cols),
        [big] * 7 + [flat, flat, (tall // 2, LANES), line],
        (weights, first, second, emit, mom, a, e, fr, fp, r, q, t, dens, mat),
        [sspec()] + [vspec()] * 13,
        scratch=[vmem(flat), vmem((4 * pairs, LANES))],
        name="frame",
        aliases={5 + k: k for k in range(9)},
    )
    capacity = dens
    for turn in range(ITERS):
        gathered = lax.all_to_all(out, ("radius", "polar"), 0, 0, tiled=True)
        if turn + 1 == ITERS:
            e, part = call(
                functools.partial(last_update_kernel, pairs, cols),
                [big, (cols // 2, LANES)],
                (gathered, a, e, r, q),
                [vspec()] * 5,
                scratch=[vmem(flat)],
                name="last_update",
            )
            sums = spread(part, "group")
            (energy,) = call(
                functools.partial(energy_kernel, pairs, rows, cols),
                [(groups, rows, cols)],
                (e,),
                [vspec()],
                name="energy",
            )
            (mat,) = call(
                functools.partial(material_kernel, count, rows, cols),
                [(rows, cols)],
                (fixed, capacity, *sums),
                [vspec()] * (2 + count),
                name="material",
            )
            break
        first, last = turn == 0, turn + 2 == ITERS
        extra = [emit] if first else []
        e, part, c1, c2 = call(
            functools.partial(update_kernel, pairs),
            [big, (1 + len(extra), tall // 2, LANES), (pairs, LANES), (pairs, LANES)],
            (gathered, a, e, r, q, *extra),
            [vspec()] * (5 + len(extra)),
            scratch=[vmem(flat)],
            name="update",
        )
        sums = spread(part, "group")
        if first:
            column, fixed = call(
                functools.partial(heating_kernel, groups, rows, cols, polar_count),
                [(rows, cols), flat],
                (stellar_flux, gathered, dens, mat, flux_lanes),
                [sspec()] + [vspec()] * 4,
                name="heating",
            )
        r, q, out, *more = call(
            functools.partial(next_kernel, groups, rows, count, turn, last),
            [big, big, line] + ([] if last else [big, flat]) + ([flat] if first else []),
            (weights, c1, c2, a, fr, fp, r, q, t, fixed, capacity, mat, *sums),
            [sspec()] + [vspec()] * (11 + count),
            scratch=[vmem(flat), vmem((4 * pairs, LANES))],
            name="next",
        )
        if not last:
            t, mat, *more = more
        if first:
            (capacity,) = more
    return (energy, mat, column)


def solution(mesh):
    return jax.shard_map(
        per_device,
        mesh=mesh,
        in_specs=(
            P("radius", "polar"),
            P("group", "radius", "polar"),
            P("group", "radius", "polar"),
            P("radius", "polar"),
            P("group"),
            P("radius"),
        ),
        out_specs=(P("group", "radius", "polar"), P("radius", "polar"), P("radius", "polar")),
        check_vma=False,
    )
```

```python
import functools
import jax
import jax.numpy as jnp
from jax import lax
from jax.experimental import pallas as pl
from jax.experimental.pallas import tpu as pltpu
from jax.sharding import PartitionSpec as P


ITERS = 3
HALO = 8
LANES = 128
HALF = LANES // 2
STEP = 64
VMEM_LIMIT = 12 * 1024 * 1024
HIGHEST = lax.Precision.HIGHEST
OUTSIDE = 1.6e38


def vspec():
    return pl.BlockSpec(memory_space=pltpu.VMEM)


def sspec():
    return pl.BlockSpec(memory_space=pltpu.SMEM)


def hspec():
    return pl.BlockSpec(memory_space=pltpu.HBM)


def call(kernel, outs, args, specs, scratch=(), flops=1000000, nbytes=1000000, name=None, limit=VMEM_LIMIT, aliases=None):
    return pl.pallas_call(
        kernel,
        out_shape=[jax.ShapeDtypeStruct(s, jnp.float32) for s in outs],
        in_specs=specs,
        out_specs=[vspec() for _ in outs],
        scratch_shapes=list(scratch),
        compiler_params=pltpu.CompilerParams(vmem_limit_bytes=limit),
        cost_estimate=pl.CostEstimate(flops=flops, bytes_accessed=nbytes, transcendentals=0),
        name=name,
        input_output_aliases=aliases or {},
    )(*args)


def lane_of(height=1):
    return lax.broadcasted_iota(jnp.int32, (height, LANES), 1)


def pieces(tall):
    cuts = [0, HALO]
    while cuts[-1] + STEP < tall - HALO:
        cuts.append(cuts[-1] + STEP)
    cuts += [tall - HALO, tall]
    return list(zip(cuts[:-1], cuts[1:]))


def partner(axis, inner, outer):
    even = lax.rem(lax.axis_index(axis), 2) == 0
    return even, jnp.where(even, inner, outer), jnp.where(even, outer, inner)


def pack_rows_kernel(groups, rows, flux, opacity, old, density, material, first, second, *scratch):
    even, lo_first, lo_second = partner("radius", rows - HALO, 0)
    sems = scratch[-1]
    sides = ((first, lo_first, even), (second, lo_second, jnp.logical_not(even)))
    copies = []
    for side, (_, lo, at_end) in enumerate(sides):
        op_buf, old_buf, dens_buf, mat_buf = scratch[4 * side : 4 * side + 4]
        lo = pl.multiple_of(lo, HALO)
        base = pl.multiple_of(jnp.where(at_end, rows - 2 * HALO, 0), 2 * HALO)
        moves = (
            (opacity.at[:, pl.ds(base, 2 * HALO), :], op_buf),
            (old.at[:, pl.ds(lo, HALO), :], old_buf),
            (density.at[pl.ds(lo, HALO), :], dens_buf),
            (material.at[pl.ds(lo, HALO), :], mat_buf),
        )
        for k, (src, dst) in enumerate(moves):
            copies.append(pltpu.make_async_copy(src, dst, sems.at[4 * side + k]))
    for c in copies:
        c.start()
    for c in copies:
        c.wait()
    lane = lane_of(HALO) % HALF
    for side, (out, lo, at_end) in enumerate(sides):
        op_buf, old_buf, dens_buf, mat_buf = scratch[4 * side : 4 * side + 4]
        dens = dens_buf[...]
        for g in range(groups):
            part = op_buf[g].astype(jnp.float32)
            out[g] = jnp.where(at_end, part[HALO:], part[:HALO]) * dens
            out[groups + g] = old_buf[g]
        out[2 * groups] = dens
        out[2 * groups + 1] = mat_buf[...]
        place = jnp.where(at_end, 0, rows + HALO)
        vec = jnp.zeros((HALO, LANES), jnp.float32)
        for i in range(HALO):
            vec = jnp.where(lane == place + i, flux[lo + i], vec)
        for at_lane in range(0, out.shape[2], LANES):
            out[2 * groups + 2, :, at_lane : at_lane + LANES] = vec


def turn_kernel(
    groups, rows, cols, opacity, old, density, material, got_first, got_second,
    a_ref, e_ref, dens_ref, mat_ref, flux_ref, to_first, to_second,
):
    pairs = groups // 2
    plane_of_flux = 2 * groups + 2
    flux_ref[...] = got_first[plane_of_flux, :, :LANES] + got_second[plane_of_flux, :, :LANES]
    even, _, _ = partner("radius", 0, 0)
    for lo in range(0, cols, LANES):
        hi = lo + LANES

        def tile(plane, own):
            one, two = got_first[plane, :, lo:hi], got_second[plane, :, lo:hi]
            return jnp.concatenate([jnp.where(even, two, one), own, jnp.where(even, one, two)], axis=0)

        d = tile(2 * groups, density[:, lo:hi])
        d = jnp.concatenate([d, d], axis=0).T
        m = tile(2 * groups + 1, material[:, lo:hi])
        m = jnp.concatenate([m, m], axis=0).T
        dens_ref[HALO + lo : HALO + hi, :] = d
        mat_ref[HALO + lo : HALO + hi, :] = m

        def one(p, carry):
            both = []
            for h in range(2):
                g = 2 * p + h
                both.append(tile(g, opacity[g, :, lo:hi].astype(jnp.float32) * density[:, lo:hi]))
            a = jnp.concatenate(both, axis=0).T
            a_ref[p, HALO + lo : HALO + hi, :] = jnp.where(dens_ref[HALO + lo : HALO + hi, :] > 0.0, a, 1.0)
            both = [tile(groups + 2 * p + h, old[2 * p + h, :, lo:hi]) for h in range(2)]
            e_ref[p, HALO + lo : HALO + hi, :] = jnp.concatenate(both, axis=0).T
            return carry

        lax.fori_loop(0, pairs, one, 0, unroll=8)
    _, lo_first, lo_second = partner("polar", cols, HALO)
    for out, lo in ((to_first, lo_first), (to_second, lo_second)):
        edge = pl.ds(pl.multiple_of(lo, HALO), HALO)
        for p in range(pairs):
            out[p] = a_ref[p, edge, :]
            out[pairs + p] = e_ref[p, edge, :]
        out[2 * pairs] = dens_ref[edge, :]
        out[2 * pairs + 1] = mat_ref[edge, :]


def next_row(v):
    return pltpu.roll(v, LANES - 1, 1)


def prev_row(v):
    return pltpu.roll(v, 1, 1)


def after(ref, lead, lo, hi, here, end):
    if hi < end:
        return ref[(*lead, slice(lo + 1, hi + 1), slice(None))]
    return pltpu.roll(here, hi - lo - 1, 0)


def before(ref, lead, lo, hi, here, begin):
    if lo > begin:
        return ref[(*lead, slice(lo - 1, hi - 1), slice(None))]
    return pltpu.roll(here, 1, 0)


def at(lo, hi):
    return (slice(lo, hi), slice(None))


def flux_sum(p, lo, hi, v_ref, v, fr_ref, fp_ref, span):
    begin, end = span
    fp = fp_ref[(p, *at(lo, hi))]
    fp_before = before(fp_ref, (p,), lo, hi, fp, begin)
    polar = fp * (v - after(v_ref, (p,), lo, hi, v, end)) + fp_before * (
        v - before(v_ref, (p,), lo, hi, v, begin)
    )
    fr = fr_ref[(p, *at(lo, hi))] * (v - next_row(v))
    return polar + (fr - prev_row(fr))


def tile_sum(v):
    acc = v[:HALO]
    for lo in range(HALO, v.shape[0], HALO):
        acc = acc + v[lo : lo + HALO]
    return acc


def krylov(p, pairs, parts, span, own, a_ref, fr_ref, fp_ref, r_ref, q_ref, t_ref, mom, old_mom=None):
    sums = [jnp.zeros((HALO, LANES), jnp.float32) for _ in range(4)]
    for lo, hi in parts:
        r = r_ref[(p, *at(lo, hi))]
        q = r + a_ref[(p, *at(lo, hi))] * r + flux_sum(p, lo, hi, r_ref, r, fr_ref, fp_ref, span)
        q_ref[(p, *at(lo, hi))] = q
        if lo >= own[0] and hi <= own[1]:
            sums[0] = sums[0] + tile_sum(r * r)
            sums[1] = sums[1] + tile_sum(r * q)
            sums[2] = sums[2] + tile_sum(q * q)
    for lo, hi in parts:
        inside = lo >= own[0] and hi <= own[1]
        if not inside and t_ref is None:
            continue
        q = q_ref[(p, *at(lo, hi))]
        t = q + a_ref[(p, *at(lo, hi))] * q + flux_sum(p, lo, hi, q_ref, q, fr_ref, fp_ref, span)
        if t_ref is not None:
            t_ref[(p, *at(lo, hi))] = t
        if inside:
            sums[3] = sums[3] + tile_sum(q * t)
    for k in range(4):
        total = jnp.sum(sums[k], axis=0, keepdims=True)
        if old_mom is not None:
            total = total + old_mom[pl.ds(k * pairs + p, 1), :]
        mom[pl.ds(k * pairs + p, 1), :] = total


def send_moments(pairs, rows, mom, out, row_sums):
    lane = lane_of(4 * pairs)
    x = mom[...]
    first = jnp.where((lane >= HALO) & (lane < HALO + rows), x, 0.0)
    second = jnp.where((lane >= HALF + HALO) & (lane < HALF + HALO + rows), x, 0.0)
    both = jnp.concatenate([first, second, jnp.zeros((LANES - 8 * pairs, LANES), jnp.float32)], axis=0)
    line = lax.dot_general(
        jnp.ones((HALO, LANES), jnp.float32), both, (((1,), (1,)), ((), ())),
        precision=HIGHEST, preferred_element_type=jnp.float32,
    )
    if row_sums is not None:
        line = jnp.where(lane_of(HALO) < HALF, line, row_sums)
    for lo in range(0, out.shape[0], HALO):
        out[lo : lo + HALO, :] = line


def weight_of(weights, p):
    return jnp.where(lane_of(HALO) < HALF, weights[2 * p], weights[2 * p + 1])[:1]


def fold(s):
    s = s + pltpu.roll(s, HALF, 1)
    middle = s.shape[0] // 2
    return jnp.where(lane_of(middle) < HALF, s[:middle], s[middle:])


def unfold(s):
    other = pltpu.roll(s, HALF, 1)
    low = lane_of(s.shape[0]) < HALF
    return jnp.where(low, s, other), jnp.where(low, other, s)


def first_residual(p, w, inverse_parts, parts, span, dens_ref, mat_ref, a_ref, e_ref, fr_ref, fp_ref, r_ref, inv):
    begin, end = span
    for lo, hi in inverse_parts:
        a, e = a_ref[(p, *at(lo, hi))], e_ref[(p, *at(lo, hi))]
        slope_r = 0.5 * (next_row(e) - prev_row(e))
        slope_p = 0.5 * (after(e_ref, (p,), lo, hi, e, end) - before(e_ref, (p,), lo, hi, e, begin))
        n2 = slope_r * slope_r + slope_p * slope_p
        u = a * e
        s = 2.0 * u + jnp.sqrt(n2)
        inv[lo:hi, :] = jnp.where(dens_ref[lo:hi, :] > 0.0, (n2 + 3.0 * u * s) / (e * s), OUTSIDE)
    for lo, hi in parts:
        d = inv[lo:hi, :]
        fr_ref[(p, *at(lo, hi))] = 2.0 / (d + next_row(d))
        fp_ref[(p, *at(lo, hi))] = 2.0 / (d + after(inv, (), lo, hi, d, end))
    for lo, hi in parts:
        a, e = a_ref[(p, *at(lo, hi))], e_ref[(p, *at(lo, hi))]
        r_ref[(p, *at(lo, hi))] = a * (w * mat_ref[lo:hi, :] - e) - flux_sum(
            p, lo, hi, e_ref, e, fr_ref, fp_ref, span
        )


def inner_kernel(
    groups, cols, weights, a_ref, e_ref, dens_ref, mat_ref,
    fr_ref, fp_ref, r_ref, q_ref, t_ref, emit, mom, inv,
):
    pairs = groups // 2
    span = (HALO, HALO + cols)
    parts = [(lo + HALO, hi + HALO) for lo, hi in pieces(cols)]
    own = (2 * HALO, cols)
    emit[...] = jnp.zeros(emit.shape, jnp.float32)

    def one(p, carry):
        w = weight_of(weights, p)
        for lo, hi in parts:
            emit[lo:hi, :] += a_ref[(p, *at(lo, hi))] * w
        first_residual(p, w, parts, parts, span, dens_ref, mat_ref, a_ref, e_ref, fr_ref, fp_ref, r_ref, inv)
        krylov(p, pairs, parts, span, own, a_ref, fr_ref, fp_ref, r_ref, q_ref, t_ref, mom)
        return carry

    lax.fori_loop(0, pairs, one, 0, unroll=2)


def frame_kernel(groups, rows, cols, weights, got_first, got_second, emit, old_mom, *rest):
    a_ref, e_ref, fr_ref, fp_ref, r_ref, q_ref, t_ref, dens_ref, mat_ref, emit_out, out, inv, mom = rest[9:]
    pairs = groups // 2
    tall = cols + 2 * HALO
    span = (0, tall)
    even, _, _ = partner("polar", 0, 0)
    ends = ((0, HALO), (tall - HALO, tall))

    def halo(side, plane):
        one, two = got_first[plane], got_second[plane]
        return jnp.where(even, two, one) if side == 0 else jnp.where(even, one, two)

    for side, (lo, hi) in enumerate(ends):
        dens_ref[lo:hi, :] = halo(side, 2 * pairs)
        mat_ref[lo:hi, :] = halo(side, 2 * pairs + 1)
    parts = [(0, HALO), (HALO, 2 * HALO), (cols, cols + HALO), (cols + HALO, tall)]
    inverse_parts = parts[:2] + [(2 * HALO, 3 * HALO)] + parts[2:]

    def one(p, emitted):
        w = weight_of(weights, p)
        sums = []
        for side, (lo, hi) in enumerate(ends):
            a = jnp.where(dens_ref[lo:hi, :] > 0.0, halo(side, p), 1.0)
            a_ref[(p, *at(lo, hi))] = a
            e_ref[(p, *at(lo, hi))] = halo(side, pairs + p)
            sums.append(emitted[side] + a * w)
        first_residual(
            p, w, inverse_parts, parts, span, dens_ref, mat_ref, a_ref, e_ref, fr_ref, fp_ref, r_ref, inv
        )
        krylov(
            p, pairs, parts, span, (HALO, HALO + cols), a_ref, fr_ref, fp_ref, r_ref, q_ref, t_ref, mom, old_mom
        )
        return tuple(sums)

    zero = jnp.zeros((HALO, LANES), jnp.float32)
    low, high = lax.fori_loop(0, pairs, one, (zero, zero), unroll=8)
    emit_out[...] = fold(jnp.concatenate([low, emit[HALO : HALO + cols, :], high], axis=0))
    row_sums = jnp.sum(tile_sum(dens_ref[HALO : HALO + cols, :]), axis=0, keepdims=True)
    send_moments(pairs, rows, mom, out, row_sums)


def steps(pairs, gathered):
    total = jnp.sum(gathered[...], axis=0, keepdims=True)
    lane = lane_of(pairs)
    sub = lax.broadcasted_iota(jnp.int32, (pairs, LANES), 0)

    def moment(k):
        first, second = (
            jnp.sum(jnp.where(lane == sub + (4 * h + k) * pairs, total, 0.0), axis=1, keepdims=True)
            for h in range(2)
        )
        return jnp.where(lane < HALF, first, second)

    m0, m1, m2, m3 = (moment(k) for k in range(4))
    k1, k2, k3 = m1 / m0, m2 / m0, m3 / m0
    first = 1.0 / k1
    det = jnp.maximum(k2 - k1 * k1, 0.0)
    beta = det / (k1 * k1)
    low = k1 * k3 - k2 * k2
    second = jnp.minimum(jnp.where(low > 0.0, k1 * det / low, 0.0), 1.0)
    return first + second * (1.0 + beta), first * second


def absorbed(pairs, c1, c2, a_ref, e_ref, r_ref, q_ref, e_out, s):
    tall = a_ref.shape[1]
    for lo, hi in pieces(tall):
        total = jnp.zeros((hi - lo, LANES), jnp.float32)
        for p in range(pairs):
            e = (
                e_ref[(p, *at(lo, hi))]
                + c1[p : p + 1, :] * r_ref[(p, *at(lo, hi))]
                - c2[p : p + 1, :] * q_ref[(p, *at(lo, hi))]
            )
            e_out[(p, *at(lo, hi))] = e
            total = total + a_ref[(p, *at(lo, hi))] * e
        s[lo:hi, :] = total


def update_kernel(pairs, gathered, a_ref, e_ref, r_ref, q_ref, *rest):
    if len(rest) == 6:
        emit, *rest = rest
    else:
        emit = None
    e_out, s_out, c1_ref, c2_ref, s = rest
    c1, c2 = steps(pairs, gathered)
    c1_ref[...] = c1
    c2_ref[...] = c2
    absorbed(pairs, c1, c2, a_ref, e_ref, r_ref, q_ref, e_out, s)
    s_out[0] = fold(s[...])
    if emit is not None:
        s_out[1] = emit[...]


def last_update_kernel(pairs, cols, gathered, a_ref, e_ref, r_ref, q_ref, e_out, s_out, s):
    c1, c2 = steps(pairs, gathered)
    absorbed(pairs, c1, c2, a_ref, e_ref, r_ref, q_ref, e_out, s)
    s_out[...] = fold(s[HALO : HALO + cols, :])


def energy_kernel(pairs, rows, cols, e_ref, out):
    def one(p, carry):
        for lo in range(0, cols, LANES):
            block = e_ref[p, HALO + lo : HALO + lo + LANES, :].T
            out[2 * p, :, lo : lo + LANES] = block[HALO : HALO + rows]
            out[2 * p + 1, :, lo : lo + LANES] = block[HALF + HALO : HALF + HALO + rows]
        return carry

    lax.fori_loop(0, pairs, one, 0, unroll=4)


def turned_back(v, rows):
    parts = [v[lo : lo + LANES].T[HALO : HALO + rows] for lo in range(0, v.shape[0], LANES)]
    return jnp.concatenate(parts, axis=1)


def heating_kernel(
    groups, rows, cols, polar_count, flux, gathered, dens_ref, mat_ref, flux_ref, column_out, fixed_out
):
    tall = dens_ref.shape[0]
    radius, polar = lax.axis_index("radius"), lax.axis_index("polar")
    dens = dens_ref[...]
    row_id = lax.broadcasted_iota(jnp.int32, gathered.shape, 0)
    ahead = (row_id >= radius * polar_count) & (row_id < radius * polar_count + polar)
    carried = jnp.sum(jnp.where(ahead, gathered[...], 0.0), axis=0, keepdims=True)
    lane = lane_of()
    carried = jnp.where(lane < HALF, pltpu.roll(carried, HALF, 1), carried)
    dst = lax.broadcasted_iota(jnp.int32, (tall, tall), 0)
    src = lax.broadcasted_iota(jnp.int32, (tall, tall), 1)
    coeff = jnp.where(
        (src >= HALO) & (src <= dst), 1.0, jnp.where((src < HALO) & (src > dst), -1.0, 0.0)
    )
    within = lax.dot_general(
        coeff, dens, (((1,), (0,)), ((), ())), precision=HIGHEST, preferred_element_type=jnp.float32
    )
    column = 2.0 / (cols * polar_count) * (carried + within)
    vec = flux_ref[0:1, :]
    for i in range(rows):
        vec = jnp.where(lane % HALF == HALO + i, flux[i], vec)
    fixed_out[...] = 16.0 * dens * mat_ref[...] + vec * dens * jnp.exp(-column)
    column_out[...] = turned_back(column[HALO : HALO + cols], rows)


def summed(refs, lead=()):
    total = refs[0][(*lead, ...)]
    for s in refs[1:]:
        total = total + s[(*lead, ...)]
    return total


def next_kernel(groups, rows, count, turn, last, weights, c1_ref, c2_ref, a_ref, fr_ref, fp_ref, r_in, q_in, t_in, fixed, cap_in, mat_ref, *rest):
    pairs = groups // 2
    sums = rest[:count]
    rest = rest[count:]
    outs, (delta, mom) = rest[:-2], rest[-2:]
    r_ref, q_ref, out, *outs = outs
    t_ref = None if last else outs.pop(0)
    m_ref = None if last else outs.pop(0)
    tall = fixed.shape[0]
    parts = pieces(tall)
    half = tall // 2
    folded = summed(sums, (0,))
    if turn == 0:
        cap_out = outs.pop(0)
        dens = cap_in[...]
        emits = jnp.concatenate(unfold(summed(sums, (1,))), axis=0)
        cap_out[...] = 16.0 * jnp.where(dens > 0.0, dens, 1.0) + emits
        cap_in = cap_out
    for k, total in enumerate(unfold(folded)):
        here = at(k * half, (k + 1) * half)
        nxt = (fixed[here] + total) / cap_in[here]
        delta[here] = nxt - mat_ref[here]
        if m_ref is not None:
            m_ref[here] = nxt

    def one(p, carry):
        w = weight_of(weights, p)
        c1 = c1_ref[pl.ds(p, 1), :]
        c2 = c2_ref[pl.ds(p, 1), :]
        for lo, hi in parts:
            here = (p, *at(lo, hi))
            r_ref[here] = (
                r_in[here] - c1 * q_in[here] + c2 * t_in[here] + a_ref[here] * (w * delta[lo:hi, :])
            )
        krylov(p, pairs, parts, (0, tall), (HALO, tall - HALO), a_ref, fr_ref, fp_ref, r_ref, q_ref, t_ref, mom)
        return carry

    lax.fori_loop(0, pairs, one, 0, unroll=2)
    send_moments(pairs, rows, mom, out, None)


def material_kernel(count, rows, cols, fixed, capacity, *rest):
    sums, out = rest[:count], rest[count]
    total = jnp.concatenate(unfold(summed(sums)), axis=0)
    here = at(HALO, HALO + cols)
    out[...] = turned_back((fixed[here] + total) / capacity[here], rows)


def spread(part, axis):
    count = lax.axis_size(axis)
    return [part] + [lax.ppermute(part, axis, [(i, i ^ s) for i in range(count)]) for s in range(1, count)]


def exchanged(first, second, axis):
    count = lax.axis_size(axis)
    got_first = lax.ppermute(first, axis, [(i, i ^ 1) for i in range(count)])
    links = [(i, i + 1) for i in range(1, count - 1, 2)]
    got_second = lax.ppermute(second, axis, links + [(j, i) for i, j in links])
    return got_first, got_second


def per_device(density, opacity, radiation_old, material_old, weights, stellar_flux):
    groups, rows, cols = opacity.shape
    pairs, tall = groups // 2, cols + 2 * HALO
    assert rows + 2 * HALO == HALF
    polar_count = lax.axis_size("polar")
    count = lax.axis_size("group")
    devices = lax.axis_size("radius") * polar_count
    planes = 2 * groups + 3
    big, flat, core = (pairs, tall, LANES), (tall, LANES), (cols, LANES)
    line = (devices, LANES)
    vmem = lambda shape: pltpu.VMEM(shape, jnp.float32)

    strips = [
        pltpu.VMEM((groups, 2 * HALO, cols), jnp.bfloat16),
        vmem((groups, HALO, cols)),
        vmem((HALO, cols)),
        vmem((HALO, cols)),
    ]
    first, second = call(
        functools.partial(pack_rows_kernel, groups, rows),
        [(planes, HALO, cols)] * 2,
        (stellar_flux, opacity, radiation_old, density, material_old),
        [sspec()] + [hspec()] * 4,
        scratch=strips * 2 + [pltpu.SemaphoreType.DMA((8,))],
        name="pack_rows",
        limit=60 * 1024 * 1024,
    )
    first, second = exchanged(first, second, "radius")
    a, e, dens, mat, flux_lanes, first, second = call(
        functools.partial(turn_kernel, groups, rows, cols),
        [big] * 2 + [flat, flat, (HALO, LANES)] + [(2 * pairs + 2, HALO, LANES)] * 2,
        (opacity, radiation_old, density, material_old, first, second),
        [vspec()] * 6,
        name="turn",
    )
    first, second = exchanged(first, second, "polar")
    fr, fp, r, q, t, emit, mom = call(
        functools.partial(inner_kernel, groups, cols),
        [big] * 5 + [flat, (4 * pairs, LANES)],
        (weights, a, e, dens, mat),
        [sspec()] + [vspec()] * 4,
        scratch=[vmem(flat)],
        name="inner",
    )
    a, e, fr, fp, r, q, t, dens, mat, emit, out = call(
        functools.partial(frame_kernel, groups, rows, cols),
        [big] * 7 + [flat, flat, (tall // 2, LANES), line],
        (weights, first, second, emit, mom, a, e, fr, fp, r, q, t, dens, mat),
        [sspec()] + [vspec()] * 13,
        scratch=[vmem(flat), vmem((4 * pairs, LANES))],
        name="frame",
        aliases={5 + k: k for k in range(9)},
    )
    capacity = dens
    for turn in range(ITERS):
        gathered = lax.all_to_all(out, ("radius", "polar"), 0, 0, tiled=True)
        if turn + 1 == ITERS:
            e, part = call(
                functools.partial(last_update_kernel, pairs, cols),
                [big, (cols // 2, LANES)],
                (gathered, a, e, r, q),
                [vspec()] * 5,
                scratch=[vmem(flat)],
                name="last_update",
            )
            sums = spread(part, "group")
            (energy,) = call(
                functools.partial(energy_kernel, pairs, rows, cols),
                [(groups, rows, cols)],
                (e,),
                [vspec()],
                name="energy",
            )
            (mat,) = call(
                functools.partial(material_kernel, count, rows, cols),
                [(rows, cols)],
                (fixed, capacity, *sums),
                [vspec()] * (2 + count),
                name="material",
            )
            break
        first, last = turn == 0, turn + 2 == ITERS
        extra = [emit] if first else []
        e, part, c1, c2 = call(
            functools.partial(update_kernel, pairs),
            [big, (1 + len(extra), tall // 2, LANES), (pairs, LANES), (pairs, LANES)],
            (gathered, a, e, r, q, *extra),
            [vspec()] * (5 + len(extra)),
            scratch=[vmem(flat)],
            name="update",
        )
        sums = spread(part, "group")
        if first:
            column, fixed = call(
                functools.partial(heating_kernel, groups, rows, cols, polar_count),
                [(rows, cols), flat],
                (stellar_flux, gathered, dens, mat, flux_lanes),
                [sspec()] + [vspec()] * 4,
                name="heating",
            )
        r, q, out, *more = call(
            functools.partial(next_kernel, groups, rows, count, turn, last),
            [big, big, line] + ([] if last else [big, flat]) + ([flat] if first else []),
            (weights, c1, c2, a, fr, fp, r, q, t, fixed, capacity, mat, *sums),
            [sspec()] + [vspec()] * (11 + count),
            scratch=[vmem(flat), vmem((4 * pairs, LANES))],
            name="next",
        )
        if not last:
            t, mat, *more = more
        if first:
            (capacity,) = more
    return (energy, mat, column)


def solution(mesh):
    return jax.shard_map(
        per_device,
        mesh=mesh,
        in_specs=(
            P("radius", "polar"),
            P("group", "radius", "polar"),
            P("group", "radius", "polar"),
            P("radius", "polar"),
            P("group"),
            P("radius"),
        ),
        out_specs=(P("group", "radius", "polar"), P("radius", "polar"), P("radius", "polar")),
        check_vma=False,
    )
```

```python
import functools
import jax
import jax.numpy as jnp
from jax import lax
from jax.experimental import pallas as pl
from jax.experimental.pallas import tpu as pltpu
from jax.sharding import PartitionSpec as P


ITERS = 3
HALO = 8
LANES = 128
HALF = LANES // 2
STEP = 64
VMEM_LIMIT = 12 * 1024 * 1024
HIGHEST = lax.Precision.HIGHEST
OUTSIDE = 1.6e38


def vspec():
    return pl.BlockSpec(memory_space=pltpu.VMEM)


def sspec():
    return pl.BlockSpec(memory_space=pltpu.SMEM)


def hspec():
    return pl.BlockSpec(memory_space=pltpu.HBM)


def call(kernel, outs, args, specs, scratch=(), flops=1000000, nbytes=1000000, name=None, limit=VMEM_LIMIT, aliases=None):
    return pl.pallas_call(
        kernel,
        out_shape=[jax.ShapeDtypeStruct(s, jnp.float32) for s in outs],
        in_specs=specs,
        out_specs=[vspec() for _ in outs],
        scratch_shapes=list(scratch),
        compiler_params=pltpu.CompilerParams(vmem_limit_bytes=limit),
        cost_estimate=pl.CostEstimate(flops=flops, bytes_accessed=nbytes, transcendentals=0),
        name=name,
        input_output_aliases=aliases or {},
    )(*args)


def lane_of(height=1):
    return lax.broadcasted_iota(jnp.int32, (height, LANES), 1)


def pieces(tall):
    cuts = [0, HALO]
    while cuts[-1] + STEP < tall - HALO:
        cuts.append(cuts[-1] + STEP)
    cuts += [tall - HALO, tall]
    return list(zip(cuts[:-1], cuts[1:]))


def partner(axis, inner, outer):
    even = lax.rem(lax.axis_index(axis), 2) == 0
    return even, jnp.where(even, inner, outer), jnp.where(even, outer, inner)


def pack_rows_kernel(groups, rows, flux_in, opacity, old, density, material, first, second, *scratch):
    even, lo_first, lo_second = partner("radius", rows - HALO, 0)
    flux, sems = scratch[-2:]
    sides = ((first, lo_first, even), (second, lo_second, jnp.logical_not(even)))
    copies = [pltpu.make_async_copy(flux_in, flux, sems.at[8])]
    for side, (_, lo, at_end) in enumerate(sides):
        op_buf, old_buf, dens_buf, mat_buf = scratch[4 * side : 4 * side + 4]
        lo = pl.multiple_of(lo, HALO)
        base = pl.multiple_of(jnp.where(at_end, rows - 2 * HALO, 0), 2 * HALO)
        moves = (
            (opacity.at[:, pl.ds(base, 2 * HALO), :], op_buf),
            (old.at[:, pl.ds(lo, HALO), :], old_buf),
            (density.at[pl.ds(lo, HALO), :], dens_buf),
            (material.at[pl.ds(lo, HALO), :], mat_buf),
        )
        for k, (src, dst) in enumerate(moves):
            copies.append(pltpu.make_async_copy(src, dst, sems.at[4 * side + k]))
    for c in copies:
        c.start()
    for c in copies:
        c.wait()
    lane = lane_of(HALO) % HALF
    for side, (out, lo, at_end) in enumerate(sides):
        op_buf, old_buf, dens_buf, mat_buf = scratch[4 * side : 4 * side + 4]
        dens = dens_buf[...]
        for g in range(groups):
            part = op_buf[g].astype(jnp.float32)
            out[g] = jnp.where(at_end, part[HALO:], part[:HALO]) * dens
            out[groups + g] = old_buf[g]
        out[2 * groups] = dens
        out[2 * groups + 1] = mat_buf[...]
        place = jnp.where(at_end, 0, rows + HALO)
        vec = jnp.zeros((HALO, LANES), jnp.float32)
        for i in range(HALO):
            vec = jnp.where(lane == place + i, flux[lo + i], vec)
        for at_lane in range(0, out.shape[2], LANES):
            out[2 * groups + 2, :, at_lane : at_lane + LANES] = vec


def turn_kernel(
    groups, rows, cols, opacity, old, density, material, got_first, got_second,
    a_ref, e_ref, dens_ref, mat_ref, flux_ref, to_first, to_second,
):
    pairs = groups // 2
    plane_of_flux = 2 * groups + 2
    flux_ref[...] = got_first[plane_of_flux, :, :LANES] + got_second[plane_of_flux, :, :LANES]
    even, _, _ = partner("radius", 0, 0)
    for lo in range(0, cols, LANES):
        hi = lo + LANES

        def tile(plane, own):
            one, two = got_first[plane, :, lo:hi], got_second[plane, :, lo:hi]
            return jnp.concatenate([jnp.where(even, two, one), own, jnp.where(even, one, two)], axis=0)

        d = tile(2 * groups, density[:, lo:hi])
        d = jnp.concatenate([d, d], axis=0).T
        m = tile(2 * groups + 1, material[:, lo:hi])
        m = jnp.concatenate([m, m], axis=0).T
        dens_ref[HALO + lo : HALO + hi, :] = d
        mat_ref[HALO + lo : HALO + hi, :] = m

        def one(p, carry):
            both = []
            for h in range(2):
                g = 2 * p + h
                both.append(tile(g, opacity[g, :, lo:hi].astype(jnp.float32) * density[:, lo:hi]))
            a = jnp.concatenate(both, axis=0).T
            a_ref[p, HALO + lo : HALO + hi, :] = jnp.where(dens_ref[HALO + lo : HALO + hi, :] > 0.0, a, 1.0)
            both = [tile(groups + 2 * p + h, old[2 * p + h, :, lo:hi]) for h in range(2)]
            e_ref[p, HALO + lo : HALO + hi, :] = jnp.concatenate(both, axis=0).T
            return carry

        lax.fori_loop(0, pairs, one, 0, unroll=8)
    _, lo_first, lo_second = partner("polar", cols, HALO)
    for out, lo in ((to_first, lo_first), (to_second, lo_second)):
        edge = pl.ds(pl.multiple_of(lo, HALO), HALO)
        for p in range(pairs):
            out[p] = a_ref[p, edge, :]
            out[pairs + p] = e_ref[p, edge, :]
        out[2 * pairs] = dens_ref[edge, :]
        out[2 * pairs + 1] = mat_ref[edge, :]


def next_row(v):
    return pltpu.roll(v, LANES - 1, 1)


def prev_row(v):
    return pltpu.roll(v, 1, 1)


def after(ref, lead, lo, hi, here, end):
    if hi < end:
        return ref[(*lead, slice(lo + 1, hi + 1), slice(None))]
    return pltpu.roll(here, hi - lo - 1, 0)


def before(ref, lead, lo, hi, here, begin):
    if lo > begin:
        return ref[(*lead, slice(lo - 1, hi - 1), slice(None))]
    return pltpu.roll(here, 1, 0)


def at(lo, hi):
    return (slice(lo, hi), slice(None))


def flux_sum(p, lo, hi, v_ref, v, fr_ref, fp_ref, span):
    begin, end = span
    fp = fp_ref[(p, *at(lo, hi))]
    fp_before = before(fp_ref, (p,), lo, hi, fp, begin)
    polar = fp * (v - after(v_ref, (p,), lo, hi, v, end)) + fp_before * (
        v - before(v_ref, (p,), lo, hi, v, begin)
    )
    fr = fr_ref[(p, *at(lo, hi))] * (v - next_row(v))
    return polar + (fr - prev_row(fr))


def tile_sum(v):
    acc = v[:HALO]
    for lo in range(HALO, v.shape[0], HALO):
        acc = acc + v[lo : lo + HALO]
    return acc


def krylov(p, pairs, parts, span, own, a_ref, fr_ref, fp_ref, r_ref, q_ref, t_ref, mom, old_mom=None):
    sums = [jnp.zeros((HALO, LANES), jnp.float32) for _ in range(4)]
    for lo, hi in parts:
        r = r_ref[(p, *at(lo, hi))]
        q = r + a_ref[(p, *at(lo, hi))] * r + flux_sum(p, lo, hi, r_ref, r, fr_ref, fp_ref, span)
        q_ref[(p, *at(lo, hi))] = q
        if lo >= own[0] and hi <= own[1]:
            sums[0] = sums[0] + tile_sum(r * r)
            sums[1] = sums[1] + tile_sum(r * q)
            sums[2] = sums[2] + tile_sum(q * q)
    for lo, hi in parts:
        inside = lo >= own[0] and hi <= own[1]
        if not inside and t_ref is None:
            continue
        q = q_ref[(p, *at(lo, hi))]
        t = q + a_ref[(p, *at(lo, hi))] * q + flux_sum(p, lo, hi, q_ref, q, fr_ref, fp_ref, span)
        if t_ref is not None:
            t_ref[(p, *at(lo, hi))] = t
        if inside:
            sums[3] = sums[3] + tile_sum(q * t)
    for k in range(4):
        total = jnp.sum(sums[k], axis=0, keepdims=True)
        if old_mom is not None:
            total = total + old_mom[pl.ds(k * pairs + p, 1), :]
        mom[pl.ds(k * pairs + p, 1), :] = total


def send_moments(pairs, rows, mom, out, row_sums):
    lane = lane_of(4 * pairs)
    x = mom[...]
    first = jnp.where((lane >= HALO) & (lane < HALO + rows), x, 0.0)
    second = jnp.where((lane >= HALF + HALO) & (lane < HALF + HALO + rows), x, 0.0)
    both = jnp.concatenate([first, second, jnp.zeros((LANES - 8 * pairs, LANES), jnp.float32)], axis=0)
    line = lax.dot_general(
        jnp.ones((HALO, LANES), jnp.float32), both, (((1,), (1,)), ((), ())),
        precision=HIGHEST, preferred_element_type=jnp.float32,
    )
    if row_sums is not None:
        line = jnp.where(lane_of(HALO) < HALF, line, row_sums)
    for lo in range(0, out.shape[0], HALO):
        out[lo : lo + HALO, :] = line


def weight_of(weights, p):
    return jnp.where(lane_of(HALO) < HALF, weights[2 * p], weights[2 * p + 1])[:1]


def fold(s):
    s = s + pltpu.roll(s, HALF, 1)
    middle = s.shape[0] // 2
    return jnp.where(lane_of(middle) < HALF, s[:middle], s[middle:])


def unfold(s):
    other = pltpu.roll(s, HALF, 1)
    low = lane_of(s.shape[0]) < HALF
    return jnp.where(low, s, other), jnp.where(low, other, s)


def first_residual(p, w, inverse_parts, parts, span, dens_ref, mat_ref, a_ref, e_ref, fr_ref, fp_ref, r_ref, inv):
    begin, end = span
    for lo, hi in inverse_parts:
        a, e = a_ref[(p, *at(lo, hi))], e_ref[(p, *at(lo, hi))]
        slope_r = 0.5 * (next_row(e) - prev_row(e))
        slope_p = 0.5 * (after(e_ref, (p,), lo, hi, e, end) - before(e_ref, (p,), lo, hi, e, begin))
        n2 = slope_r * slope_r + slope_p * slope_p
        u = a * e
        s = 2.0 * u + jnp.sqrt(n2)
        inv[lo:hi, :] = jnp.where(dens_ref[lo:hi, :] > 0.0, (n2 + 3.0 * u * s) / (e * s), OUTSIDE)
    for lo, hi in parts:
        d = inv[lo:hi, :]
        fr_ref[(p, *at(lo, hi))] = 2.0 / (d + next_row(d))
        fp_ref[(p, *at(lo, hi))] = 2.0 / (d + after(inv, (), lo, hi, d, end))
    for lo, hi in parts:
        a, e = a_ref[(p, *at(lo, hi))], e_ref[(p, *at(lo, hi))]
        r_ref[(p, *at(lo, hi))] = a * (w * mat_ref[lo:hi, :] - e) - flux_sum(
            p, lo, hi, e_ref, e, fr_ref, fp_ref, span
        )


def inner_kernel(groups, cols, half, weights, a_ref, e_ref, dens_ref, mat_ref, *rest):
    pairs = groups // 2
    if half == 0:
        edge, fr_ref, fp_ref, r_ref, q_ref, t_ref, emit, mom, edge_out, inv = rest
        edge_out[...] = edge[...]
        emit[...] = jnp.zeros(emit.shape, jnp.float32)
    else:
        fr_ref, fp_ref, r_ref, q_ref, t_ref, emit, mom, inv = rest[7:]
    bounds = (0, pairs // 2) if half == 0 else (pairs // 2, pairs)
    span = (HALO, HALO + cols)
    parts = [(lo + HALO, hi + HALO) for lo, hi in pieces(cols)]
    own = (2 * HALO, cols)

    def one(p, carry):
        w = weight_of(weights, p)
        for lo, hi in parts:
            emit[lo:hi, :] += a_ref[(p, *at(lo, hi))] * w
        first_residual(p, w, parts, parts, span, dens_ref, mat_ref, a_ref, e_ref, fr_ref, fp_ref, r_ref, inv)
        krylov(p, pairs, parts, span, own, a_ref, fr_ref, fp_ref, r_ref, q_ref, t_ref, mom)
        return carry

    lax.fori_loop(*bounds, one, 0, unroll=2)


def frame_kernel(groups, rows, cols, weights, got_first, got_second, emit, old_mom, *rest):
    a_ref, e_ref, fr_ref, fp_ref, r_ref, q_ref, t_ref, dens_ref, mat_ref, emit_out, out, inv, mom = rest[9:]
    pairs = groups // 2
    tall = cols + 2 * HALO
    span = (0, tall)
    even, _, _ = partner("polar", 0, 0)
    ends = ((0, HALO), (tall - HALO, tall))

    def halo(side, plane):
        one, two = got_first[plane], got_second[plane]
        return jnp.where(even, two, one) if side == 0 else jnp.where(even, one, two)

    for side, (lo, hi) in enumerate(ends):
        dens_ref[lo:hi, :] = halo(side, 2 * pairs)
        mat_ref[lo:hi, :] = halo(side, 2 * pairs + 1)
    parts = [(0, HALO), (HALO, 2 * HALO), (cols, cols + HALO), (cols + HALO, tall)]
    inverse_parts = parts[:2] + [(2 * HALO, 3 * HALO)] + parts[2:]

    def one(p, emitted):
        w = weight_of(weights, p)
        sums = []
        for side, (lo, hi) in enumerate(ends):
            a = jnp.where(dens_ref[lo:hi, :] > 0.0, halo(side, p), 1.0)
            a_ref[(p, *at(lo, hi))] = a
            e_ref[(p, *at(lo, hi))] = halo(side, pairs + p)
            sums.append(emitted[side] + a * w)
        first_residual(
            p, w, inverse_parts, parts, span, dens_ref, mat_ref, a_ref, e_ref, fr_ref, fp_ref, r_ref, inv
        )
        krylov(
            p, pairs, parts, span, (HALO, HALO + cols), a_ref, fr_ref, fp_ref, r_ref, q_ref, t_ref, mom, old_mom
        )
        return tuple(sums)

    zero = jnp.zeros((HALO, LANES), jnp.float32)
    low, high = lax.fori_loop(0, pairs, one, (zero, zero), unroll=8)
    emit_out[...] = fold(jnp.concatenate([low, emit[HALO : HALO + cols, :], high], axis=0))
    row_sums = jnp.sum(tile_sum(dens_ref[HALO : HALO + cols, :]), axis=0, keepdims=True)
    send_moments(pairs, rows, mom, out, row_sums)


def steps(pairs, gathered):
    total = jnp.sum(gathered[...], axis=0, keepdims=True)
    lane = lane_of(pairs)
    sub = lax.broadcasted_iota(jnp.int32, (pairs, LANES), 0)

    def moment(k):
        first, second = (
            jnp.sum(jnp.where(lane == sub + (4 * h + k) * pairs, total, 0.0), axis=1, keepdims=True)
            for h in range(2)
        )
        return jnp.where(lane < HALF, first, second)

    m0, m1, m2, m3 = (moment(k) for k in range(4))
    k1, k2, k3 = m1 / m0, m2 / m0, m3 / m0
    first = 1.0 / k1
    det = jnp.maximum(k2 - k1 * k1, 0.0)
    beta = det / (k1 * k1)
    low = k1 * k3 - k2 * k2
    second = jnp.minimum(jnp.where(low > 0.0, k1 * det / low, 0.0), 1.0)
    return first + second * (1.0 + beta), first * second


def absorbed(pairs, c1, c2, a_ref, e_ref, r_ref, q_ref, e_out, s):
    tall = a_ref.shape[1]
    for lo, hi in pieces(tall):
        total = jnp.zeros((hi - lo, LANES), jnp.float32)
        for p in range(pairs):
            e = (
                e_ref[(p, *at(lo, hi))]
                + c1[p : p + 1, :] * r_ref[(p, *at(lo, hi))]
                - c2[p : p + 1, :] * q_ref[(p, *at(lo, hi))]
            )
            e_out[(p, *at(lo, hi))] = e
            total = total + a_ref[(p, *at(lo, hi))] * e
        s[lo:hi, :] = total


def update_kernel(pairs, gathered, a_ref, e_ref, r_ref, q_ref, *rest):
    if len(rest) == 6:
        emit, *rest = rest
    else:
        emit = None
    e_out, s_out, c1_ref, c2_ref, s = rest
    c1, c2 = steps(pairs, gathered)
    c1_ref[...] = c1
    c2_ref[...] = c2
    absorbed(pairs, c1, c2, a_ref, e_ref, r_ref, q_ref, e_out, s)
    s_out[0] = fold(s[...])
    if emit is not None:
        s_out[1] = emit[...]


def last_update_kernel(pairs, cols, gathered, a_ref, e_ref, r_ref, q_ref, e_out, s_out, s):
    c1, c2 = steps(pairs, gathered)
    absorbed(pairs, c1, c2, a_ref, e_ref, r_ref, q_ref, e_out, s)
    s_out[...] = fold(s[HALO : HALO + cols, :])


def energy_kernel(pairs, rows, cols, e_ref, out):
    def one(p, carry):
        for lo in range(0, cols, LANES):
            block = e_ref[p, HALO + lo : HALO + lo + LANES, :].T
            out[2 * p, :, lo : lo + LANES] = block[HALO : HALO + rows]
            out[2 * p + 1, :, lo : lo + LANES] = block[HALF + HALO : HALF + HALO + rows]
        return carry

    lax.fori_loop(0, pairs, one, 0, unroll=4)


def turned_back(v, rows):
    parts = [v[lo : lo + LANES].T[HALO : HALO + rows] for lo in range(0, v.shape[0], LANES)]
    return jnp.concatenate(parts, axis=1)


def heating_kernel(
    groups, rows, cols, polar_count, flux, gathered, dens_ref, mat_ref, flux_ref, column_out, fixed_out
):
    tall = dens_ref.shape[0]
    radius, polar = lax.axis_index("radius"), lax.axis_index("polar")
    dens = dens_ref[...]
    row_id = lax.broadcasted_iota(jnp.int32, gathered.shape, 0)
    ahead = (row_id >= radius * polar_count) & (row_id < radius * polar_count + polar)
    carried = jnp.sum(jnp.where(ahead, gathered[...], 0.0), axis=0, keepdims=True)
    lane = lane_of()
    carried = jnp.where(lane < HALF, pltpu.roll(carried, HALF, 1), carried)
    dst = lax.broadcasted_iota(jnp.int32, (tall, tall), 0)
    src = lax.broadcasted_iota(jnp.int32, (tall, tall), 1)
    coeff = jnp.where(
        (src >= HALO) & (src <= dst), 1.0, jnp.where((src < HALO) & (src > dst), -1.0, 0.0)
    )
    within = lax.dot_general(
        coeff, dens, (((1,), (0,)), ((), ())), precision=HIGHEST, preferred_element_type=jnp.float32
    )
    column = 2.0 / (cols * polar_count) * (carried + within)
    vec = flux_ref[0:1, :]
    for i in range(rows):
        vec = jnp.where(lane % HALF == HALO + i, flux[i], vec)
    fixed_out[...] = 16.0 * dens * mat_ref[...] + vec * dens * jnp.exp(-column)
    column_out[...] = turned_back(column[HALO : HALO + cols], rows)


def summed(refs, lead=()):
    total = refs[0][(*lead, ...)]
    for s in refs[1:]:
        total = total + s[(*lead, ...)]
    return total


def next_kernel(groups, rows, count, turn, last, weights, c1_ref, c2_ref, a_ref, fr_ref, fp_ref, r_in, q_in, t_in, fixed, cap_in, mat_ref, *rest):
    pairs = groups // 2
    sums = rest[:count]
    rest = rest[count:]
    outs, (delta, mom) = rest[:-2], rest[-2:]
    r_ref, q_ref, out, *outs = outs
    t_ref = None if last else outs.pop(0)
    m_ref = None if last else outs.pop(0)
    tall = fixed.shape[0]
    parts = pieces(tall)
    half = tall // 2
    folded = summed(sums, (0,))
    if turn == 0:
        cap_out = outs.pop(0)
        dens = cap_in[...]
        emits = jnp.concatenate(unfold(summed(sums, (1,))), axis=0)
        cap_out[...] = 16.0 * jnp.where(dens > 0.0, dens, 1.0) + emits
        cap_in = cap_out
    for k, total in enumerate(unfold(folded)):
        here = at(k * half, (k + 1) * half)
        nxt = (fixed[here] + total) / cap_in[here]
        delta[here] = nxt - mat_ref[here]
        if m_ref is not None:
            m_ref[here] = nxt

    def one(p, carry):
        w = weight_of(weights, p)
        c1 = c1_ref[pl.ds(p, 1), :]
        c2 = c2_ref[pl.ds(p, 1), :]
        for lo, hi in parts:
            here = (p, *at(lo, hi))
            r_ref[here] = (
                r_in[here] - c1 * q_in[here] + c2 * t_in[here] + a_ref[here] * (w * delta[lo:hi, :])
            )
        krylov(p, pairs, parts, (0, tall), (HALO, tall - HALO), a_ref, fr_ref, fp_ref, r_ref, q_ref, t_ref, mom)
        return carry

    lax.fori_loop(0, pairs, one, 0, unroll=2)
    send_moments(pairs, rows, mom, out, None)


def material_kernel(count, rows, cols, fixed, capacity, *rest):
    sums, out = rest[:count], rest[count]
    total = jnp.concatenate(unfold(summed(sums)), axis=0)
    here = at(HALO, HALO + cols)
    out[...] = turned_back((fixed[here] + total) / capacity[here], rows)


def spread(part, axis):
    count = lax.axis_size(axis)
    return [part] + [lax.ppermute(part, axis, [(i, i ^ s) for i in range(count)]) for s in range(1, count)]


def pair_up(first, axis):
    return lax.ppermute(first, axis, [(i, i ^ 1) for i in range(lax.axis_size(axis))])


def pair_across(second, axis):
    links = [(i, i + 1) for i in range(1, lax.axis_size(axis) - 1, 2)]
    return lax.ppermute(second, axis, links + [(j, i) for i, j in links])


def per_device(density, opacity, radiation_old, material_old, weights, stellar_flux):
    groups, rows, cols = opacity.shape
    pairs, tall = groups // 2, cols + 2 * HALO
    assert rows + 2 * HALO == HALF
    polar_count = lax.axis_size("polar")
    count = lax.axis_size("group")
    devices = lax.axis_size("radius") * polar_count
    planes = 2 * groups + 3
    big, flat, core = (pairs, tall, LANES), (tall, LANES), (cols, LANES)
    line = (devices, LANES)
    edge = (2 * pairs + 2, HALO, LANES)
    vmem = lambda shape: pltpu.VMEM(shape, jnp.float32)

    strips = [
        pltpu.VMEM((groups, 2 * HALO, cols), jnp.bfloat16),
        vmem((groups, HALO, cols)),
        vmem((HALO, cols)),
        vmem((HALO, cols)),
    ]
    first, second = call(
        functools.partial(pack_rows_kernel, groups, rows),
        [(planes, HALO, cols)] * 2,
        tuple(
            pltpu.with_memory_space_constraint(v, pltpu.HBM)
            for v in (stellar_flux, opacity, radiation_old, density, material_old)
        ),
        [hspec()] * 5,
        scratch=strips * 2 + [pltpu.SMEM((rows,), jnp.float32), pltpu.SemaphoreType.DMA((9,))],
        name="pack_rows",
        limit=20 * 1024 * 1024,
    )
    first, second = pair_up(first, "radius"), pair_across(second, "radius")
    a, e, dens, mat, flux_lanes, first, second = call(
        functools.partial(turn_kernel, groups, rows, cols),
        [big] * 2 + [flat, flat, (HALO, LANES), edge, edge],
        (opacity, radiation_old, density, material_old, first, second),
        [vspec()] * 6,
        name="turn",
    )
    first = pair_up(first, "polar")
    *state, second = call(
        functools.partial(inner_kernel, groups, cols, 0),
        [big] * 5 + [flat, (4 * pairs, LANES), edge],
        (weights, a, e, dens, mat, second),
        [sspec()] + [vspec()] * 5,
        scratch=[vmem(flat)],
        name="inner_first",
    )
    second = pair_across(second, "polar")
    fr, fp, r, q, t, emit, mom = call(
        functools.partial(inner_kernel, groups, cols, 1),
        [big] * 5 + [flat, (4 * pairs, LANES)],
        (weights, a, e, dens, mat, *state),
        [sspec()] + [vspec()] * 11,
        scratch=[vmem(flat)],
        name="inner_second",
        aliases={5 + k: k for k in range(7)},
    )
    a, e, fr, fp, r, q, t, dens, mat, emit, out = call(
        functools.partial(frame_kernel, groups, rows, cols),
        [big] * 7 + [flat, flat, (tall // 2, LANES), line],
        (weights, first, second, emit, mom, a, e, fr, fp, r, q, t, dens, mat),
        [sspec()] + [vspec()] * 13,
        scratch=[vmem(flat), vmem((4 * pairs, LANES))],
        name="frame",
        aliases={5 + k: k for k in range(9)},
    )
    capacity = dens
    for turn in range(ITERS):
        gathered = lax.all_to_all(out, ("radius", "polar"), 0, 0, tiled=True)
        if turn + 1 == ITERS:
            e, part = call(
                functools.partial(last_update_kernel, pairs, cols),
                [big, (cols // 2, LANES)],
                (gathered, a, e, r, q),
                [vspec()] * 5,
                scratch=[vmem(flat)],
                name="last_update",
            )
            sums = spread(part, "group")
            (energy,) = call(
                functools.partial(energy_kernel, pairs, rows, cols),
                [(groups, rows, cols)],
                (e,),
                [vspec()],
                name="energy",
            )
            (mat,) = call(
                functools.partial(material_kernel, count, rows, cols),
                [(rows, cols)],
                (fixed, capacity, *sums),
                [vspec()] * (2 + count),
                name="material",
            )
            break
        first, last = turn == 0, turn + 2 == ITERS
        extra = [emit] if first else []
        e, part, c1, c2 = call(
            functools.partial(update_kernel, pairs),
            [big, (1 + len(extra), tall // 2, LANES), (pairs, LANES), (pairs, LANES)],
            (gathered, a, e, r, q, *extra),
            [vspec()] * (5 + len(extra)),
            scratch=[vmem(flat)],
            name="update",
        )
        sums = spread(part, "group")
        if first:
            column, fixed = call(
                functools.partial(heating_kernel, groups, rows, cols, polar_count),
                [(rows, cols), flat],
                (stellar_flux, gathered, dens, mat, flux_lanes),
                [sspec()] + [vspec()] * 4,
                name="heating",
            )
        r, q, out, *more = call(
            functools.partial(next_kernel, groups, rows, count, turn, last),
            [big, big, line] + ([] if last else [big, flat]) + ([flat] if first else []),
            (weights, c1, c2, a, fr, fp, r, q, t, fixed, capacity, mat, *sums),
            [sspec()] + [vspec()] * (11 + count),
            scratch=[vmem(flat), vmem((4 * pairs, LANES))],
            name="next",
        )
        if not last:
            t, mat, *more = more
        if first:
            (capacity,) = more
    return (energy, mat, column)


def solution(mesh):
    return jax.shard_map(
        per_device,
        mesh=mesh,
        in_specs=(
            P("radius", "polar"),
            P("group", "radius", "polar"),
            P("group", "radius", "polar"),
            P("radius", "polar"),
            P("group"),
            P("radius"),
        ),
        out_specs=(P("group", "radius", "polar"), P("radius", "polar"), P("radius", "polar")),
        check_vma=False,
    )
```

```python
import functools
import jax
import jax.numpy as jnp
from jax import lax
from jax.experimental import pallas as pl
from jax.experimental.pallas import tpu as pltpu
from jax.sharding import PartitionSpec as P


ITERS = 3
HALO = 8
LANES = 128
HALF = LANES // 2
STEP = 64
VMEM_LIMIT = 12 * 1024 * 1024
HIGHEST = lax.Precision.HIGHEST
OUTSIDE = 1.6e38


def vspec():
    return pl.BlockSpec(memory_space=pltpu.VMEM)


def sspec():
    return pl.BlockSpec(memory_space=pltpu.SMEM)


def hspec():
    return pl.BlockSpec(memory_space=pltpu.HBM)


def call(kernel, outs, args, specs, scratch=(), flops=1000000, nbytes=1000000, name=None, limit=VMEM_LIMIT, aliases=None):
    return pl.pallas_call(
        kernel,
        out_shape=[jax.ShapeDtypeStruct(s, jnp.float32) for s in outs],
        in_specs=specs,
        out_specs=[vspec() for _ in outs],
        scratch_shapes=list(scratch),
        compiler_params=pltpu.CompilerParams(vmem_limit_bytes=limit),
        cost_estimate=pl.CostEstimate(flops=flops, bytes_accessed=nbytes, transcendentals=0),
        name=name,
        input_output_aliases=aliases or {},
    )(*args)


def lane_of(height=1):
    return lax.broadcasted_iota(jnp.int32, (height, LANES), 1)


def pieces(tall):
    cuts = [0, HALO]
    while cuts[-1] + STEP < tall - HALO:
        cuts.append(cuts[-1] + STEP)
    cuts += [tall - HALO, tall]
    return list(zip(cuts[:-1], cuts[1:]))


def partner(axis, inner, outer):
    even = lax.rem(lax.axis_index(axis), 2) == 0
    return even, jnp.where(even, inner, outer), jnp.where(even, outer, inner)


def pack_rows_kernel(groups, rows, flux_in, opacity, old, density, material, first, second, *scratch):
    even, lo_first, lo_second = partner("radius", rows - HALO, 0)
    flux, sems = scratch[-2:]
    sides = ((first, lo_first, even), (second, lo_second, jnp.logical_not(even)))
    copies = [pltpu.make_async_copy(flux_in, flux, sems.at[8])]
    for side, (_, lo, at_end) in enumerate(sides):
        op_buf, old_buf, dens_buf, mat_buf = scratch[4 * side : 4 * side + 4]
        lo = pl.multiple_of(lo, HALO)
        base = pl.multiple_of(jnp.where(at_end, rows - 2 * HALO, 0), 2 * HALO)
        moves = (
            (opacity.at[:, pl.ds(base, 2 * HALO), :], op_buf),
            (old.at[:, pl.ds(lo, HALO), :], old_buf),
            (density.at[pl.ds(lo, HALO), :], dens_buf),
            (material.at[pl.ds(lo, HALO), :], mat_buf),
        )
        for k, (src, dst) in enumerate(moves):
            copies.append(pltpu.make_async_copy(src, dst, sems.at[4 * side + k]))
    for c in copies:
        c.start()
    for c in copies:
        c.wait()
    lane = lane_of(HALO) % HALF
    for side, (out, lo, at_end) in enumerate(sides):
        op_buf, old_buf, dens_buf, mat_buf = scratch[4 * side : 4 * side + 4]
        dens = dens_buf[...]
        for g in range(groups):
            part = op_buf[g].astype(jnp.float32)
            out[g] = jnp.where(at_end, part[HALO:], part[:HALO]) * dens
            out[groups + g] = old_buf[g]
        out[2 * groups] = dens
        out[2 * groups + 1] = mat_buf[...]
        place = jnp.where(at_end, 0, rows + HALO)
        vec = jnp.zeros((HALO, LANES), jnp.float32)
        for i in range(HALO):
            vec = jnp.where(lane == place + i, flux[lo + i], vec)
        for at_lane in range(0, out.shape[2], LANES):
            out[2 * groups + 2, :, at_lane : at_lane + LANES] = vec


def turn_kernel(
    groups, rows, cols, opacity, old, density, material, got_second, got_first,
    a_ref, e_ref, dens_ref, mat_ref, flux_ref, to_first, to_second,
):
    pairs = groups // 2
    plane_of_flux = 2 * groups + 2
    flux_ref[...] = got_first[plane_of_flux, :, :LANES] + got_second[plane_of_flux, :, :LANES]
    even, _, _ = partner("radius", 0, 0)
    for lo in range(0, cols, LANES):
        hi = lo + LANES

        def tile(plane, own):
            one, two = got_first[plane, :, lo:hi], got_second[plane, :, lo:hi]
            return jnp.concatenate([jnp.where(even, two, one), own, jnp.where(even, one, two)], axis=0)

        d = tile(2 * groups, density[:, lo:hi])
        d = jnp.concatenate([d, d], axis=0).T
        m = tile(2 * groups + 1, material[:, lo:hi])
        m = jnp.concatenate([m, m], axis=0).T
        dens_ref[HALO + lo : HALO + hi, :] = d
        mat_ref[HALO + lo : HALO + hi, :] = m

        def one(p, carry):
            both = []
            for h in range(2):
                g = 2 * p + h
                both.append(tile(g, opacity[g, :, lo:hi].astype(jnp.float32) * density[:, lo:hi]))
            a = jnp.concatenate(both, axis=0).T
            a_ref[p, HALO + lo : HALO + hi, :] = jnp.where(dens_ref[HALO + lo : HALO + hi, :] > 0.0, a, 1.0)
            both = [tile(groups + 2 * p + h, old[2 * p + h, :, lo:hi]) for h in range(2)]
            e_ref[p, HALO + lo : HALO + hi, :] = jnp.concatenate(both, axis=0).T
            return carry

        lax.fori_loop(0, pairs, one, 0, unroll=8)
    _, lo_first, lo_second = partner("polar", cols, HALO)
    for out, lo in ((to_first, lo_first), (to_second, lo_second)):
        edge = pl.ds(pl.multiple_of(lo, HALO), HALO)
        for p in range(pairs):
            out[p] = a_ref[p, edge, :]
            out[pairs + p] = e_ref[p, edge, :]
        out[2 * pairs] = dens_ref[edge, :]
        out[2 * pairs + 1] = mat_ref[edge, :]


def next_row(v):
    return pltpu.roll(v, LANES - 1, 1)


def prev_row(v):
    return pltpu.roll(v, 1, 1)


def after(ref, lead, lo, hi, here, end):
    if hi < end:
        return ref[(*lead, slice(lo + 1, hi + 1), slice(None))]
    return pltpu.roll(here, hi - lo - 1, 0)


def before(ref, lead, lo, hi, here, begin):
    if lo > begin:
        return ref[(*lead, slice(lo - 1, hi - 1), slice(None))]
    return pltpu.roll(here, 1, 0)


def at(lo, hi):
    return (slice(lo, hi), slice(None))


def flux_sum(p, lo, hi, v_ref, v, fr_ref, fp_ref, span):
    begin, end = span
    fp = fp_ref[(p, *at(lo, hi))]
    fp_before = before(fp_ref, (p,), lo, hi, fp, begin)
    polar = fp * (v - after(v_ref, (p,), lo, hi, v, end)) + fp_before * (
        v - before(v_ref, (p,), lo, hi, v, begin)
    )
    fr = fr_ref[(p, *at(lo, hi))] * (v - next_row(v))
    return polar + (fr - prev_row(fr))


def tile_sum(v):
    acc = v[:HALO]
    for lo in range(HALO, v.shape[0], HALO):
        acc = acc + v[lo : lo + HALO]
    return acc


def krylov(p, pairs, parts, span, own, a_ref, fr_ref, fp_ref, r_ref, q_ref, t_ref, mom, old_mom=None):
    sums = [jnp.zeros((HALO, LANES), jnp.float32) for _ in range(4)]
    for lo, hi in parts:
        r = r_ref[(p, *at(lo, hi))]
        q = r + a_ref[(p, *at(lo, hi))] * r + flux_sum(p, lo, hi, r_ref, r, fr_ref, fp_ref, span)
        q_ref[(p, *at(lo, hi))] = q
        if lo >= own[0] and hi <= own[1]:
            sums[0] = sums[0] + tile_sum(r * r)
            sums[1] = sums[1] + tile_sum(r * q)
            sums[2] = sums[2] + tile_sum(q * q)
    for lo, hi in parts:
        inside = lo >= own[0] and hi <= own[1]
        if not inside and t_ref is None:
            continue
        q = q_ref[(p, *at(lo, hi))]
        t = q + a_ref[(p, *at(lo, hi))] * q + flux_sum(p, lo, hi, q_ref, q, fr_ref, fp_ref, span)
        if t_ref is not None:
            t_ref[(p, *at(lo, hi))] = t
        if inside:
            sums[3] = sums[3] + tile_sum(q * t)
    for k in range(4):
        total = jnp.sum(sums[k], axis=0, keepdims=True)
        if old_mom is not None:
            total = total + old_mom[pl.ds(k * pairs + p, 1), :]
        mom[pl.ds(k * pairs + p, 1), :] = total


def send_moments(pairs, rows, mom, out, row_sums):
    lane = lane_of(4 * pairs)
    x = mom[...]
    first = jnp.where((lane >= HALO) & (lane < HALO + rows), x, 0.0)
    second = jnp.where((lane >= HALF + HALO) & (lane < HALF + HALO + rows), x, 0.0)
    both = jnp.concatenate([first, second, jnp.zeros((LANES - 8 * pairs, LANES), jnp.float32)], axis=0)
    line = lax.dot_general(
        jnp.ones((HALO, LANES), jnp.float32), both, (((1,), (1,)), ((), ())),
        precision=HIGHEST, preferred_element_type=jnp.float32,
    )
    if row_sums is not None:
        line = jnp.where(lane_of(HALO) < HALF, line, row_sums)
    for lo in range(0, out.shape[0], HALO):
        out[lo : lo + HALO, :] = line


def weight_of(weights, p):
    return jnp.where(lane_of(HALO) < HALF, weights[2 * p], weights[2 * p + 1])[:1]


def fold(s):
    s = s + pltpu.roll(s, HALF, 1)
    middle = s.shape[0] // 2
    return jnp.where(lane_of(middle) < HALF, s[:middle], s[middle:])


def unfold(s):
    other = pltpu.roll(s, HALF, 1)
    low = lane_of(s.shape[0]) < HALF
    return jnp.where(low, s, other), jnp.where(low, other, s)


def first_residual(p, w, inverse_parts, parts, span, dens_ref, mat_ref, a_ref, e_ref, fr_ref, fp_ref, r_ref, inv):
    begin, end = span
    for lo, hi in inverse_parts:
        a, e = a_ref[(p, *at(lo, hi))], e_ref[(p, *at(lo, hi))]
        slope_r = 0.5 * (next_row(e) - prev_row(e))
        slope_p = 0.5 * (after(e_ref, (p,), lo, hi, e, end) - before(e_ref, (p,), lo, hi, e, begin))
        n2 = slope_r * slope_r + slope_p * slope_p
        u = a * e
        s = 2.0 * u + jnp.sqrt(n2)
        inv[lo:hi, :] = jnp.where(dens_ref[lo:hi, :] > 0.0, (n2 + 3.0 * u * s) / (e * s), OUTSIDE)
    for lo, hi in parts:
        d = inv[lo:hi, :]
        fr_ref[(p, *at(lo, hi))] = 2.0 / (d + next_row(d))
        fp_ref[(p, *at(lo, hi))] = 2.0 / (d + after(inv, (), lo, hi, d, end))
    for lo, hi in parts:
        a, e = a_ref[(p, *at(lo, hi))], e_ref[(p, *at(lo, hi))]
        r_ref[(p, *at(lo, hi))] = a * (w * mat_ref[lo:hi, :] - e) - flux_sum(
            p, lo, hi, e_ref, e, fr_ref, fp_ref, span
        )


def inner_kernel(groups, cols, half, weights, a_ref, e_ref, dens_ref, mat_ref, *rest):
    pairs = groups // 2
    if half == 0:
        edge, fr_ref, fp_ref, r_ref, q_ref, t_ref, emit, mom, edge_out, inv = rest
        edge_out[...] = edge[...]
        emit[...] = jnp.zeros(emit.shape, jnp.float32)
    else:
        fr_ref, fp_ref, r_ref, q_ref, t_ref, emit, mom, inv = rest[7:]
    bounds = (0, pairs // 4) if half == 0 else (pairs // 4, pairs)
    span = (HALO, HALO + cols)
    parts = [(lo + HALO, hi + HALO) for lo, hi in pieces(cols)]
    own = (2 * HALO, cols)

    def one(p, carry):
        w = weight_of(weights, p)
        for lo, hi in parts:
            emit[lo:hi, :] += a_ref[(p, *at(lo, hi))] * w
        first_residual(p, w, parts, parts, span, dens_ref, mat_ref, a_ref, e_ref, fr_ref, fp_ref, r_ref, inv)
        krylov(p, pairs, parts, span, own, a_ref, fr_ref, fp_ref, r_ref, q_ref, t_ref, mom)
        return carry

    lax.fori_loop(*bounds, one, 0, unroll=2)


def frame_kernel(groups, rows, cols, weights, got_first, got_second, emit, old_mom, *rest):
    a_ref, e_ref, fr_ref, fp_ref, r_ref, q_ref, t_ref, dens_ref, mat_ref, emit_out, out, inv, mom = rest[9:]
    pairs = groups // 2
    tall = cols + 2 * HALO
    span = (0, tall)
    even, _, _ = partner("polar", 0, 0)
    ends = ((0, HALO), (tall - HALO, tall))

    def halo(side, plane):
        one, two = got_first[plane], got_second[plane]
        return jnp.where(even, two, one) if side == 0 else jnp.where(even, one, two)

    for side, (lo, hi) in enumerate(ends):
        dens_ref[lo:hi, :] = halo(side, 2 * pairs)
        mat_ref[lo:hi, :] = halo(side, 2 * pairs + 1)
    parts = [(0, HALO), (HALO, 2 * HALO), (cols, cols + HALO), (cols + HALO, tall)]
    inverse_parts = parts[:2] + [(2 * HALO, 3 * HALO)] + parts[2:]

    def one(p, emitted):
        w = weight_of(weights, p)
        sums = []
        for side, (lo, hi) in enumerate(ends):
            a = jnp.where(dens_ref[lo:hi, :] > 0.0, halo(side, p), 1.0)
            a_ref[(p, *at(lo, hi))] = a
            e_ref[(p, *at(lo, hi))] = halo(side, pairs + p)
            sums.append(emitted[side] + a * w)
        first_residual(
            p, w, inverse_parts, parts, span, dens_ref, mat_ref, a_ref, e_ref, fr_ref, fp_ref, r_ref, inv
        )
        krylov(
            p, pairs, parts, span, (HALO, HALO + cols), a_ref, fr_ref, fp_ref, r_ref, q_ref, t_ref, mom, old_mom
        )
        return tuple(sums)

    zero = jnp.zeros((HALO, LANES), jnp.float32)
    low, high = lax.fori_loop(0, pairs, one, (zero, zero), unroll=8)
    emit_out[...] = fold(jnp.concatenate([low, emit[HALO : HALO + cols, :], high], axis=0))
    row_sums = jnp.sum(tile_sum(dens_ref[HALO : HALO + cols, :]), axis=0, keepdims=True)
    send_moments(pairs, rows, mom, out, row_sums)


def steps(pairs, gathered):
    total = jnp.sum(gathered[...], axis=0, keepdims=True)
    lane = lane_of(pairs)
    sub = lax.broadcasted_iota(jnp.int32, (pairs, LANES), 0)

    def moment(k):
        first, second = (
            jnp.sum(jnp.where(lane == sub + (4 * h + k) * pairs, total, 0.0), axis=1, keepdims=True)
            for h in range(2)
        )
        return jnp.where(lane < HALF, first, second)

    m0, m1, m2, m3 = (moment(k) for k in range(4))
    k1, k2, k3 = m1 / m0, m2 / m0, m3 / m0
    first = 1.0 / k1
    det = jnp.maximum(k2 - k1 * k1, 0.0)
    beta = det / (k1 * k1)
    low = k1 * k3 - k2 * k2
    second = jnp.minimum(jnp.where(low > 0.0, k1 * det / low, 0.0), 1.0)
    return first + second * (1.0 + beta), first * second


def absorbed(pairs, c1, c2, a_ref, e_ref, r_ref, q_ref, e_out, s):
    tall = a_ref.shape[1]
    for lo, hi in pieces(tall):
        total = jnp.zeros((hi - lo, LANES), jnp.float32)
        for p in range(pairs):
            e = (
                e_ref[(p, *at(lo, hi))]
                + c1[p : p + 1, :] * r_ref[(p, *at(lo, hi))]
                - c2[p : p + 1, :] * q_ref[(p, *at(lo, hi))]
            )
            e_out[(p, *at(lo, hi))] = e
            total = total + a_ref[(p, *at(lo, hi))] * e
        s[lo:hi, :] = total


def update_kernel(pairs, gathered, a_ref, e_ref, r_ref, q_ref, *rest):
    if len(rest) == 6:
        emit, *rest = rest
    else:
        emit = None
    e_out, s_out, c1_ref, c2_ref, s = rest
    c1, c2 = steps(pairs, gathered)
    c1_ref[...] = c1
    c2_ref[...] = c2
    absorbed(pairs, c1, c2, a_ref, e_ref, r_ref, q_ref, e_out, s)
    s_out[0] = fold(s[...])
    if emit is not None:
        s_out[1] = emit[...]


def last_update_kernel(pairs, cols, gathered, a_ref, e_ref, r_ref, q_ref, e_out, s_out, s):
    c1, c2 = steps(pairs, gathered)
    absorbed(pairs, c1, c2, a_ref, e_ref, r_ref, q_ref, e_out, s)
    s_out[...] = fold(s[HALO : HALO + cols, :])


def energy_kernel(pairs, rows, cols, e_ref, out):
    def one(p, carry):
        for lo in range(0, cols, LANES):
            block = e_ref[p, HALO + lo : HALO + lo + LANES, :].T
            out[2 * p, :, lo : lo + LANES] = block[HALO : HALO + rows]
            out[2 * p + 1, :, lo : lo + LANES] = block[HALF + HALO : HALF + HALO + rows]
        return carry

    lax.fori_loop(0, pairs, one, 0, unroll=4)


def turned_back(v, rows):
    parts = [v[lo : lo + LANES].T[HALO : HALO + rows] for lo in range(0, v.shape[0], LANES)]
    return jnp.concatenate(parts, axis=1)


def heating_kernel(
    groups, rows, cols, polar_count, flux, gathered, dens_ref, mat_ref, flux_ref, column_out, fixed_out
):
    tall = dens_ref.shape[0]
    radius, polar = lax.axis_index("radius"), lax.axis_index("polar")
    dens = dens_ref[...]
    row_id = lax.broadcasted_iota(jnp.int32, gathered.shape, 0)
    ahead = (row_id >= radius * polar_count) & (row_id < radius * polar_count + polar)
    carried = jnp.sum(jnp.where(ahead, gathered[...], 0.0), axis=0, keepdims=True)
    lane = lane_of()
    carried = jnp.where(lane < HALF, pltpu.roll(carried, HALF, 1), carried)
    dst = lax.broadcasted_iota(jnp.int32, (tall, tall), 0)
    src = lax.broadcasted_iota(jnp.int32, (tall, tall), 1)
    coeff = jnp.where(
        (src >= HALO) & (src <= dst), 1.0, jnp.where((src < HALO) & (src > dst), -1.0, 0.0)
    )
    within = lax.dot_general(
        coeff, dens, (((1,), (0,)), ((), ())), precision=HIGHEST, preferred_element_type=jnp.float32
    )
    column = 2.0 / (cols * polar_count) * (carried + within)
    vec = flux_ref[0:1, :]
    for i in range(rows):
        vec = jnp.where(lane % HALF == HALO + i, flux[i], vec)
    fixed_out[...] = 16.0 * dens * mat_ref[...] + vec * dens * jnp.exp(-column)
    column_out[...] = turned_back(column[HALO : HALO + cols], rows)


def summed(refs, lead=()):
    total = refs[0][(*lead, ...)]
    for s in refs[1:]:
        total = total + s[(*lead, ...)]
    return total


def next_kernel(groups, rows, count, turn, last, weights, c1_ref, c2_ref, a_ref, fr_ref, fp_ref, r_in, q_in, t_in, fixed, cap_in, mat_ref, *rest):
    pairs = groups // 2
    sums = rest[:count]
    rest = rest[count:]
    outs, (delta, mom) = rest[:-2], rest[-2:]
    r_ref, q_ref, out, *outs = outs
    t_ref = None if last else outs.pop(0)
    m_ref = None if last else outs.pop(0)
    tall = fixed.shape[0]
    parts = pieces(tall)
    half = tall // 2
    folded = summed(sums, (0,))
    if turn == 0:
        cap_out = outs.pop(0)
        dens = cap_in[...]
        emits = jnp.concatenate(unfold(summed(sums, (1,))), axis=0)
        cap_out[...] = 16.0 * jnp.where(dens > 0.0, dens, 1.0) + emits
        cap_in = cap_out
    for k, total in enumerate(unfold(folded)):
        here = at(k * half, (k + 1) * half)
        nxt = (fixed[here] + total) / cap_in[here]
        delta[here] = nxt - mat_ref[here]
        if m_ref is not None:
            m_ref[here] = nxt

    def one(p, carry):
        w = weight_of(weights, p)
        c1 = c1_ref[pl.ds(p, 1), :]
        c2 = c2_ref[pl.ds(p, 1), :]
        for lo, hi in parts:
            here = (p, *at(lo, hi))
            r_ref[here] = (
                r_in[here] - c1 * q_in[here] + c2 * t_in[here] + a_ref[here] * (w * delta[lo:hi, :])
            )
        krylov(p, pairs, parts, (0, tall), (HALO, tall - HALO), a_ref, fr_ref, fp_ref, r_ref, q_ref, t_ref, mom)
        return carry

    lax.fori_loop(0, pairs, one, 0, unroll=2)
    send_moments(pairs, rows, mom, out, None)


def material_kernel(count, rows, cols, fixed, capacity, *rest):
    sums, out = rest[:count], rest[count]
    total = jnp.concatenate(unfold(summed(sums)), axis=0)
    here = at(HALO, HALO + cols)
    out[...] = turned_back((fixed[here] + total) / capacity[here], rows)


def spread(part, axis):
    count = lax.axis_size(axis)
    return [part] + [lax.ppermute(part, axis, [(i, i ^ s) for i in range(count)]) for s in range(1, count)]


def pair_up(first, axis):
    return lax.ppermute(first, axis, [(i, i ^ 1) for i in range(lax.axis_size(axis))])


def pair_across(second, axis):
    links = [(i, i + 1) for i in range(1, lax.axis_size(axis) - 1, 2)]
    return lax.ppermute(second, axis, links + [(j, i) for i, j in links])


def per_device(density, opacity, radiation_old, material_old, weights, stellar_flux):
    groups, rows, cols = opacity.shape
    pairs, tall = groups // 2, cols + 2 * HALO
    assert rows + 2 * HALO == HALF
    polar_count = lax.axis_size("polar")
    count = lax.axis_size("group")
    devices = lax.axis_size("radius") * polar_count
    planes = 2 * groups + 3
    big, flat, core = (pairs, tall, LANES), (tall, LANES), (cols, LANES)
    line = (devices, LANES)
    edge = (2 * pairs + 2, HALO, LANES)
    vmem = lambda shape: pltpu.VMEM(shape, jnp.float32)

    strips = [
        pltpu.VMEM((groups, 2 * HALO, cols), jnp.bfloat16),
        vmem((groups, HALO, cols)),
        vmem((HALO, cols)),
        vmem((HALO, cols)),
    ]
    first, second = call(
        functools.partial(pack_rows_kernel, groups, rows),
        [(planes, HALO, cols)] * 2,
        tuple(
            pltpu.with_memory_space_constraint(v, pltpu.HBM)
            for v in (stellar_flux, opacity, radiation_old, density, material_old)
        ),
        [hspec()] * 5,
        scratch=strips * 2 + [pltpu.SMEM((rows,), jnp.float32), pltpu.SemaphoreType.DMA((9,))],
        name="pack_rows",
        limit=20 * 1024 * 1024,
    )
    second = pair_across(second, "radius")
    first = pair_up(first, "radius")
    a, e, dens, mat, flux_lanes, first, second = call(
        functools.partial(turn_kernel, groups, rows, cols),
        [big] * 2 + [flat, flat, (HALO, LANES), edge, edge],
        (opacity, radiation_old, density, material_old, second, first),
        [vspec()] * 6,
        name="turn",
    )
    first = pair_up(first, "polar")
    *state, second = call(
        functools.partial(inner_kernel, groups, cols, 0),
        [big] * 5 + [flat, (4 * pairs, LANES), edge],
        (weights, a, e, dens, mat, second),
        [sspec()] + [vspec()] * 5,
        scratch=[vmem(flat)],
        name="inner_first",
    )
    second = pair_across(second, "polar")
    fr, fp, r, q, t, emit, mom = call(
        functools.partial(inner_kernel, groups, cols, 1),
        [big] * 5 + [flat, (4 * pairs, LANES)],
        (weights, a, e, dens, mat, *state),
        [sspec()] + [vspec()] * 11,
        scratch=[vmem(flat)],
        name="inner_second",
        aliases={5 + k: k for k in range(7)},
    )
    a, e, fr, fp, r, q, t, dens, mat, emit, out = call(
        functools.partial(frame_kernel, groups, rows, cols),
        [big] * 7 + [flat, flat, (tall // 2, LANES), line],
        (weights, first, second, emit, mom, a, e, fr, fp, r, q, t, dens, mat),
        [sspec()] + [vspec()] * 13,
        scratch=[vmem(flat), vmem((4 * pairs, LANES))],
        name="frame",
        aliases={5 + k: k for k in range(9)},
    )
    capacity = dens
    for turn in range(ITERS):
        gathered = lax.all_to_all(out, ("radius", "polar"), 0, 0, tiled=True)
        if turn + 1 == ITERS:
            e, part = call(
                functools.partial(last_update_kernel, pairs, cols),
                [big, (cols // 2, LANES)],
                (gathered, a, e, r, q),
                [vspec()] * 5,
                scratch=[vmem(flat)],
                name="last_update",
            )
            sums = spread(part, "group")
            (energy,) = call(
                functools.partial(energy_kernel, pairs, rows, cols),
                [(groups, rows, cols)],
                (e,),
                [vspec()],
                name="energy",
            )
            (mat,) = call(
                functools.partial(material_kernel, count, rows, cols),
                [(rows, cols)],
                (fixed, capacity, *sums),
                [vspec()] * (2 + count),
                name="material",
            )
            break
        first, last = turn == 0, turn + 2 == ITERS
        extra = [emit] if first else []
        e, part, c1, c2 = call(
            functools.partial(update_kernel, pairs),
            [big, (1 + len(extra), tall // 2, LANES), (pairs, LANES), (pairs, LANES)],
            (gathered, a, e, r, q, *extra),
            [vspec()] * (5 + len(extra)),
            scratch=[vmem(flat)],
            name="update",
        )
        sums = spread(part, "group")
        if first:
            column, fixed = call(
                functools.partial(heating_kernel, groups, rows, cols, polar_count),
                [(rows, cols), flat],
                (stellar_flux, gathered, dens, mat, flux_lanes),
                [sspec()] + [vspec()] * 4,
                name="heating",
            )
        r, q, out, *more = call(
            functools.partial(next_kernel, groups, rows, count, turn, last),
            [big, big, line] + ([] if last else [big, flat]) + ([flat] if first else []),
            (weights, c1, c2, a, fr, fp, r, q, t, fixed, capacity, mat, *sums),
            [sspec()] + [vspec()] * (11 + count),
            scratch=[vmem(flat), vmem((4 * pairs, LANES))],
            name="next",
        )
        if not last:
            t, mat, *more = more
        if first:
            (capacity,) = more
    return (energy, mat, column)


def solution(mesh):
    return jax.shard_map(
        per_device,
        mesh=mesh,
        in_specs=(
            P("radius", "polar"),
            P("group", "radius", "polar"),
            P("group", "radius", "polar"),
            P("radius", "polar"),
            P("group"),
            P("radius"),
        ),
        out_specs=(P("group", "radius", "polar"), P("radius", "polar"), P("radius", "polar")),
        check_vma=False,
    )
```

```python
import functools
import jax
import jax.numpy as jnp
from jax import lax
from jax.experimental import pallas as pl
from jax.experimental.pallas import tpu as pltpu
from jax.sharding import PartitionSpec as P


ITERS = 3
HALO = 8
LANES = 128
HALF = LANES // 2
STEP = 64
VMEM_LIMIT = 12 * 1024 * 1024
HIGHEST = lax.Precision.HIGHEST
OUTSIDE = 1.6e38


def vspec():
    return pl.BlockSpec(memory_space=pltpu.VMEM)


def sspec():
    return pl.BlockSpec(memory_space=pltpu.SMEM)


def hspec():
    return pl.BlockSpec(memory_space=pltpu.HBM)


def call(kernel, outs, args, specs, scratch=(), flops=1000000, nbytes=1000000, name=None, limit=VMEM_LIMIT, aliases=None):
    return pl.pallas_call(
        kernel,
        out_shape=[jax.ShapeDtypeStruct(s, jnp.float32) for s in outs],
        in_specs=specs,
        out_specs=[vspec() for _ in outs],
        scratch_shapes=list(scratch),
        compiler_params=pltpu.CompilerParams(vmem_limit_bytes=limit),
        cost_estimate=pl.CostEstimate(flops=flops, bytes_accessed=nbytes, transcendentals=0),
        name=name,
        input_output_aliases=aliases or {},
    )(*args)


def lane_of(height=1):
    return lax.broadcasted_iota(jnp.int32, (height, LANES), 1)


def pieces(tall):
    cuts = [0, HALO]
    while cuts[-1] + STEP < tall - HALO:
        cuts.append(cuts[-1] + STEP)
    cuts += [tall - HALO, tall]
    return list(zip(cuts[:-1], cuts[1:]))


def partner(axis, inner, outer):
    even = lax.rem(lax.axis_index(axis), 2) == 0
    return even, jnp.where(even, inner, outer), jnp.where(even, outer, inner)


def pack_rows_kernel(groups, rows, flux_in, opacity, old, density, material, first, second, *scratch):
    even, lo_first, lo_second = partner("radius", rows - HALO, 0)
    flux, sems = scratch[-2:]
    sides = ((first, lo_first, even), (second, lo_second, jnp.logical_not(even)))
    copies = [pltpu.make_async_copy(flux_in, flux, sems.at[8])]
    for side, (_, lo, at_end) in enumerate(sides):
        op_buf, old_buf, dens_buf, mat_buf = scratch[4 * side : 4 * side + 4]
        lo = pl.multiple_of(lo, HALO)
        base = pl.multiple_of(jnp.where(at_end, rows - 2 * HALO, 0), 2 * HALO)
        moves = (
            (opacity.at[:, pl.ds(base, 2 * HALO), :], op_buf),
            (old.at[:, pl.ds(lo, HALO), :], old_buf),
            (density.at[pl.ds(lo, HALO), :], dens_buf),
            (material.at[pl.ds(lo, HALO), :], mat_buf),
        )
        for k, (src, dst) in enumerate(moves):
            copies.append(pltpu.make_async_copy(src, dst, sems.at[4 * side + k]))
    for c in copies:
        c.start()
    for c in copies:
        c.wait()
    lane = lane_of(HALO) % HALF
    for side, (out, lo, at_end) in enumerate(sides):
        op_buf, old_buf, dens_buf, mat_buf = scratch[4 * side : 4 * side + 4]
        dens = dens_buf[...]
        for g in range(groups):
            part = op_buf[g].astype(jnp.float32)
            out[g] = jnp.where(at_end, part[HALO:], part[:HALO]) * dens
            out[groups + g] = old_buf[g]
        out[2 * groups] = dens
        out[2 * groups + 1] = mat_buf[...]
        place = jnp.where(at_end, 0, rows + HALO)
        vec = jnp.zeros((HALO, LANES), jnp.float32)
        for i in range(HALO):
            vec = jnp.where(lane == place + i, flux[lo + i], vec)
        for at_lane in range(0, out.shape[2], LANES):
            out[2 * groups + 2, :, at_lane : at_lane + LANES] = vec


def turn_kernel(
    groups, rows, cols, opacity, old, density, material, got_second, got_first,
    a_ref, e_ref, dens_ref, mat_ref, flux_ref, to_first, to_second,
):
    pairs = groups // 2
    plane_of_flux = 2 * groups + 2
    flux_ref[...] = got_first[plane_of_flux, :, :LANES] + got_second[plane_of_flux, :, :LANES]
    even, _, _ = partner("radius", 0, 0)
    for lo in range(0, cols, LANES):
        hi = lo + LANES

        def tile(plane, own):
            one, two = got_first[plane, :, lo:hi], got_second[plane, :, lo:hi]
            return jnp.concatenate([jnp.where(even, two, one), own, jnp.where(even, one, two)], axis=0)

        d = tile(2 * groups, density[:, lo:hi])
        d = jnp.concatenate([d, d], axis=0).T
        m = tile(2 * groups + 1, material[:, lo:hi])
        m = jnp.concatenate([m, m], axis=0).T
        dens_ref[HALO + lo : HALO + hi, :] = d
        mat_ref[HALO + lo : HALO + hi, :] = m

        def one(p, carry):
            both = []
            for h in range(2):
                g = 2 * p + h
                both.append(tile(g, opacity[g, :, lo:hi].astype(jnp.float32) * density[:, lo:hi]))
            a = jnp.concatenate(both, axis=0).T
            a_ref[p, HALO + lo : HALO + hi, :] = jnp.where(dens_ref[HALO + lo : HALO + hi, :] > 0.0, a, 1.0)
            both = [tile(groups + 2 * p + h, old[2 * p + h, :, lo:hi]) for h in range(2)]
            e_ref[p, HALO + lo : HALO + hi, :] = jnp.concatenate(both, axis=0).T
            return carry

        lax.fori_loop(0, pairs, one, 0, unroll=8)
    _, lo_first, lo_second = partner("polar", cols, HALO)
    for out, lo in ((to_first, lo_first), (to_second, lo_second)):
        edge = pl.ds(pl.multiple_of(lo, HALO), HALO)
        for p in range(pairs):
            out[p] = a_ref[p, edge, :]
            out[pairs + p] = e_ref[p, edge, :]
        out[2 * pairs] = dens_ref[edge, :]
        out[2 * pairs + 1] = mat_ref[edge, :]


def next_row(v):
    return pltpu.roll(v, LANES - 1, 1)


def prev_row(v):
    return pltpu.roll(v, 1, 1)


def after(ref, lead, lo, hi, here, end):
    if hi < end:
        return ref[(*lead, slice(lo + 1, hi + 1), slice(None))]
    return pltpu.roll(here, hi - lo - 1, 0)


def before(ref, lead, lo, hi, here, begin):
    if lo > begin:
        return ref[(*lead, slice(lo - 1, hi - 1), slice(None))]
    return pltpu.roll(here, 1, 0)


def at(lo, hi):
    return (slice(lo, hi), slice(None))


def flux_sum(p, lo, hi, v_ref, v, fr_ref, fp_ref, span):
    begin, end = span
    fp = fp_ref[(p, *at(lo, hi))]
    fp_before = before(fp_ref, (p,), lo, hi, fp, begin)
    polar = fp * (v - after(v_ref, (p,), lo, hi, v, end)) + fp_before * (
        v - before(v_ref, (p,), lo, hi, v, begin)
    )
    fr = fr_ref[(p, *at(lo, hi))] * (v - next_row(v))
    return polar + (fr - prev_row(fr))


def tile_sum(v):
    acc = v[:HALO]
    for lo in range(HALO, v.shape[0], HALO):
        acc = acc + v[lo : lo + HALO]
    return acc


def krylov(p, pairs, parts, span, own, b_ref, fr_ref, fp_ref, r_ref, q_ref, t_ref, mom, old_mom=None):
    sums = [jnp.zeros((HALO, LANES), jnp.float32) for _ in range(4)]
    for lo, hi in parts:
        r = r_ref[(p, *at(lo, hi))]
        q = b_ref[(p, *at(lo, hi))] * r + flux_sum(p, lo, hi, r_ref, r, fr_ref, fp_ref, span)
        q_ref[(p, *at(lo, hi))] = q
        if lo >= own[0] and hi <= own[1]:
            sums[0] = sums[0] + tile_sum(r * r)
            sums[1] = sums[1] + tile_sum(r * q)
            sums[2] = sums[2] + tile_sum(q * q)
    for lo, hi in parts:
        inside = lo >= own[0] and hi <= own[1]
        if not inside and t_ref is None:
            continue
        q = q_ref[(p, *at(lo, hi))]
        t = b_ref[(p, *at(lo, hi))] * q + flux_sum(p, lo, hi, q_ref, q, fr_ref, fp_ref, span)
        if t_ref is not None:
            t_ref[(p, *at(lo, hi))] = t
        if inside:
            sums[3] = sums[3] + tile_sum(q * t)
    for k in range(4):
        total = jnp.sum(sums[k], axis=0, keepdims=True)
        if old_mom is not None:
            total = total + old_mom[pl.ds(k * pairs + p, 1), :]
        mom[pl.ds(k * pairs + p, 1), :] = total


def send_moments(pairs, rows, mom, out, row_sums):
    lane = lane_of(4 * pairs)
    x = mom[...]
    first = jnp.where((lane >= HALO) & (lane < HALO + rows), x, 0.0)
    second = jnp.where((lane >= HALF + HALO) & (lane < HALF + HALO + rows), x, 0.0)
    both = jnp.concatenate([first, second, jnp.zeros((LANES - 8 * pairs, LANES), jnp.float32)], axis=0)
    line = lax.dot_general(
        jnp.ones((HALO, LANES), jnp.float32), both, (((1,), (1,)), ((), ())),
        precision=HIGHEST, preferred_element_type=jnp.float32,
    )
    if row_sums is not None:
        line = jnp.where(lane_of(HALO) < HALF, line, row_sums)
    for lo in range(0, out.shape[0], HALO):
        out[lo : lo + HALO, :] = line


def weight_of(weights, p):
    return jnp.where(lane_of(HALO) < HALF, weights[2 * p], weights[2 * p + 1])[:1]


def fold(s):
    s = s + pltpu.roll(s, HALF, 1)
    middle = s.shape[0] // 2
    return jnp.where(lane_of(middle) < HALF, s[:middle], s[middle:])


def unfold(s):
    other = pltpu.roll(s, HALF, 1)
    low = lane_of(s.shape[0]) < HALF
    return jnp.where(low, s, other), jnp.where(low, other, s)


def first_residual(p, w, inverse_parts, parts, span, dens_ref, mat_ref, a_ref, e_ref, fr_ref, fp_ref, r_ref, inv):
    begin, end = span
    for lo, hi in inverse_parts:
        a, e = a_ref[(p, *at(lo, hi))], e_ref[(p, *at(lo, hi))]
        slope_r = next_row(e) - prev_row(e)
        slope_p = after(e_ref, (p,), lo, hi, e, end) - before(e_ref, (p,), lo, hi, e, begin)
        n2 = slope_r * slope_r + slope_p * slope_p
        u = a * e
        s = 4.0 * u + n2 * lax.rsqrt(n2 + 1e-37)
        inv[lo:hi, :] = jnp.where(dens_ref[lo:hi, :] > 0.0, (n2 + 6.0 * u * s) / (e * s), OUTSIDE)
    for lo, hi in parts:
        d = inv[lo:hi, :]
        fr_ref[(p, *at(lo, hi))] = 4.0 / (d + next_row(d))
        fp_ref[(p, *at(lo, hi))] = 4.0 / (d + after(inv, (), lo, hi, d, end))
    for lo, hi in parts:
        a, e = a_ref[(p, *at(lo, hi))], e_ref[(p, *at(lo, hi))]
        r_ref[(p, *at(lo, hi))] = a * (w * mat_ref[lo:hi, :] - e) - flux_sum(
            p, lo, hi, e_ref, e, fr_ref, fp_ref, span
        )


def inner_kernel(
    groups, cols, weights, a_ref, e_ref, dens_ref, mat_ref,
    fr_ref, fp_ref, r_ref, q_ref, t_ref, b_ref, emit, mom, inv,
):
    pairs = groups // 2
    span = (HALO, HALO + cols)
    parts = [(lo + HALO, hi + HALO) for lo, hi in pieces(cols)]
    own = (2 * HALO, cols)
    emit[...] = jnp.zeros(emit.shape, jnp.float32)

    def one(p, carry):
        w = weight_of(weights, p)
        for lo, hi in parts:
            a = a_ref[(p, *at(lo, hi))]
            b_ref[(p, *at(lo, hi))] = 1.0 + a
            emit[lo:hi, :] += a * w
        first_residual(p, w, parts, parts, span, dens_ref, mat_ref, a_ref, e_ref, fr_ref, fp_ref, r_ref, inv)
        krylov(p, pairs, parts, span, own, b_ref, fr_ref, fp_ref, r_ref, q_ref, t_ref, mom)
        return carry

    lax.fori_loop(0, pairs, one, 0, unroll=2)


def frame_kernel(groups, rows, cols, weights, got_first, got_second, emit, old_mom, *rest):
    a_ref, e_ref, fr_ref, fp_ref, r_ref, q_ref, t_ref, b_ref, dens_ref, mat_ref = rest[10:20]
    emit_out, out, inv, mom = rest[20:]
    pairs = groups // 2
    tall = cols + 2 * HALO
    span = (0, tall)
    even, _, _ = partner("polar", 0, 0)
    ends = ((0, HALO), (tall - HALO, tall))

    def halo(side, plane):
        one, two = got_first[plane], got_second[plane]
        return jnp.where(even, two, one) if side == 0 else jnp.where(even, one, two)

    for side, (lo, hi) in enumerate(ends):
        dens_ref[lo:hi, :] = halo(side, 2 * pairs)
        mat_ref[lo:hi, :] = halo(side, 2 * pairs + 1)
    parts = [(0, HALO), (HALO, 2 * HALO), (cols, cols + HALO), (cols + HALO, tall)]
    inverse_parts = parts[:2] + [(2 * HALO, 3 * HALO)] + parts[2:]

    def one(p, emitted):
        w = weight_of(weights, p)
        sums = []
        for side, (lo, hi) in enumerate(ends):
            a = jnp.where(dens_ref[lo:hi, :] > 0.0, halo(side, p), 1.0)
            a_ref[(p, *at(lo, hi))] = a
            b_ref[(p, *at(lo, hi))] = 1.0 + a
            e_ref[(p, *at(lo, hi))] = halo(side, pairs + p)
            sums.append(emitted[side] + a * w)
        first_residual(
            p, w, inverse_parts, parts, span, dens_ref, mat_ref, a_ref, e_ref, fr_ref, fp_ref, r_ref, inv
        )
        krylov(
            p, pairs, parts, span, (HALO, HALO + cols), b_ref, fr_ref, fp_ref, r_ref, q_ref, t_ref, mom, old_mom
        )
        return tuple(sums)

    zero = jnp.zeros((HALO, LANES), jnp.float32)
    low, high = lax.fori_loop(0, pairs, one, (zero, zero), unroll=8)
    emit_out[...] = fold(jnp.concatenate([low, emit[HALO : HALO + cols, :], high], axis=0))
    row_sums = jnp.sum(tile_sum(dens_ref[HALO : HALO + cols, :]), axis=0, keepdims=True)
    send_moments(pairs, rows, mom, out, row_sums)


def steps(pairs, gathered):
    total = jnp.sum(gathered[...], axis=0, keepdims=True)
    lane = lane_of(pairs)
    sub = lax.broadcasted_iota(jnp.int32, (pairs, LANES), 0)

    def moment(k):
        first, second = (
            jnp.sum(jnp.where(lane == sub + (4 * h + k) * pairs, total, 0.0), axis=1, keepdims=True)
            for h in range(2)
        )
        return jnp.where(lane < HALF, first, second)

    m0, m1, m2, m3 = (moment(k) for k in range(4))
    k1, k2, k3 = m1 / m0, m2 / m0, m3 / m0
    first = 1.0 / k1
    det = jnp.maximum(k2 - k1 * k1, 0.0)
    beta = det / (k1 * k1)
    low = k1 * k3 - k2 * k2
    second = jnp.minimum(jnp.where(low > 0.0, k1 * det / low, 0.0), 1.0)
    return first + second * (1.0 + beta), first * second


def absorbed(pairs, c1, c2, a_ref, e_ref, r_ref, q_ref, e_out, s):
    tall = a_ref.shape[1]
    for lo, hi in pieces(tall):
        total = jnp.zeros((hi - lo, LANES), jnp.float32)
        for p in range(pairs):
            e = (
                e_ref[(p, *at(lo, hi))]
                + c1[p : p + 1, :] * r_ref[(p, *at(lo, hi))]
                - c2[p : p + 1, :] * q_ref[(p, *at(lo, hi))]
            )
            e_out[(p, *at(lo, hi))] = e
            total = total + a_ref[(p, *at(lo, hi))] * e
        s[lo:hi, :] = total


def update_kernel(pairs, gathered, a_ref, e_ref, r_ref, q_ref, *rest):
    if len(rest) == 6:
        emit, *rest = rest
    else:
        emit = None
    e_out, s_out, c1_ref, c2_ref, s = rest
    c1, c2 = steps(pairs, gathered)
    c1_ref[...] = c1
    c2_ref[...] = c2
    absorbed(pairs, c1, c2, a_ref, e_ref, r_ref, q_ref, e_out, s)
    s_out[0] = fold(s[...])
    if emit is not None:
        s_out[1] = emit[...]


def last_update_kernel(pairs, cols, gathered, a_ref, e_ref, r_ref, q_ref, e_out, s_out, s):
    c1, c2 = steps(pairs, gathered)
    absorbed(pairs, c1, c2, a_ref, e_ref, r_ref, q_ref, e_out, s)
    s_out[...] = fold(s[HALO : HALO + cols, :])


def energy_kernel(pairs, rows, cols, e_ref, out):
    def one(p, carry):
        for lo in range(0, cols, LANES):
            block = e_ref[p, HALO + lo : HALO + lo + LANES, :].T
            out[2 * p, :, lo : lo + LANES] = block[HALO : HALO + rows]
            out[2 * p + 1, :, lo : lo + LANES] = block[HALF + HALO : HALF + HALO + rows]
        return carry

    lax.fori_loop(0, pairs, one, 0, unroll=4)


def turned_back(v, rows):
    parts = [v[lo : lo + LANES].T[HALO : HALO + rows] for lo in range(0, v.shape[0], LANES)]
    return jnp.concatenate(parts, axis=1)


def heating_kernel(
    groups, rows, cols, polar_count, flux, gathered, dens_ref, mat_ref, flux_ref, column_out, fixed_out
):
    tall = dens_ref.shape[0]
    radius, polar = lax.axis_index("radius"), lax.axis_index("polar")
    dens = dens_ref[...]
    row_id = lax.broadcasted_iota(jnp.int32, gathered.shape, 0)
    ahead = (row_id >= radius * polar_count) & (row_id < radius * polar_count + polar)
    carried = jnp.sum(jnp.where(ahead, gathered[...], 0.0), axis=0, keepdims=True)
    lane = lane_of()
    carried = jnp.where(lane < HALF, pltpu.roll(carried, HALF, 1), carried)
    dst = lax.broadcasted_iota(jnp.int32, (tall, tall), 0)
    src = lax.broadcasted_iota(jnp.int32, (tall, tall), 1)
    coeff = jnp.where(
        (src >= HALO) & (src <= dst), 1.0, jnp.where((src < HALO) & (src > dst), -1.0, 0.0)
    )
    within = lax.dot_general(
        coeff, dens, (((1,), (0,)), ((), ())), precision=HIGHEST, preferred_element_type=jnp.float32
    )
    column = 2.0 / (cols * polar_count) * (carried + within)
    vec = flux_ref[0:1, :]
    for i in range(rows):
        vec = jnp.where(lane % HALF == HALO + i, flux[i], vec)
    fixed_out[...] = 16.0 * dens * mat_ref[...] + vec * dens * jnp.exp(-column)
    column_out[...] = turned_back(column[HALO : HALO + cols], rows)


def summed(refs, lead=()):
    total = refs[0][(*lead, ...)]
    for s in refs[1:]:
        total = total + s[(*lead, ...)]
    return total


def next_kernel(groups, rows, count, turn, last, weights, c1_ref, c2_ref, a_ref, b_ref, fr_ref, fp_ref, r_in, q_in, t_in, fixed, cap_in, mat_ref, *rest):
    pairs = groups // 2
    sums = rest[:count]
    rest = rest[count:]
    outs, (delta, mom) = rest[:-2], rest[-2:]
    r_ref, q_ref, out, *outs = outs
    t_ref = None if last else outs.pop(0)
    m_ref = None if last else outs.pop(0)
    tall = fixed.shape[0]
    parts = pieces(tall)
    half = tall // 2
    folded = summed(sums, (0,))
    if turn == 0:
        cap_out = outs.pop(0)
        dens = cap_in[...]
        emits = jnp.concatenate(unfold(summed(sums, (1,))), axis=0)
        cap_out[...] = 16.0 * jnp.where(dens > 0.0, dens, 1.0) + emits
        cap_in = cap_out
    for k, total in enumerate(unfold(folded)):
        here = at(k * half, (k + 1) * half)
        nxt = (fixed[here] + total) / cap_in[here]
        delta[here] = nxt - mat_ref[here]
        if m_ref is not None:
            m_ref[here] = nxt

    def one(p, carry):
        w = weight_of(weights, p)
        c1 = c1_ref[pl.ds(p, 1), :]
        c2 = c2_ref[pl.ds(p, 1), :]
        for lo, hi in parts:
            here = (p, *at(lo, hi))
            r_ref[here] = (
                r_in[here] - c1 * q_in[here] + c2 * t_in[here] + a_ref[here] * (w * delta[lo:hi, :])
            )
        krylov(p, pairs, parts, (0, tall), (HALO, tall - HALO), b_ref, fr_ref, fp_ref, r_ref, q_ref, t_ref, mom)
        return carry

    lax.fori_loop(0, pairs, one, 0, unroll=2)
    send_moments(pairs, rows, mom, out, None)


def material_kernel(count, rows, cols, fixed, capacity, *rest):
    sums, out = rest[:count], rest[count]
    total = jnp.concatenate(unfold(summed(sums)), axis=0)
    here = at(HALO, HALO + cols)
    out[...] = turned_back((fixed[here] + total) / capacity[here], rows)


def spread(part, axis):
    count = lax.axis_size(axis)
    return [part] + [lax.ppermute(part, axis, [(i, i ^ s) for i in range(count)]) for s in range(1, count)]


def pair_up(first, axis):
    return lax.ppermute(first, axis, [(i, i ^ 1) for i in range(lax.axis_size(axis))])


def pair_across(second, axis):
    links = [(i, i + 1) for i in range(1, lax.axis_size(axis) - 1, 2)]
    return lax.ppermute(second, axis, links + [(j, i) for i, j in links])


def per_device(density, opacity, radiation_old, material_old, weights, stellar_flux):
    groups, rows, cols = opacity.shape
    pairs, tall = groups // 2, cols + 2 * HALO
    assert rows + 2 * HALO == HALF
    polar_count = lax.axis_size("polar")
    count = lax.axis_size("group")
    devices = lax.axis_size("radius") * polar_count
    planes = 2 * groups + 3
    big, flat, core = (pairs, tall, LANES), (tall, LANES), (cols, LANES)
    line = (devices, LANES)
    edge = (2 * pairs + 2, HALO, LANES)
    vmem = lambda shape: pltpu.VMEM(shape, jnp.float32)

    strips = [
        pltpu.VMEM((groups, 2 * HALO, cols), jnp.bfloat16),
        vmem((groups, HALO, cols)),
        vmem((HALO, cols)),
        vmem((HALO, cols)),
    ]
    first, second = call(
        functools.partial(pack_rows_kernel, groups, rows),
        [(planes, HALO, cols)] * 2,
        tuple(
            pltpu.with_memory_space_constraint(v, pltpu.HBM)
            for v in (stellar_flux, opacity, radiation_old, density, material_old)
        ),
        [hspec()] * 5,
        scratch=strips * 2 + [pltpu.SMEM((rows,), jnp.float32), pltpu.SemaphoreType.DMA((9,))],
        name="pack_rows",
        limit=20 * 1024 * 1024,
    )
    second = pair_across(second, "radius")
    first = pair_up(first, "radius")
    a, e, dens, mat, flux_lanes, first, second = call(
        functools.partial(turn_kernel, groups, rows, cols),
        [big] * 2 + [flat, flat, (HALO, LANES), edge, edge],
        (opacity, radiation_old, density, material_old, second, first),
        [vspec()] * 6,
        name="turn",
    )
    first, second = pair_up(first, "polar"), pair_across(second, "polar")
    fr, fp, r, q, t, b, emit, mom = call(
        functools.partial(inner_kernel, groups, cols),
        [big] * 6 + [flat, (4 * pairs, LANES)],
        (weights, a, e, dens, mat),
        [sspec()] + [vspec()] * 4,
        scratch=[vmem(flat)],
        name="inner",
    )
    a, e, fr, fp, r, q, t, b, dens, mat, emit, out = call(
        functools.partial(frame_kernel, groups, rows, cols),
        [big] * 8 + [flat, flat, (tall // 2, LANES), line],
        (weights, first, second, emit, mom, a, e, fr, fp, r, q, t, b, dens, mat),
        [sspec()] + [vspec()] * 14,
        scratch=[vmem(flat), vmem((4 * pairs, LANES))],
        name="frame",
        aliases={5 + k: k for k in range(10)},
    )
    capacity = dens
    for turn in range(ITERS):
        gathered = lax.all_to_all(out, ("radius", "polar"), 0, 0, tiled=True)
        if turn + 1 == ITERS:
            e, part = call(
                functools.partial(last_update_kernel, pairs, cols),
                [big, (cols // 2, LANES)],
                (gathered, a, e, r, q),
                [vspec()] * 5,
                scratch=[vmem(flat)],
                name="last_update",
            )
            sums = spread(part, "group")
            (energy,) = call(
                functools.partial(energy_kernel, pairs, rows, cols),
                [(groups, rows, cols)],
                (e,),
                [vspec()],
                name="energy",
            )
            (mat,) = call(
                functools.partial(material_kernel, count, rows, cols),
                [(rows, cols)],
                (fixed, capacity, *sums),
                [vspec()] * (2 + count),
                name="material",
            )
            break
        first, last = turn == 0, turn + 2 == ITERS
        extra = [emit] if first else []
        e, part, c1, c2 = call(
            functools.partial(update_kernel, pairs),
            [big, (1 + len(extra), tall // 2, LANES), (pairs, LANES), (pairs, LANES)],
            (gathered, a, e, r, q, *extra),
            [vspec()] * (5 + len(extra)),
            scratch=[vmem(flat)],
            name="update",
        )
        sums = spread(part, "group")
        if first:
            column, fixed = call(
                functools.partial(heating_kernel, groups, rows, cols, polar_count),
                [(rows, cols), flat],
                (stellar_flux, gathered, dens, mat, flux_lanes),
                [sspec()] + [vspec()] * 4,
                name="heating",
            )
        r, q, out, *more = call(
            functools.partial(next_kernel, groups, rows, count, turn, last),
            [big, big, line] + ([] if last else [big, flat]) + ([flat] if first else []),
            (weights, c1, c2, a, b, fr, fp, r, q, t, fixed, capacity, mat, *sums),
            [sspec()] + [vspec()] * (12 + count),
            scratch=[vmem(flat), vmem((4 * pairs, LANES))],
            name="next",
        )
        if not last:
            t, mat, *more = more
        if first:
            (capacity,) = more
    return (energy, mat, column)


def solution(mesh):
    return jax.shard_map(
        per_device,
        mesh=mesh,
        in_specs=(
            P("radius", "polar"),
            P("group", "radius", "polar"),
            P("group", "radius", "polar"),
            P("radius", "polar"),
            P("group"),
            P("radius"),
        ),
        out_specs=(P("group", "radius", "polar"), P("radius", "polar"), P("radius", "polar")),
        check_vma=False,
    )
```

```python
import functools
import jax
import jax.numpy as jnp
from jax import lax
from jax.experimental import pallas as pl
from jax.experimental.pallas import tpu as pltpu
from jax.sharding import PartitionSpec as P


ITERS = 3
HALO = 8
LANES = 128
HALF = LANES // 2
STEP = 64
VMEM_LIMIT = 12 * 1024 * 1024
HIGHEST = lax.Precision.HIGHEST
OUTSIDE = 1.6e38


def vspec():
    return pl.BlockSpec(memory_space=pltpu.VMEM)


def sspec():
    return pl.BlockSpec(memory_space=pltpu.SMEM)


def hspec():
    return pl.BlockSpec(memory_space=pltpu.HBM)


def call(kernel, outs, args, specs, scratch=(), flops=1000000, nbytes=1000000, name=None, limit=VMEM_LIMIT, aliases=None):
    return pl.pallas_call(
        kernel,
        out_shape=[jax.ShapeDtypeStruct(s, jnp.float32) for s in outs],
        in_specs=specs,
        out_specs=[vspec() for _ in outs],
        scratch_shapes=list(scratch),
        compiler_params=pltpu.CompilerParams(vmem_limit_bytes=limit),
        cost_estimate=pl.CostEstimate(flops=flops, bytes_accessed=nbytes, transcendentals=0),
        name=name,
        input_output_aliases=aliases or {},
    )(*args)


def lane_of(height=1):
    return lax.broadcasted_iota(jnp.int32, (height, LANES), 1)


def pieces(tall):
    cuts = [0, HALO]
    while cuts[-1] + STEP < tall - HALO:
        cuts.append(cuts[-1] + STEP)
    cuts += [tall - HALO, tall]
    return list(zip(cuts[:-1], cuts[1:]))


def partner(axis, inner, outer):
    even = lax.rem(lax.axis_index(axis), 2) == 0
    return even, jnp.where(even, inner, outer), jnp.where(even, outer, inner)


def pack_rows_kernel(groups, rows, flux_in, opacity, old, density, material, first, second, *scratch):
    even, lo_first, lo_second = partner("radius", rows - HALO, 0)
    flux, sems = scratch[-2:]
    sides = ((first, lo_first, even), (second, lo_second, jnp.logical_not(even)))
    copies = [pltpu.make_async_copy(flux_in, flux, sems.at[8])]
    for side, (_, lo, at_end) in enumerate(sides):
        op_buf, old_buf, dens_buf, mat_buf = scratch[4 * side : 4 * side + 4]
        lo = pl.multiple_of(lo, HALO)
        base = pl.multiple_of(jnp.where(at_end, rows - 2 * HALO, 0), 2 * HALO)
        moves = (
            (opacity.at[:, pl.ds(base, 2 * HALO), :], op_buf),
            (old.at[:, pl.ds(lo, HALO), :], old_buf),
            (density.at[pl.ds(lo, HALO), :], dens_buf),
            (material.at[pl.ds(lo, HALO), :], mat_buf),
        )
        for k, (src, dst) in enumerate(moves):
            copies.append(pltpu.make_async_copy(src, dst, sems.at[4 * side + k]))
    for c in copies:
        c.start()
    for c in copies:
        c.wait()
    lane = lane_of(HALO) % HALF
    for side, (out, lo, at_end) in enumerate(sides):
        op_buf, old_buf, dens_buf, mat_buf = scratch[4 * side : 4 * side + 4]
        dens = dens_buf[...]
        for g in range(groups):
            part = op_buf[g].astype(jnp.float32)
            out[g] = jnp.where(at_end, part[HALO:], part[:HALO]) * dens
            out[groups + g] = old_buf[g]
        out[2 * groups] = dens
        out[2 * groups + 1] = mat_buf[...]
        place = jnp.where(at_end, 0, rows + HALO)
        vec = jnp.zeros((HALO, LANES), jnp.float32)
        for i in range(HALO):
            vec = jnp.where(lane == place + i, flux[lo + i], vec)
        for at_lane in range(0, out.shape[2], LANES):
            out[2 * groups + 2, :, at_lane : at_lane + LANES] = vec


def turn_kernel(
    groups, rows, cols, opacity, old, density, material, got_second, got_first,
    a_ref, e_ref, dens_ref, mat_ref, flux_ref, to_first, to_second,
):
    pairs = groups // 2
    plane_of_flux = 2 * groups + 2
    flux_ref[...] = got_first[plane_of_flux, :, :LANES] + got_second[plane_of_flux, :, :LANES]
    even, _, _ = partner("radius", 0, 0)
    for lo in range(0, cols, LANES):
        hi = lo + LANES

        def tile(plane, own):
            one, two = got_first[plane, :, lo:hi], got_second[plane, :, lo:hi]
            return jnp.concatenate([jnp.where(even, two, one), own, jnp.where(even, one, two)], axis=0)

        d = tile(2 * groups, density[:, lo:hi])
        d = jnp.concatenate([d, d], axis=0).T
        m = tile(2 * groups + 1, material[:, lo:hi])
        m = jnp.concatenate([m, m], axis=0).T
        dens_ref[HALO + lo : HALO + hi, :] = d
        mat_ref[HALO + lo : HALO + hi, :] = m

        def one(p, carry):
            both = []
            for h in range(2):
                g = 2 * p + h
                both.append(tile(g, opacity[g, :, lo:hi].astype(jnp.float32) * density[:, lo:hi]))
            a = jnp.concatenate(both, axis=0).T
            a_ref[p, HALO + lo : HALO + hi, :] = jnp.where(dens_ref[HALO + lo : HALO + hi, :] > 0.0, a, 1.0)
            both = [tile(groups + 2 * p + h, old[2 * p + h, :, lo:hi]) for h in range(2)]
            e_ref[p, HALO + lo : HALO + hi, :] = jnp.concatenate(both, axis=0).T
            return carry

        lax.fori_loop(0, pairs, one, 0, unroll=8)
    _, lo_first, lo_second = partner("polar", cols, HALO)
    for out, lo in ((to_first, lo_first), (to_second, lo_second)):
        edge = pl.ds(pl.multiple_of(lo, HALO), HALO)
        for p in range(pairs):
            out[p] = a_ref[p, edge, :]
            out[pairs + p] = e_ref[p, edge, :]
        out[2 * pairs] = dens_ref[edge, :]
        out[2 * pairs + 1] = mat_ref[edge, :]


def next_row(v):
    return pltpu.roll(v, LANES - 1, 1)


def prev_row(v):
    return pltpu.roll(v, 1, 1)


def after(ref, lead, lo, hi, here, end):
    if hi < end:
        return ref[(*lead, slice(lo + 1, hi + 1), slice(None))]
    return pltpu.roll(here, hi - lo - 1, 0)


def before(ref, lead, lo, hi, here, begin):
    if lo > begin:
        return ref[(*lead, slice(lo - 1, hi - 1), slice(None))]
    return pltpu.roll(here, 1, 0)


def at(lo, hi):
    return (slice(lo, hi), slice(None))


def flux_sum(p, lo, hi, v_ref, v, fr_ref, fp_ref, span):
    begin, end = span
    fp = fp_ref[(p, *at(lo, hi))]
    fp_before = before(fp_ref, (p,), lo, hi, fp, begin)
    polar = fp * (v - after(v_ref, (p,), lo, hi, v, end)) + fp_before * (
        v - before(v_ref, (p,), lo, hi, v, begin)
    )
    fr = fr_ref[(p, *at(lo, hi))] * (v - next_row(v))
    return polar + (fr - prev_row(fr))


def tile_sum(v):
    acc = v[:HALO]
    for lo in range(HALO, v.shape[0], HALO):
        acc = acc + v[lo : lo + HALO]
    return acc


def krylov(p, pairs, parts, span, own, b_ref, fr_ref, fp_ref, r_ref, q_ref, t_ref, mom, old_mom=None):
    sums = [jnp.zeros((HALO, LANES), jnp.float32) for _ in range(4)]
    for lo, hi in parts:
        r = r_ref[(p, *at(lo, hi))]
        q = b_ref[(p, *at(lo, hi))] * r + flux_sum(p, lo, hi, r_ref, r, fr_ref, fp_ref, span)
        q_ref[(p, *at(lo, hi))] = q
        if lo >= own[0] and hi <= own[1]:
            sums[0] = sums[0] + tile_sum(r * r)
            sums[1] = sums[1] + tile_sum(r * q)
            sums[2] = sums[2] + tile_sum(q * q)
    for lo, hi in parts:
        inside = lo >= own[0] and hi <= own[1]
        if not inside and t_ref is None:
            continue
        q = q_ref[(p, *at(lo, hi))]
        t = b_ref[(p, *at(lo, hi))] * q + flux_sum(p, lo, hi, q_ref, q, fr_ref, fp_ref, span)
        if t_ref is not None:
            t_ref[(p, *at(lo, hi))] = t
        if inside:
            sums[3] = sums[3] + tile_sum(q * t)
    for k in range(4):
        total = jnp.sum(sums[k], axis=0, keepdims=True)
        if old_mom is not None:
            total = total + old_mom[pl.ds(k * pairs + p, 1), :]
        mom[pl.ds(k * pairs + p, 1), :] = total


def send_moments(pairs, rows, mom, out, row_sums):
    lane = lane_of(4 * pairs)
    x = mom[...]
    first = jnp.where((lane >= HALO) & (lane < HALO + rows), x, 0.0)
    second = jnp.where((lane >= HALF + HALO) & (lane < HALF + HALO + rows), x, 0.0)
    both = jnp.concatenate([first, second, jnp.zeros((LANES - 8 * pairs, LANES), jnp.float32)], axis=0)
    line = lax.dot_general(
        jnp.ones((HALO, LANES), jnp.float32), both, (((1,), (1,)), ((), ())),
        precision=HIGHEST, preferred_element_type=jnp.float32,
    )
    if row_sums is not None:
        line = jnp.where(lane_of(HALO) < HALF, line, row_sums)
    for lo in range(0, out.shape[0], HALO):
        out[lo : lo + HALO, :] = line


def weight_of(weights, p):
    return jnp.where(lane_of(HALO) < HALF, weights[2 * p], weights[2 * p + 1])[:1]


def fold(s):
    s = s + pltpu.roll(s, HALF, 1)
    middle = s.shape[0] // 2
    return jnp.where(lane_of(middle) < HALF, s[:middle], s[middle:])


def unfold(s):
    other = pltpu.roll(s, HALF, 1)
    low = lane_of(s.shape[0]) < HALF
    return jnp.where(low, s, other), jnp.where(low, other, s)


def first_residual(p, w, inverse_parts, parts, span, dens_ref, mat_ref, a_ref, e_ref, fr_ref, fp_ref, r_ref, inv):
    begin, end = span
    for lo, hi in inverse_parts:
        a, e = a_ref[(p, *at(lo, hi))], e_ref[(p, *at(lo, hi))]
        slope_r = next_row(e) - prev_row(e)
        slope_p = after(e_ref, (p,), lo, hi, e, end) - before(e_ref, (p,), lo, hi, e, begin)
        n2 = slope_r * slope_r + slope_p * slope_p
        u = a * e
        s = 4.0 * u + n2 * lax.rsqrt(n2 + 1e-37)
        inv[lo:hi, :] = jnp.where(dens_ref[lo:hi, :] > 0.0, (n2 + 6.0 * u * s) / (e * s), OUTSIDE)
    for lo, hi in parts:
        d = inv[lo:hi, :]
        fr_ref[(p, *at(lo, hi))] = 4.0 / (d + next_row(d))
        fp_ref[(p, *at(lo, hi))] = 4.0 / (d + after(inv, (), lo, hi, d, end))
    for lo, hi in parts:
        a, e = a_ref[(p, *at(lo, hi))], e_ref[(p, *at(lo, hi))]
        r_ref[(p, *at(lo, hi))] = a * (w * mat_ref[lo:hi, :] - e) - flux_sum(
            p, lo, hi, e_ref, e, fr_ref, fp_ref, span
        )


def inner_kernel(
    groups, cols, weights, a_ref, e_ref, dens_ref, mat_ref,
    fr_ref, fp_ref, r_ref, q_ref, t_ref, b_ref, emit, mom, inv,
):
    pairs = groups // 2
    span = (HALO, HALO + cols)
    parts = [(lo + HALO, hi + HALO) for lo, hi in pieces(cols)]
    own = (2 * HALO, cols)
    emit[...] = jnp.zeros(emit.shape, jnp.float32)

    def one(p, carry):
        w = weight_of(weights, p)
        for lo, hi in parts:
            a = a_ref[(p, *at(lo, hi))]
            b_ref[(p, *at(lo, hi))] = 1.0 + a
            emit[lo:hi, :] += a * w
        first_residual(p, w, parts, parts, span, dens_ref, mat_ref, a_ref, e_ref, fr_ref, fp_ref, r_ref, inv)
        krylov(p, pairs, parts, span, own, b_ref, fr_ref, fp_ref, r_ref, q_ref, t_ref, mom)
        return carry

    lax.fori_loop(0, pairs, one, 0, unroll=2)


def frame_kernel(groups, rows, cols, weights, got_first, got_second, emit, old_mom, *rest):
    a_ref, e_ref, fr_ref, fp_ref, r_ref, q_ref, t_ref, b_ref, dens_ref, mat_ref = rest[10:20]
    emit_out, out, inv, mom = rest[20:]
    pairs = groups // 2
    tall = cols + 2 * HALO
    span = (0, tall)
    even, _, _ = partner("polar", 0, 0)
    ends = ((0, HALO), (tall - HALO, tall))

    def halo(side, plane):
        one, two = got_first[plane], got_second[plane]
        return jnp.where(even, two, one) if side == 0 else jnp.where(even, one, two)

    for side, (lo, hi) in enumerate(ends):
        dens_ref[lo:hi, :] = halo(side, 2 * pairs)
        mat_ref[lo:hi, :] = halo(side, 2 * pairs + 1)
    parts = [(0, HALO), (HALO, 2 * HALO), (cols, cols + HALO), (cols + HALO, tall)]
    inverse_parts = parts[:2] + [(2 * HALO, 3 * HALO)] + parts[2:]

    def one(p, emitted):
        w = weight_of(weights, p)
        sums = []
        for side, (lo, hi) in enumerate(ends):
            a = jnp.where(dens_ref[lo:hi, :] > 0.0, halo(side, p), 1.0)
            a_ref[(p, *at(lo, hi))] = a
            b_ref[(p, *at(lo, hi))] = 1.0 + a
            e_ref[(p, *at(lo, hi))] = halo(side, pairs + p)
            sums.append(emitted[side] + a * w)
        first_residual(
            p, w, inverse_parts, parts, span, dens_ref, mat_ref, a_ref, e_ref, fr_ref, fp_ref, r_ref, inv
        )
        krylov(
            p, pairs, parts, span, (HALO, HALO + cols), b_ref, fr_ref, fp_ref, r_ref, q_ref, t_ref, mom, old_mom
        )
        return tuple(sums)

    zero = jnp.zeros((HALO, LANES), jnp.float32)
    low, high = lax.fori_loop(0, pairs, one, (zero, zero), unroll=8)
    emit_out[...] = fold(jnp.concatenate([low, emit[HALO : HALO + cols, :], high], axis=0))
    row_sums = jnp.sum(tile_sum(dens_ref[HALO : HALO + cols, :]), axis=0, keepdims=True)
    send_moments(pairs, rows, mom, out, row_sums)


def steps(pairs, gathered):
    total = jnp.sum(gathered[...], axis=0, keepdims=True)
    lane = lane_of(pairs)
    sub = lax.broadcasted_iota(jnp.int32, (pairs, LANES), 0)

    def moment(k):
        first, second = (
            jnp.sum(jnp.where(lane == sub + (4 * h + k) * pairs, total, 0.0), axis=1, keepdims=True)
            for h in range(2)
        )
        return jnp.where(lane < HALF, first, second)

    m0, m1, m2, m3 = (moment(k) for k in range(4))
    k1, k2, k3 = m1 / m0, m2 / m0, m3 / m0
    first = 1.0 / k1
    det = jnp.maximum(k2 - k1 * k1, 0.0)
    beta = det / (k1 * k1)
    low = k1 * k3 - k2 * k2
    second = jnp.minimum(jnp.where(low > 0.0, k1 * det / low, 0.0), 1.0)
    return first + second * (1.0 + beta), first * second


def absorbed(pairs, c1, c2, a_ref, e_ref, r_ref, q_ref, e_out, s):
    tall = a_ref.shape[1]
    for lo, hi in pieces(tall):
        total = jnp.zeros((hi - lo, LANES), jnp.float32)
        for p in range(pairs):
            e = (
                e_ref[(p, *at(lo, hi))]
                + c1[p : p + 1, :] * r_ref[(p, *at(lo, hi))]
                - c2[p : p + 1, :] * q_ref[(p, *at(lo, hi))]
            )
            e_out[(p, *at(lo, hi))] = e
            total = total + a_ref[(p, *at(lo, hi))] * e
        s[lo:hi, :] = total


def update_kernel(pairs, gathered, a_ref, e_ref, r_ref, q_ref, *rest):
    if len(rest) == 6:
        emit, *rest = rest
    else:
        emit = None
    e_out, s_out, c1_ref, c2_ref, s = rest
    c1, c2 = steps(pairs, gathered)
    c1_ref[...] = c1
    c2_ref[...] = c2
    absorbed(pairs, c1, c2, a_ref, e_ref, r_ref, q_ref, e_out, s)
    s_out[0] = fold(s[...])
    if emit is not None:
        s_out[1] = emit[...]


def turned_back(v, rows):
    parts = [v[lo : lo + LANES].T[HALO : HALO + rows] for lo in range(0, v.shape[0], LANES)]
    return jnp.concatenate(parts, axis=1)


def last_update_kernel(pairs, rows, cols, gathered, a_ref, e_ref, r_ref, q_ref, e_out, s_out, s):
    c1, c2 = steps(pairs, gathered)
    absorbed(pairs, c1, c2, a_ref, e_ref, r_ref, q_ref, e_out, s)
    total = s[HALO : HALO + cols, :]
    s_out[...] = turned_back(total + pltpu.roll(total, HALF, 1), rows)


def energy_kernel(pairs, rows, cols, e_ref, fixed, capacity, out, fixed_out, capacity_out):
    def one(p, carry):
        for lo in range(0, cols, LANES):
            block = e_ref[p, HALO + lo : HALO + lo + LANES, :].T
            out[2 * p, :, lo : lo + LANES] = block[HALO : HALO + rows]
            out[2 * p + 1, :, lo : lo + LANES] = block[HALF + HALO : HALF + HALO + rows]
        return carry

    lax.fori_loop(0, pairs, one, 0, unroll=4)
    fixed_out[...] = turned_back(fixed[HALO : HALO + cols, :], rows)
    capacity_out[...] = turned_back(capacity[HALO : HALO + cols, :], rows)


def heating_kernel(
    groups, rows, cols, polar_count, flux, gathered, dens_ref, mat_ref, flux_ref, column_out, fixed_out
):
    tall = dens_ref.shape[0]
    radius, polar = lax.axis_index("radius"), lax.axis_index("polar")
    dens = dens_ref[...]
    row_id = lax.broadcasted_iota(jnp.int32, gathered.shape, 0)
    ahead = (row_id >= radius * polar_count) & (row_id < radius * polar_count + polar)
    carried = jnp.sum(jnp.where(ahead, gathered[...], 0.0), axis=0, keepdims=True)
    lane = lane_of()
    carried = jnp.where(lane < HALF, pltpu.roll(carried, HALF, 1), carried)
    dst = lax.broadcasted_iota(jnp.int32, (tall, tall), 0)
    src = lax.broadcasted_iota(jnp.int32, (tall, tall), 1)
    coeff = jnp.where(
        (src >= HALO) & (src <= dst), 1.0, jnp.where((src < HALO) & (src > dst), -1.0, 0.0)
    )
    within = lax.dot_general(
        coeff, dens, (((1,), (0,)), ((), ())), precision=HIGHEST, preferred_element_type=jnp.float32
    )
    column = 2.0 / (cols * polar_count) * (carried + within)
    vec = flux_ref[0:1, :]
    for i in range(rows):
        vec = jnp.where(lane % HALF == HALO + i, flux[i], vec)
    fixed_out[...] = 16.0 * dens * mat_ref[...] + vec * dens * jnp.exp(-column)
    column_out[...] = turned_back(column[HALO : HALO + cols], rows)


def summed(refs, lead=()):
    total = refs[0][(*lead, ...)]
    for s in refs[1:]:
        total = total + s[(*lead, ...)]
    return total


def next_kernel(groups, rows, count, turn, last, weights, c1_ref, c2_ref, a_ref, b_ref, fr_ref, fp_ref, r_in, q_in, t_in, fixed, cap_in, mat_ref, *rest):
    pairs = groups // 2
    sums = rest[:count]
    rest = rest[count:]
    outs, (delta, mom) = rest[:-2], rest[-2:]
    r_ref, q_ref, out, *outs = outs
    t_ref = None if last else outs.pop(0)
    m_ref = None if last else outs.pop(0)
    tall = fixed.shape[0]
    parts = pieces(tall)
    half = tall // 2
    folded = summed(sums, (0,))
    if turn == 0:
        cap_out = outs.pop(0)
        dens = cap_in[...]
        emits = jnp.concatenate(unfold(summed(sums, (1,))), axis=0)
        cap_out[...] = 16.0 * jnp.where(dens > 0.0, dens, 1.0) + emits
        cap_in = cap_out
    for k, total in enumerate(unfold(folded)):
        here = at(k * half, (k + 1) * half)
        nxt = (fixed[here] + total) / cap_in[here]
        delta[here] = nxt - mat_ref[here]
        if m_ref is not None:
            m_ref[here] = nxt

    def one(p, carry):
        w = weight_of(weights, p)
        c1 = c1_ref[pl.ds(p, 1), :]
        c2 = c2_ref[pl.ds(p, 1), :]
        for lo, hi in parts:
            here = (p, *at(lo, hi))
            r_ref[here] = (
                r_in[here] - c1 * q_in[here] + c2 * t_in[here] + a_ref[here] * (w * delta[lo:hi, :])
            )
        krylov(p, pairs, parts, (0, tall), (HALO, tall - HALO), b_ref, fr_ref, fp_ref, r_ref, q_ref, t_ref, mom)
        return carry

    lax.fori_loop(0, pairs, one, 0, unroll=2)
    send_moments(pairs, rows, mom, out, None)


def material_kernel(fixed, capacity, *rest):
    sums, out = rest[:-1], rest[-1]
    out[...] = (fixed[...] + summed(sums)) / capacity[...]


def spread(part, axis):
    count = lax.axis_size(axis)
    return [part] + [lax.ppermute(part, axis, [(i, i ^ s) for i in range(count)]) for s in range(1, count)]


def pair_up(first, axis):
    return lax.ppermute(first, axis, [(i, i ^ 1) for i in range(lax.axis_size(axis))])


def pair_across(second, axis):
    links = [(i, i + 1) for i in range(1, lax.axis_size(axis) - 1, 2)]
    return lax.ppermute(second, axis, links + [(j, i) for i, j in links])


def per_device(density, opacity, radiation_old, material_old, weights, stellar_flux):
    groups, rows, cols = opacity.shape
    pairs, tall = groups // 2, cols + 2 * HALO
    assert rows + 2 * HALO == HALF
    polar_count = lax.axis_size("polar")
    count = lax.axis_size("group")
    devices = lax.axis_size("radius") * polar_count
    planes = 2 * groups + 3
    big, flat, core = (pairs, tall, LANES), (tall, LANES), (cols, LANES)
    line = (devices, LANES)
    edge = (2 * pairs + 2, HALO, LANES)
    vmem = lambda shape: pltpu.VMEM(shape, jnp.float32)

    strips = [
        pltpu.VMEM((groups, 2 * HALO, cols), jnp.bfloat16),
        vmem((groups, HALO, cols)),
        vmem((HALO, cols)),
        vmem((HALO, cols)),
    ]
    first, second = call(
        functools.partial(pack_rows_kernel, groups, rows),
        [(planes, HALO, cols)] * 2,
        tuple(
            pltpu.with_memory_space_constraint(v, pltpu.HBM)
            for v in (stellar_flux, opacity, radiation_old, density, material_old)
        ),
        [hspec()] * 5,
        scratch=strips * 2 + [pltpu.SMEM((rows,), jnp.float32), pltpu.SemaphoreType.DMA((9,))],
        name="pack_rows",
        limit=20 * 1024 * 1024,
    )
    second = pair_across(second, "radius")
    first = pair_up(first, "radius")
    a, e, dens, mat, flux_lanes, first, second = call(
        functools.partial(turn_kernel, groups, rows, cols),
        [big] * 2 + [flat, flat, (HALO, LANES), edge, edge],
        (opacity, radiation_old, density, material_old, second, first),
        [vspec()] * 6,
        name="turn",
    )
    first, second = pair_up(first, "polar"), pair_across(second, "polar")
    fr, fp, r, q, t, b, emit, mom = call(
        functools.partial(inner_kernel, groups, cols),
        [big] * 6 + [flat, (4 * pairs, LANES)],
        (weights, a, e, dens, mat),
        [sspec()] + [vspec()] * 4,
        scratch=[vmem(flat)],
        name="inner",
    )
    a, e, fr, fp, r, q, t, b, dens, mat, emit, out = call(
        functools.partial(frame_kernel, groups, rows, cols),
        [big] * 8 + [flat, flat, (tall // 2, LANES), line],
        (weights, first, second, emit, mom, a, e, fr, fp, r, q, t, b, dens, mat),
        [sspec()] + [vspec()] * 14,
        scratch=[vmem(flat), vmem((4 * pairs, LANES))],
        name="frame",
        aliases={5 + k: k for k in range(10)},
    )
    capacity = dens
    for turn in range(ITERS):
        gathered = lax.all_to_all(out, ("radius", "polar"), 0, 0, tiled=True)
        if turn + 1 == ITERS:
            e, part = call(
                functools.partial(last_update_kernel, pairs, rows, cols),
                [big, (rows, cols)],
                (gathered, a, e, r, q),
                [vspec()] * 5,
                scratch=[vmem(flat)],
                name="last_update",
            )
            sums = spread(part, "group")
            energy, fixed, capacity = call(
                functools.partial(energy_kernel, pairs, rows, cols),
                [(groups, rows, cols), (rows, cols), (rows, cols)],
                (e, fixed, capacity),
                [vspec()] * 3,
                name="energy",
            )
            (mat,) = call(
                material_kernel,
                [(rows, cols)],
                (fixed, capacity, *sums),
                [vspec()] * (2 + count),
                name="material",
            )
            break
        first, last = turn == 0, turn + 2 == ITERS
        extra = [emit] if first else []
        e, part, c1, c2 = call(
            functools.partial(update_kernel, pairs),
            [big, (1 + len(extra), tall // 2, LANES), (pairs, LANES), (pairs, LANES)],
            (gathered, a, e, r, q, *extra),
            [vspec()] * (5 + len(extra)),
            scratch=[vmem(flat)],
            name="update",
        )
        sums = spread(part, "group")
        if first:
            column, fixed = call(
                functools.partial(heating_kernel, groups, rows, cols, polar_count),
                [(rows, cols), flat],
                (stellar_flux, gathered, dens, mat, flux_lanes),
                [sspec()] + [vspec()] * 4,
                name="heating",
            )
        r, q, out, *more = call(
            functools.partial(next_kernel, groups, rows, count, turn, last),
            [big, big, line] + ([] if last else [big, flat]) + ([flat] if first else []),
            (weights, c1, c2, a, b, fr, fp, r, q, t, fixed, capacity, mat, *sums),
            [sspec()] + [vspec()] * (12 + count),
            scratch=[vmem(flat), vmem((4 * pairs, LANES))],
            name="next",
        )
        if not last:
            t, mat, *more = more
        if first:
            (capacity,) = more
    return (energy, mat, column)


def solution(mesh):
    return jax.shard_map(
        per_device,
        mesh=mesh,
        in_specs=(
            P("radius", "polar"),
            P("group", "radius", "polar"),
            P("group", "radius", "polar"),
            P("radius", "polar"),
            P("group"),
            P("radius"),
        ),
        out_specs=(P("group", "radius", "polar"), P("radius", "polar"), P("radius", "polar")),
        check_vma=False,
    )
```

```python
import functools
import jax
import jax.numpy as jnp
from jax import lax
from jax.experimental import pallas as pl
from jax.experimental.pallas import tpu as pltpu
from jax.sharding import PartitionSpec as P


ITERS = 3
HALO = 8
LANES = 128
HALF = LANES // 2
STEP = 64
VMEM_LIMIT = 12 * 1024 * 1024
HIGHEST = lax.Precision.HIGHEST
OUTSIDE = 1.6e38


def vspec():
    return pl.BlockSpec(memory_space=pltpu.VMEM)


def sspec():
    return pl.BlockSpec(memory_space=pltpu.SMEM)


def hspec():
    return pl.BlockSpec(memory_space=pltpu.HBM)


def call(kernel, outs, args, specs, scratch=(), flops=1000000, nbytes=1000000, name=None, limit=VMEM_LIMIT, aliases=None):
    return pl.pallas_call(
        kernel,
        out_shape=[jax.ShapeDtypeStruct(s, jnp.float32) for s in outs],
        in_specs=specs,
        out_specs=[vspec() for _ in outs],
        scratch_shapes=list(scratch),
        compiler_params=pltpu.CompilerParams(vmem_limit_bytes=limit),
        cost_estimate=pl.CostEstimate(flops=flops, bytes_accessed=nbytes, transcendentals=0),
        name=name,
        input_output_aliases=aliases or {},
    )(*args)


def lane_of(height=1):
    return lax.broadcasted_iota(jnp.int32, (height, LANES), 1)


def pieces(tall):
    cuts = [0, HALO]
    while cuts[-1] + STEP < tall - HALO:
        cuts.append(cuts[-1] + STEP)
    cuts += [tall - HALO, tall]
    return list(zip(cuts[:-1], cuts[1:]))


def partner(axis, inner, outer):
    even = lax.rem(lax.axis_index(axis), 2) == 0
    return even, jnp.where(even, inner, outer), jnp.where(even, outer, inner)


def pack_rows_kernel(groups, rows, flux_in, opacity, old, density, material, first, second, *scratch):
    even, lo_first, lo_second = partner("radius", rows - HALO, 0)
    flux, sems = scratch[-2:]
    sides = ((first, lo_first, even), (second, lo_second, jnp.logical_not(even)))
    copies = [pltpu.make_async_copy(flux_in, flux, sems.at[8])]
    for side, (_, lo, at_end) in enumerate(sides):
        op_buf, old_buf, dens_buf, mat_buf = scratch[4 * side : 4 * side + 4]
        lo = pl.multiple_of(lo, HALO)
        base = pl.multiple_of(jnp.where(at_end, rows - 2 * HALO, 0), 2 * HALO)
        moves = (
            (opacity.at[:, pl.ds(base, 2 * HALO), :], op_buf),
            (old.at[:, pl.ds(lo, HALO), :], old_buf),
            (density.at[pl.ds(lo, HALO), :], dens_buf),
            (material.at[pl.ds(lo, HALO), :], mat_buf),
        )
        for k, (src, dst) in enumerate(moves):
            copies.append(pltpu.make_async_copy(src, dst, sems.at[4 * side + k]))
    for c in copies:
        c.start()
    for c in copies:
        c.wait()
    lane = lane_of(HALO) % HALF
    for side, (out, lo, at_end) in enumerate(sides):
        op_buf, old_buf, dens_buf, mat_buf = scratch[4 * side : 4 * side + 4]
        dens = dens_buf[...]
        for g in range(groups):
            part = op_buf[g].astype(jnp.float32)
            out[g] = jnp.where(at_end, part[HALO:], part[:HALO]) * dens
            out[groups + g] = old_buf[g]
        out[2 * groups] = dens
        out[2 * groups + 1] = mat_buf[...]
        place = jnp.where(at_end, 0, rows + HALO)
        vec = jnp.zeros((HALO, LANES), jnp.float32)
        for i in range(HALO):
            vec = jnp.where(lane == place + i, flux[lo + i], vec)
        for at_lane in range(0, out.shape[2], LANES):
            out[2 * groups + 2, :, at_lane : at_lane + LANES] = vec


def turn_kernel(
    groups, rows, cols, opacity, old, density, material, got_second, got_first,
    a_ref, e_ref, dens_ref, mat_ref, flux_ref, to_first, to_second,
):
    pairs = groups // 2
    plane_of_flux = 2 * groups + 2
    flux_ref[...] = got_first[plane_of_flux, :, :LANES] + got_second[plane_of_flux, :, :LANES]
    even, _, _ = partner("radius", 0, 0)
    for lo in range(0, cols, LANES):
        hi = lo + LANES

        def tile(plane, own):
            one, two = got_first[plane, :, lo:hi], got_second[plane, :, lo:hi]
            return jnp.concatenate([jnp.where(even, two, one), own, jnp.where(even, one, two)], axis=0)

        d = tile(2 * groups, density[:, lo:hi])
        d = jnp.concatenate([d, d], axis=0).T
        m = tile(2 * groups + 1, material[:, lo:hi])
        m = jnp.concatenate([m, m], axis=0).T
        dens_ref[HALO + lo : HALO + hi, :] = d
        mat_ref[HALO + lo : HALO + hi, :] = m

        def one(p, carry):
            both = []
            for h in range(2):
                g = 2 * p + h
                both.append(tile(g, opacity[g, :, lo:hi].astype(jnp.float32) * density[:, lo:hi]))
            a = jnp.concatenate(both, axis=0).T
            a_ref[p, HALO + lo : HALO + hi, :] = jnp.where(dens_ref[HALO + lo : HALO + hi, :] > 0.0, a, 1.0)
            both = [tile(groups + 2 * p + h, old[2 * p + h, :, lo:hi]) for h in range(2)]
            e_ref[p, HALO + lo : HALO + hi, :] = jnp.concatenate(both, axis=0).T
            return carry

        lax.fori_loop(0, pairs, one, 0, unroll=8)
    _, lo_first, lo_second = partner("polar", cols, HALO)
    for out, lo in ((to_first, lo_first), (to_second, lo_second)):
        edge = pl.ds(pl.multiple_of(lo, HALO), HALO)
        for p in range(pairs):
            out[p] = a_ref[p, edge, :]
            out[pairs + p] = e_ref[p, edge, :]
        out[2 * pairs] = dens_ref[edge, :]
        out[2 * pairs + 1] = mat_ref[edge, :]


def next_row(v):
    return pltpu.roll(v, LANES - 1, 1)


def prev_row(v):
    return pltpu.roll(v, 1, 1)


def after(ref, lead, lo, hi, here, end):
    if hi < end:
        return ref[(*lead, slice(lo + 1, hi + 1), slice(None))]
    return pltpu.roll(here, hi - lo - 1, 0)


def before(ref, lead, lo, hi, here, begin):
    if lo > begin:
        return ref[(*lead, slice(lo - 1, hi - 1), slice(None))]
    return pltpu.roll(here, 1, 0)


def at(lo, hi):
    return (slice(lo, hi), slice(None))


def flux_sum(p, lo, hi, v_ref, v, fr_ref, fp_ref, span):
    begin, end = span
    fp = fp_ref[(p, *at(lo, hi))]
    fp_before = before(fp_ref, (p,), lo, hi, fp, begin)
    polar = fp * (v - after(v_ref, (p,), lo, hi, v, end)) + fp_before * (
        v - before(v_ref, (p,), lo, hi, v, begin)
    )
    fr = fr_ref[(p, *at(lo, hi))] * (v - next_row(v))
    return polar + (fr - prev_row(fr))


def tile_sum(v):
    acc = v[:HALO]
    for lo in range(HALO, v.shape[0], HALO):
        acc = acc + v[lo : lo + HALO]
    return acc


def krylov(p, pairs, parts, span, own, b_ref, fr_ref, fp_ref, r_ref, q_ref, t_ref, mom, old_mom=None):
    sums = [jnp.zeros((HALO, LANES), jnp.float32) for _ in range(4)]
    for lo, hi in parts:
        r = r_ref[(p, *at(lo, hi))]
        q = b_ref[(p, *at(lo, hi))] * r + flux_sum(p, lo, hi, r_ref, r, fr_ref, fp_ref, span)
        q_ref[(p, *at(lo, hi))] = q
        if lo >= own[0] and hi <= own[1]:
            sums[0] = sums[0] + tile_sum(r * r)
            sums[1] = sums[1] + tile_sum(r * q)
            sums[2] = sums[2] + tile_sum(q * q)
    for lo, hi in parts:
        inside = lo >= own[0] and hi <= own[1]
        if not inside and t_ref is None:
            continue
        q = q_ref[(p, *at(lo, hi))]
        t = b_ref[(p, *at(lo, hi))] * q + flux_sum(p, lo, hi, q_ref, q, fr_ref, fp_ref, span)
        if t_ref is not None:
            t_ref[(p, *at(lo, hi))] = t
        if inside:
            sums[3] = sums[3] + tile_sum(q * t)
    for k in range(4):
        total = jnp.sum(sums[k], axis=0, keepdims=True)
        if old_mom is not None:
            total = total + old_mom[pl.ds(k * pairs + p, 1), :]
        mom[pl.ds(k * pairs + p, 1), :] = total


def send_moments(pairs, rows, mom, out, row_sums):
    lane = lane_of(4 * pairs)
    x = mom[...]
    first = jnp.where((lane >= HALO) & (lane < HALO + rows), x, 0.0)
    second = jnp.where((lane >= HALF + HALO) & (lane < HALF + HALO + rows), x, 0.0)
    both = jnp.concatenate([first, second, jnp.zeros((LANES - 8 * pairs, LANES), jnp.float32)], axis=0)
    line = lax.dot_general(
        jnp.ones((HALO, LANES), jnp.float32), both, (((1,), (1,)), ((), ())),
        precision=HIGHEST, preferred_element_type=jnp.float32,
    )
    if row_sums is not None:
        line = jnp.where(lane_of(HALO) < HALF, line, row_sums)
    for lo in range(0, out.shape[0], HALO):
        out[lo : lo + HALO, :] = line


def weight_of(weights, p):
    return jnp.where(lane_of(HALO) < HALF, weights[2 * p], weights[2 * p + 1])[:1]


def fold(s):
    s = s + pltpu.roll(s, HALF, 1)
    middle = s.shape[0] // 2
    return jnp.where(lane_of(middle) < HALF, s[:middle], s[middle:])


def unfold(s):
    other = pltpu.roll(s, HALF, 1)
    low = lane_of(s.shape[0]) < HALF
    return jnp.where(low, s, other), jnp.where(low, other, s)


def first_residual(p, w, inverse_parts, parts, span, dens_ref, mat_ref, a_ref, e_ref, fr_ref, fp_ref, r_ref, inv):
    begin, end = span
    for lo, hi in inverse_parts:
        a, e = a_ref[(p, *at(lo, hi))], e_ref[(p, *at(lo, hi))]
        slope_r = next_row(e) - prev_row(e)
        slope_p = after(e_ref, (p,), lo, hi, e, end) - before(e_ref, (p,), lo, hi, e, begin)
        n2 = slope_r * slope_r + slope_p * slope_p
        u = a * e
        s = 4.0 * u + n2 * lax.rsqrt(n2 + 1e-37)
        inv[lo:hi, :] = jnp.where(dens_ref[lo:hi, :] > 0.0, (n2 + 6.0 * u * s) / (e * s), OUTSIDE)
    for lo, hi in parts:
        d = inv[lo:hi, :]
        fr_ref[(p, *at(lo, hi))] = 4.0 / (d + next_row(d))
        fp_ref[(p, *at(lo, hi))] = 4.0 / (d + after(inv, (), lo, hi, d, end))
    for lo, hi in parts:
        a, e = a_ref[(p, *at(lo, hi))], e_ref[(p, *at(lo, hi))]
        r_ref[(p, *at(lo, hi))] = a * (w * mat_ref[lo:hi, :] - e) - flux_sum(
            p, lo, hi, e_ref, e, fr_ref, fp_ref, span
        )


def inner_kernel(
    groups, cols, weights, a_ref, e_ref, dens_ref, mat_ref,
    fr_ref, fp_ref, r_ref, q_ref, t_ref, b_ref, mom, inv,
):
    pairs = groups // 2
    span = (HALO, HALO + cols)
    parts = [(lo + HALO, hi + HALO) for lo, hi in pieces(cols)]
    own = (2 * HALO, cols)

    def one(p, carry):
        w = weight_of(weights, p)
        for lo, hi in parts:
            b_ref[(p, *at(lo, hi))] = 1.0 + a_ref[(p, *at(lo, hi))]
        first_residual(p, w, parts, parts, span, dens_ref, mat_ref, a_ref, e_ref, fr_ref, fp_ref, r_ref, inv)
        krylov(p, pairs, parts, span, own, b_ref, fr_ref, fp_ref, r_ref, q_ref, t_ref, mom)
        return carry

    lax.fori_loop(0, pairs, one, 0, unroll=2)


def frame_kernel(groups, rows, cols, weights, got_first, got_second, old_mom, *rest):
    a_ref, e_ref, fr_ref, fp_ref, r_ref, q_ref, t_ref, b_ref, dens_ref, mat_ref = rest[10:20]
    out, inv, mom = rest[20:]
    pairs = groups // 2
    tall = cols + 2 * HALO
    span = (0, tall)
    even, _, _ = partner("polar", 0, 0)
    ends = ((0, HALO), (tall - HALO, tall))

    def halo(side, plane):
        one, two = got_first[plane], got_second[plane]
        return jnp.where(even, two, one) if side == 0 else jnp.where(even, one, two)

    for side, (lo, hi) in enumerate(ends):
        dens_ref[lo:hi, :] = halo(side, 2 * pairs)
        mat_ref[lo:hi, :] = halo(side, 2 * pairs + 1)
    parts = [(0, HALO), (HALO, 2 * HALO), (cols, cols + HALO), (cols + HALO, tall)]
    inverse_parts = parts[:2] + [(2 * HALO, 3 * HALO)] + parts[2:]

    def one(p, carry):
        w = weight_of(weights, p)
        for side, (lo, hi) in enumerate(ends):
            a = jnp.where(dens_ref[lo:hi, :] > 0.0, halo(side, p), 1.0)
            a_ref[(p, *at(lo, hi))] = a
            b_ref[(p, *at(lo, hi))] = 1.0 + a
            e_ref[(p, *at(lo, hi))] = halo(side, pairs + p)
        first_residual(
            p, w, inverse_parts, parts, span, dens_ref, mat_ref, a_ref, e_ref, fr_ref, fp_ref, r_ref, inv
        )
        krylov(
            p, pairs, parts, span, (HALO, HALO + cols), b_ref, fr_ref, fp_ref, r_ref, q_ref, t_ref, mom, old_mom
        )
        return carry

    lax.fori_loop(0, pairs, one, 0, unroll=8)
    row_sums = jnp.sum(tile_sum(dens_ref[HALO : HALO + cols, :]), axis=0, keepdims=True)
    send_moments(pairs, rows, mom, out, row_sums)


def steps(pairs, gathered):
    total = jnp.sum(gathered[...], axis=0, keepdims=True)
    lane = lane_of(pairs)
    sub = lax.broadcasted_iota(jnp.int32, (pairs, LANES), 0)

    def moment(k):
        first, second = (
            jnp.sum(jnp.where(lane == sub + (4 * h + k) * pairs, total, 0.0), axis=1, keepdims=True)
            for h in range(2)
        )
        return jnp.where(lane < HALF, first, second)

    m0, m1, m2, m3 = (moment(k) for k in range(4))
    k1, k2, k3 = m1 / m0, m2 / m0, m3 / m0
    first = 1.0 / k1
    det = jnp.maximum(k2 - k1 * k1, 0.0)
    beta = det / (k1 * k1)
    low = k1 * k3 - k2 * k2
    second = jnp.minimum(jnp.where(low > 0.0, k1 * det / low, 0.0), 1.0)
    return first + second * (1.0 + beta), first * second


def absorbed(pairs, c1, c2, a_ref, e_ref, r_ref, q_ref, e_out, s, weights=None, emit=None):
    tall = a_ref.shape[1]
    for lo, hi in pieces(tall):
        total = emitted = jnp.zeros((hi - lo, LANES), jnp.float32)
        for p in range(pairs):
            a = a_ref[(p, *at(lo, hi))]
            e = (
                e_ref[(p, *at(lo, hi))]
                + c1[p : p + 1, :] * r_ref[(p, *at(lo, hi))]
                - c2[p : p + 1, :] * q_ref[(p, *at(lo, hi))]
            )
            e_out[(p, *at(lo, hi))] = e
            total = total + a * e
            if emit is not None:
                emitted = emitted + a * weight_of(weights, p)
        s[lo:hi, :] = total
        if emit is not None:
            emit[lo:hi, :] = emitted


def update_kernel(pairs, first, weights, gathered, a_ref, e_ref, r_ref, q_ref, e_out, s_out, c1_ref, c2_ref, s, emit):
    c1, c2 = steps(pairs, gathered)
    c1_ref[...] = c1
    c2_ref[...] = c2
    if first:
        absorbed(pairs, c1, c2, a_ref, e_ref, r_ref, q_ref, e_out, s, weights, emit)
        s_out[1] = fold(emit[...])
    else:
        absorbed(pairs, c1, c2, a_ref, e_ref, r_ref, q_ref, e_out, s)
    s_out[0] = fold(s[...])


def turned_back(v, rows):
    parts = [v[lo : lo + LANES].T[HALO : HALO + rows] for lo in range(0, v.shape[0], LANES)]
    return jnp.concatenate(parts, axis=1)


def last_update_kernel(pairs, rows, cols, gathered, a_ref, e_ref, r_ref, q_ref, e_out, s_out, s):
    c1, c2 = steps(pairs, gathered)
    absorbed(pairs, c1, c2, a_ref, e_ref, r_ref, q_ref, e_out, s)
    total = s[HALO : HALO + cols, :]
    s_out[...] = turned_back(total + pltpu.roll(total, HALF, 1), rows)


def energy_kernel(pairs, rows, cols, e_ref, fixed, capacity, out, fixed_out, capacity_out):
    def one(p, carry):
        for lo in range(0, cols, LANES):
            block = e_ref[p, HALO + lo : HALO + lo + LANES, :].T
            out[2 * p, :, lo : lo + LANES] = block[HALO : HALO + rows]
            out[2 * p + 1, :, lo : lo + LANES] = block[HALF + HALO : HALF + HALO + rows]
        return carry

    lax.fori_loop(0, pairs, one, 0, unroll=4)
    fixed_out[...] = turned_back(fixed[HALO : HALO + cols, :], rows)
    capacity_out[...] = turned_back(capacity[HALO : HALO + cols, :], rows)


def heating_kernel(
    groups, rows, cols, polar_count, flux, gathered, dens_ref, mat_ref, flux_ref, column_out, fixed_out
):
    tall = dens_ref.shape[0]
    radius, polar = lax.axis_index("radius"), lax.axis_index("polar")
    dens = dens_ref[...]
    row_id = lax.broadcasted_iota(jnp.int32, gathered.shape, 0)
    ahead = (row_id >= radius * polar_count) & (row_id < radius * polar_count + polar)
    carried = jnp.sum(jnp.where(ahead, gathered[...], 0.0), axis=0, keepdims=True)
    lane = lane_of()
    carried = jnp.where(lane < HALF, pltpu.roll(carried, HALF, 1), carried)
    dst = lax.broadcasted_iota(jnp.int32, (tall, tall), 0)
    src = lax.broadcasted_iota(jnp.int32, (tall, tall), 1)
    coeff = jnp.where(
        (src >= HALO) & (src <= dst), 1.0, jnp.where((src < HALO) & (src > dst), -1.0, 0.0)
    )
    within = lax.dot_general(
        coeff, dens, (((1,), (0,)), ((), ())), precision=HIGHEST, preferred_element_type=jnp.float32
    )
    column = 2.0 / (cols * polar_count) * (carried + within)
    vec = flux_ref[0:1, :]
    for i in range(rows):
        vec = jnp.where(lane % HALF == HALO + i, flux[i], vec)
    fixed_out[...] = 16.0 * dens * mat_ref[...] + vec * dens * jnp.exp(-column)
    column_out[...] = turned_back(column[HALO : HALO + cols], rows)


def summed(refs, lead=()):
    total = refs[0][(*lead, ...)]
    for s in refs[1:]:
        total = total + s[(*lead, ...)]
    return total


def next_kernel(groups, rows, count, turn, last, weights, c1_ref, c2_ref, a_ref, b_ref, fr_ref, fp_ref, r_in, q_in, t_in, fixed, cap_in, mat_ref, *rest):
    pairs = groups // 2
    sums = rest[:count]
    rest = rest[count:]
    outs, (delta, mom) = rest[:-2], rest[-2:]
    r_ref, q_ref, out, *outs = outs
    t_ref = None if last else outs.pop(0)
    m_ref = None if last else outs.pop(0)
    tall = fixed.shape[0]
    parts = pieces(tall)
    half = tall // 2
    folded = summed(sums, (0,))
    if turn == 0:
        cap_out = outs.pop(0)
        dens = cap_in[...]
        emits = jnp.concatenate(unfold(summed(sums, (1,))), axis=0)
        cap_out[...] = 16.0 * jnp.where(dens > 0.0, dens, 1.0) + emits
        cap_in = cap_out
    for k, total in enumerate(unfold(folded)):
        here = at(k * half, (k + 1) * half)
        nxt = (fixed[here] + total) / cap_in[here]
        delta[here] = nxt - mat_ref[here]
        if m_ref is not None:
            m_ref[here] = nxt

    def one(p, carry):
        w = weight_of(weights, p)
        c1 = c1_ref[pl.ds(p, 1), :]
        c2 = c2_ref[pl.ds(p, 1), :]
        for lo, hi in parts:
            here = (p, *at(lo, hi))
            r_ref[here] = (
                r_in[here] - c1 * q_in[here] + c2 * t_in[here] + a_ref[here] * (w * delta[lo:hi, :])
            )
        krylov(p, pairs, parts, (0, tall), (HALO, tall - HALO), b_ref, fr_ref, fp_ref, r_ref, q_ref, t_ref, mom)
        return carry

    lax.fori_loop(0, pairs, one, 0, unroll=2)
    send_moments(pairs, rows, mom, out, None)


def material_kernel(fixed, capacity, *rest):
    sums, out = rest[:-1], rest[-1]
    out[...] = (fixed[...] + summed(sums)) / capacity[...]


def spread(part, axis):
    count = lax.axis_size(axis)
    return [part] + [lax.ppermute(part, axis, [(i, i ^ s) for i in range(count)]) for s in range(1, count)]


def pair_up(first, axis):
    return lax.ppermute(first, axis, [(i, i ^ 1) for i in range(lax.axis_size(axis))])


def pair_across(second, axis):
    links = [(i, i + 1) for i in range(1, lax.axis_size(axis) - 1, 2)]
    return lax.ppermute(second, axis, links + [(j, i) for i, j in links])


def per_device(density, opacity, radiation_old, material_old, weights, stellar_flux):
    groups, rows, cols = opacity.shape
    pairs, tall = groups // 2, cols + 2 * HALO
    assert rows + 2 * HALO == HALF
    polar_count = lax.axis_size("polar")
    count = lax.axis_size("group")
    devices = lax.axis_size("radius") * polar_count
    planes = 2 * groups + 3
    big, flat, core = (pairs, tall, LANES), (tall, LANES), (cols, LANES)
    line = (devices, LANES)
    edge = (2 * pairs + 2, HALO, LANES)
    vmem = lambda shape: pltpu.VMEM(shape, jnp.float32)

    strips = [
        pltpu.VMEM((groups, 2 * HALO, cols), jnp.bfloat16),
        vmem((groups, HALO, cols)),
        vmem((HALO, cols)),
        vmem((HALO, cols)),
    ]
    first, second = call(
        functools.partial(pack_rows_kernel, groups, rows),
        [(planes, HALO, cols)] * 2,
        tuple(
            pltpu.with_memory_space_constraint(v, pltpu.HBM)
            for v in (stellar_flux, opacity, radiation_old, density, material_old)
        ),
        [hspec()] * 5,
        scratch=strips * 2 + [pltpu.SMEM((rows,), jnp.float32), pltpu.SemaphoreType.DMA((9,))],
        name="pack_rows",
        limit=20 * 1024 * 1024,
    )
    second = pair_across(second, "radius")
    first = pair_up(first, "radius")
    a, e, dens, mat, flux_lanes, first, second = call(
        functools.partial(turn_kernel, groups, rows, cols),
        [big] * 2 + [flat, flat, (HALO, LANES), edge, edge],
        (opacity, radiation_old, density, material_old, second, first),
        [vspec()] * 6,
        name="turn",
    )
    first, second = pair_up(first, "polar"), pair_across(second, "polar")
    fr, fp, r, q, t, b, mom = call(
        functools.partial(inner_kernel, groups, cols),
        [big] * 6 + [(4 * pairs, LANES)],
        (weights, a, e, dens, mat),
        [sspec()] + [vspec()] * 4,
        scratch=[vmem(flat)],
        name="inner",
    )
    a, e, fr, fp, r, q, t, b, dens, mat, out = call(
        functools.partial(frame_kernel, groups, rows, cols),
        [big] * 8 + [flat, flat, line],
        (weights, first, second, mom, a, e, fr, fp, r, q, t, b, dens, mat),
        [sspec()] + [vspec()] * 13,
        scratch=[vmem(flat), vmem((4 * pairs, LANES))],
        name="frame",
        aliases={4 + k: k for k in range(10)},
    )
    capacity = dens
    for turn in range(ITERS):
        gathered = lax.all_to_all(out, ("radius", "polar"), 0, 0, tiled=True)
        if turn + 1 == ITERS:
            e, part = call(
                functools.partial(last_update_kernel, pairs, rows, cols),
                [big, (rows, cols)],
                (gathered, a, e, r, q),
                [vspec()] * 5,
                scratch=[vmem(flat)],
                name="last_update",
            )
            sums = spread(part, "group")
            energy, fixed, capacity = call(
                functools.partial(energy_kernel, pairs, rows, cols),
                [(groups, rows, cols), (rows, cols), (rows, cols)],
                (e, fixed, capacity),
                [vspec()] * 3,
                name="energy",
            )
            (mat,) = call(
                material_kernel,
                [(rows, cols)],
                (fixed, capacity, *sums),
                [vspec()] * (2 + count),
                name="material",
            )
            break
        first, last = turn == 0, turn + 2 == ITERS
        e, part, c1, c2 = call(
            functools.partial(update_kernel, pairs, first),
            [big, (2 if first else 1, tall // 2, LANES), (pairs, LANES), (pairs, LANES)],
            (weights, gathered, a, e, r, q),
            [sspec()] + [vspec()] * 5,
            scratch=[vmem(flat)] * 2,
            name="update",
        )
        sums = spread(part, "group")
        if first:
            column, fixed = call(
                functools.partial(heating_kernel, groups, rows, cols, polar_count),
                [(rows, cols), flat],
                (stellar_flux, gathered, dens, mat, flux_lanes),
                [sspec()] + [vspec()] * 4,
                name="heating",
            )
        r, q, out, *more = call(
            functools.partial(next_kernel, groups, rows, count, turn, last),
            [big, big, line] + ([] if last else [big, flat]) + ([flat] if first else []),
            (weights, c1, c2, a, b, fr, fp, r, q, t, fixed, capacity, mat, *sums),
            [sspec()] + [vspec()] * (12 + count),
            scratch=[vmem(flat), vmem((4 * pairs, LANES))],
            name="next",
        )
        if not last:
            t, mat, *more = more
        if first:
            (capacity,) = more
    return (energy, mat, column)


def solution(mesh):
    return jax.shard_map(
        per_device,
        mesh=mesh,
        in_specs=(
            P("radius", "polar"),
            P("group", "radius", "polar"),
            P("group", "radius", "polar"),
            P("radius", "polar"),
            P("group"),
            P("radius"),
        ),
        out_specs=(P("group", "radius", "polar"), P("radius", "polar"), P("radius", "polar")),
        check_vma=False,
    )
```

```python
import functools
import jax
import jax.numpy as jnp
from jax import lax
from jax.experimental import pallas as pl
from jax.experimental.pallas import tpu as pltpu
from jax.sharding import PartitionSpec as P


ITERS = 3
HALO = 8
LANES = 128
HALF = LANES // 2
STEP = 64
VMEM_LIMIT = 12 * 1024 * 1024
HIGHEST = lax.Precision.HIGHEST
OUTSIDE = 1.6e38


def vspec():
    return pl.BlockSpec(memory_space=pltpu.VMEM)


def sspec():
    return pl.BlockSpec(memory_space=pltpu.SMEM)


def hspec():
    return pl.BlockSpec(memory_space=pltpu.HBM)


def call(kernel, outs, args, specs, scratch=(), flops=1000000, nbytes=1000000, name=None, limit=VMEM_LIMIT, aliases=None):
    return pl.pallas_call(
        kernel,
        out_shape=[jax.ShapeDtypeStruct(s, jnp.float32) for s in outs],
        in_specs=specs,
        out_specs=[vspec() for _ in outs],
        scratch_shapes=list(scratch),
        compiler_params=pltpu.CompilerParams(vmem_limit_bytes=limit),
        cost_estimate=pl.CostEstimate(flops=flops, bytes_accessed=nbytes, transcendentals=0),
        name=name,
        input_output_aliases=aliases or {},
    )(*args)


def lane_of(height=1):
    return lax.broadcasted_iota(jnp.int32, (height, LANES), 1)


def pieces(tall):
    cuts = [0, HALO]
    while cuts[-1] + STEP < tall - HALO:
        cuts.append(cuts[-1] + STEP)
    cuts += [tall - HALO, tall]
    return list(zip(cuts[:-1], cuts[1:]))


def partner(axis, inner, outer):
    even = lax.rem(lax.axis_index(axis), 2) == 0
    return even, jnp.where(even, inner, outer), jnp.where(even, outer, inner)


def pack_rows_kernel(
    groups, rows, weights_in, flux_in, opacity, old, density, material, first, second, weight_lanes, *scratch
):
    even, lo_first, lo_second = partner("radius", rows - HALO, 0)
    weights, flux, sems = scratch[-3:]
    sides = ((first, lo_first, even), (second, lo_second, jnp.logical_not(even)))
    copies = [
        pltpu.make_async_copy(flux_in, flux, sems.at[8]),
        pltpu.make_async_copy(weights_in, weights, sems.at[9]),
    ]
    for side, (_, lo, at_end) in enumerate(sides):
        op_buf, old_buf, dens_buf, mat_buf = scratch[4 * side : 4 * side + 4]
        lo = pl.multiple_of(lo, HALO)
        base = pl.multiple_of(jnp.where(at_end, rows - 2 * HALO, 0), 2 * HALO)
        moves = (
            (opacity.at[:, pl.ds(base, 2 * HALO), :], op_buf),
            (old.at[:, pl.ds(lo, HALO), :], old_buf),
            (density.at[pl.ds(lo, HALO), :], dens_buf),
            (material.at[pl.ds(lo, HALO), :], mat_buf),
        )
        for k, (src, dst) in enumerate(moves):
            copies.append(pltpu.make_async_copy(src, dst, sems.at[4 * side + k]))
    for c in copies:
        c.start()
    for c in copies:
        c.wait()
    half = lane_of() < HALF
    for p in range(groups // 2):
        weight_lanes[p : p + 1, :] = jnp.where(half, weights[2 * p], weights[2 * p + 1])
    lane = lane_of(HALO) % HALF
    for side, (out, lo, at_end) in enumerate(sides):
        op_buf, old_buf, dens_buf, mat_buf = scratch[4 * side : 4 * side + 4]
        dens = dens_buf[...]
        for g in range(groups):
            part = op_buf[g].astype(jnp.float32)
            out[g] = jnp.where(at_end, part[HALO:], part[:HALO]) * dens
            out[groups + g] = old_buf[g]
        out[2 * groups] = dens
        out[2 * groups + 1] = mat_buf[...]
        place = jnp.where(at_end, 0, rows + HALO)
        vec = jnp.zeros((HALO, LANES), jnp.float32)
        for i in range(HALO):
            vec = jnp.where(lane == place + i, flux[lo + i], vec)
        for at_lane in range(0, out.shape[2], LANES):
            out[2 * groups + 2, :, at_lane : at_lane + LANES] = vec


def turn_kernel(
    groups, rows, cols, opacity, old, density, material, got_second, got_first,
    a_ref, e_ref, dens_ref, mat_ref, flux_ref, to_first, to_second,
):
    pairs = groups // 2
    plane_of_flux = 2 * groups + 2
    flux_ref[...] = got_first[plane_of_flux, :, :LANES] + got_second[plane_of_flux, :, :LANES]
    even, _, _ = partner("radius", 0, 0)
    for lo in range(0, cols, LANES):
        hi = lo + LANES

        def tile(plane, own):
            one, two = got_first[plane, :, lo:hi], got_second[plane, :, lo:hi]
            return jnp.concatenate([jnp.where(even, two, one), own, jnp.where(even, one, two)], axis=0)

        d = tile(2 * groups, density[:, lo:hi])
        d = jnp.concatenate([d, d], axis=0).T
        m = tile(2 * groups + 1, material[:, lo:hi])
        m = jnp.concatenate([m, m], axis=0).T
        dens_ref[HALO + lo : HALO + hi, :] = d
        mat_ref[HALO + lo : HALO + hi, :] = m

        def one(p, carry):
            both = []
            for h in range(2):
                g = 2 * p + h
                both.append(tile(g, opacity[g, :, lo:hi].astype(jnp.float32) * density[:, lo:hi]))
            a = jnp.concatenate(both, axis=0).T
            a_ref[p, HALO + lo : HALO + hi, :] = jnp.where(dens_ref[HALO + lo : HALO + hi, :] > 0.0, a, 1.0)
            both = [tile(groups + 2 * p + h, old[2 * p + h, :, lo:hi]) for h in range(2)]
            e_ref[p, HALO + lo : HALO + hi, :] = jnp.concatenate(both, axis=0).T
            return carry

        lax.fori_loop(0, pairs, one, 0, unroll=8)
    _, lo_first, lo_second = partner("polar", cols, HALO)
    for out, lo in ((to_first, lo_first), (to_second, lo_second)):
        edge = pl.ds(pl.multiple_of(lo, HALO), HALO)
        for p in range(pairs):
            out[p] = a_ref[p, edge, :]
            out[pairs + p] = e_ref[p, edge, :]
        out[2 * pairs] = dens_ref[edge, :]
        out[2 * pairs + 1] = mat_ref[edge, :]


def next_row(v):
    return pltpu.roll(v, LANES - 1, 1)


def prev_row(v):
    return pltpu.roll(v, 1, 1)


def after(ref, lead, lo, hi, here, end):
    if hi < end:
        return ref[(*lead, slice(lo + 1, hi + 1), slice(None))]
    return pltpu.roll(here, hi - lo - 1, 0)


def before(ref, lead, lo, hi, here, begin):
    if lo > begin:
        return ref[(*lead, slice(lo - 1, hi - 1), slice(None))]
    return pltpu.roll(here, 1, 0)


def at(lo, hi):
    return (slice(lo, hi), slice(None))


def flux_sum(p, lo, hi, v_ref, v, fr_ref, fp_ref, span):
    begin, end = span
    fp = fp_ref[(p, *at(lo, hi))]
    fp_before = before(fp_ref, (p,), lo, hi, fp, begin)
    polar = fp * (v - after(v_ref, (p,), lo, hi, v, end)) + fp_before * (
        v - before(v_ref, (p,), lo, hi, v, begin)
    )
    fr = fr_ref[(p, *at(lo, hi))] * (v - next_row(v))
    return polar + (fr - prev_row(fr))


def tile_sum(v):
    acc = v[:HALO]
    for lo in range(HALO, v.shape[0], HALO):
        acc = acc + v[lo : lo + HALO]
    return acc


def krylov(p, pairs, parts, span, own, b_ref, fr_ref, fp_ref, r_ref, q_ref, t_ref, mom, old_mom=None):
    sums = [jnp.zeros((HALO, LANES), jnp.float32) for _ in range(4)]
    for lo, hi in parts:
        r = r_ref[(p, *at(lo, hi))]
        q = b_ref[(p, *at(lo, hi))] * r + flux_sum(p, lo, hi, r_ref, r, fr_ref, fp_ref, span)
        q_ref[(p, *at(lo, hi))] = q
        if lo >= own[0] and hi <= own[1]:
            sums[0] = sums[0] + tile_sum(r * r)
            sums[1] = sums[1] + tile_sum(r * q)
            sums[2] = sums[2] + tile_sum(q * q)
    for lo, hi in parts:
        inside = lo >= own[0] and hi <= own[1]
        if not inside and t_ref is None:
            continue
        q = q_ref[(p, *at(lo, hi))]
        t = b_ref[(p, *at(lo, hi))] * q + flux_sum(p, lo, hi, q_ref, q, fr_ref, fp_ref, span)
        if t_ref is not None:
            t_ref[(p, *at(lo, hi))] = t
        if inside:
            sums[3] = sums[3] + tile_sum(q * t)
    for k in range(4):
        total = jnp.sum(sums[k], axis=0, keepdims=True)
        if old_mom is not None:
            total = total + old_mom[pl.ds(k * pairs + p, 1), :]
        mom[pl.ds(k * pairs + p, 1), :] = total


def send_moments(pairs, rows, mom, out, row_sums):
    lane = lane_of(4 * pairs)
    x = mom[...]
    first = jnp.where((lane >= HALO) & (lane < HALO + rows), x, 0.0)
    second = jnp.where((lane >= HALF + HALO) & (lane < HALF + HALO + rows), x, 0.0)
    both = jnp.concatenate([first, second, jnp.zeros((LANES - 8 * pairs, LANES), jnp.float32)], axis=0)
    line = lax.dot_general(
        jnp.ones((HALO, LANES), jnp.float32), both, (((1,), (1,)), ((), ())),
        precision=HIGHEST, preferred_element_type=jnp.float32,
    )
    if row_sums is not None:
        line = jnp.where(lane_of(HALO) < HALF, line, row_sums)
    for lo in range(0, out.shape[0], HALO):
        out[lo : lo + HALO, :] = line


def weight_of(weights, p):
    return weights[pl.ds(p, 1), :]


def fold(s):
    s = s + pltpu.roll(s, HALF, 1)
    middle = s.shape[0] // 2
    return jnp.where(lane_of(middle) < HALF, s[:middle], s[middle:])


def unfold(s):
    other = pltpu.roll(s, HALF, 1)
    low = lane_of(s.shape[0]) < HALF
    return jnp.where(low, s, other), jnp.where(low, other, s)


def first_residual(p, w, inverse_parts, parts, span, dens_ref, mat_ref, a_ref, e_ref, fr_ref, fp_ref, r_ref, inv):
    begin, end = span
    for lo, hi in inverse_parts:
        a, e = a_ref[(p, *at(lo, hi))], e_ref[(p, *at(lo, hi))]
        slope_r = next_row(e) - prev_row(e)
        slope_p = after(e_ref, (p,), lo, hi, e, end) - before(e_ref, (p,), lo, hi, e, begin)
        n2 = slope_r * slope_r + slope_p * slope_p
        u = a * e
        s = 4.0 * u + n2 * lax.rsqrt(n2 + 1e-37)
        inv[lo:hi, :] = jnp.where(dens_ref[lo:hi, :] > 0.0, (n2 + 6.0 * u * s) / (e * s), OUTSIDE)
    for lo, hi in parts:
        d = inv[lo:hi, :]
        fr_ref[(p, *at(lo, hi))] = 4.0 / (d + next_row(d))
        fp_ref[(p, *at(lo, hi))] = 4.0 / (d + after(inv, (), lo, hi, d, end))
    for lo, hi in parts:
        a, e = a_ref[(p, *at(lo, hi))], e_ref[(p, *at(lo, hi))]
        r_ref[(p, *at(lo, hi))] = a * (w * mat_ref[lo:hi, :] - e) - flux_sum(
            p, lo, hi, e_ref, e, fr_ref, fp_ref, span
        )


def inner_kernel(
    groups, cols, weights, a_ref, e_ref, dens_ref, mat_ref,
    fr_ref, fp_ref, r_ref, q_ref, t_ref, b_ref, mom, inv,
):
    pairs = groups // 2
    span = (HALO, HALO + cols)
    parts = [(lo + HALO, hi + HALO) for lo, hi in pieces(cols)]
    own = (2 * HALO, cols)

    def one(p, carry):
        w = weight_of(weights, p)
        for lo, hi in parts:
            b_ref[(p, *at(lo, hi))] = 1.0 + a_ref[(p, *at(lo, hi))]
        first_residual(p, w, parts, parts, span, dens_ref, mat_ref, a_ref, e_ref, fr_ref, fp_ref, r_ref, inv)
        krylov(p, pairs, parts, span, own, b_ref, fr_ref, fp_ref, r_ref, q_ref, t_ref, mom)
        return carry

    lax.fori_loop(0, pairs, one, 0, unroll=2)


def frame_kernel(groups, rows, cols, weights, got_first, got_second, old_mom, *rest):
    a_ref, e_ref, fr_ref, fp_ref, r_ref, q_ref, t_ref, b_ref, dens_ref, mat_ref = rest[10:20]
    out, inv, mom = rest[20:]
    pairs = groups // 2
    tall = cols + 2 * HALO
    span = (0, tall)
    even, _, _ = partner("polar", 0, 0)
    ends = ((0, HALO), (tall - HALO, tall))

    def halo(side, plane):
        one, two = got_first[plane], got_second[plane]
        return jnp.where(even, two, one) if side == 0 else jnp.where(even, one, two)

    for side, (lo, hi) in enumerate(ends):
        dens_ref[lo:hi, :] = halo(side, 2 * pairs)
        mat_ref[lo:hi, :] = halo(side, 2 * pairs + 1)
    parts = [(0, HALO), (HALO, 2 * HALO), (cols, cols + HALO), (cols + HALO, tall)]
    inverse_parts = parts[:2] + [(2 * HALO, 3 * HALO)] + parts[2:]

    def one(p, carry):
        w = weight_of(weights, p)
        for side, (lo, hi) in enumerate(ends):
            a = jnp.where(dens_ref[lo:hi, :] > 0.0, halo(side, p), 1.0)
            a_ref[(p, *at(lo, hi))] = a
            b_ref[(p, *at(lo, hi))] = 1.0 + a
            e_ref[(p, *at(lo, hi))] = halo(side, pairs + p)
        first_residual(
            p, w, inverse_parts, parts, span, dens_ref, mat_ref, a_ref, e_ref, fr_ref, fp_ref, r_ref, inv
        )
        krylov(
            p, pairs, parts, span, (HALO, HALO + cols), b_ref, fr_ref, fp_ref, r_ref, q_ref, t_ref, mom, old_mom
        )
        return carry

    lax.fori_loop(0, pairs, one, 0, unroll=8)
    row_sums = jnp.sum(tile_sum(dens_ref[HALO : HALO + cols, :]), axis=0, keepdims=True)
    send_moments(pairs, rows, mom, out, row_sums)


def steps(pairs, gathered):
    total = jnp.sum(gathered[...], axis=0, keepdims=True)
    lane = lane_of(pairs)
    sub = lax.broadcasted_iota(jnp.int32, (pairs, LANES), 0)

    def moment(k):
        first, second = (
            jnp.sum(jnp.where(lane == sub + (4 * h + k) * pairs, total, 0.0), axis=1, keepdims=True)
            for h in range(2)
        )
        return jnp.where(lane < HALF, first, second)

    m0, m1, m2, m3 = (moment(k) for k in range(4))
    k1, k2, k3 = m1 / m0, m2 / m0, m3 / m0
    first = 1.0 / k1
    det = jnp.maximum(k2 - k1 * k1, 0.0)
    beta = det / (k1 * k1)
    low = k1 * k3 - k2 * k2
    second = jnp.minimum(jnp.where(low > 0.0, k1 * det / low, 0.0), 1.0)
    return first + second * (1.0 + beta), first * second


def absorbed(pairs, c1, c2, a_ref, e_ref, r_ref, q_ref, e_out, s, weights=None, emit=None):
    tall = a_ref.shape[1]
    for lo, hi in pieces(tall):
        total = emitted = jnp.zeros((hi - lo, LANES), jnp.float32)
        for p in range(pairs):
            a = a_ref[(p, *at(lo, hi))]
            e = (
                e_ref[(p, *at(lo, hi))]
                + c1[p : p + 1, :] * r_ref[(p, *at(lo, hi))]
                - c2[p : p + 1, :] * q_ref[(p, *at(lo, hi))]
            )
            e_out[(p, *at(lo, hi))] = e
            total = total + a * e
            if emit is not None:
                emitted = emitted + a * weight_of(weights, p)
        s[lo:hi, :] = total
        if emit is not None:
            emit[lo:hi, :] = emitted


def update_kernel(pairs, first, weights, gathered, a_ref, e_ref, r_ref, q_ref, e_out, s_out, c1_ref, c2_ref, s, emit):
    c1, c2 = steps(pairs, gathered)
    c1_ref[...] = c1
    c2_ref[...] = c2
    if first:
        absorbed(pairs, c1, c2, a_ref, e_ref, r_ref, q_ref, e_out, s, weights, emit)
        s_out[1] = fold(emit[...])
    else:
        absorbed(pairs, c1, c2, a_ref, e_ref, r_ref, q_ref, e_out, s)
    s_out[0] = fold(s[...])


def turned_back(v, rows):
    parts = [v[lo : lo + LANES].T[HALO : HALO + rows] for lo in range(0, v.shape[0], LANES)]
    return jnp.concatenate(parts, axis=1)


def last_update_kernel(pairs, rows, cols, gathered, a_ref, e_ref, r_ref, q_ref, e_out, s_out, s):
    c1, c2 = steps(pairs, gathered)
    absorbed(pairs, c1, c2, a_ref, e_ref, r_ref, q_ref, e_out, s)
    total = s[HALO : HALO + cols, :]
    s_out[...] = turned_back(total + pltpu.roll(total, HALF, 1), rows)


def energy_kernel(pairs, rows, cols, e_ref, fixed, capacity, out, fixed_out, capacity_out):
    def one(p, carry):
        for lo in range(0, cols, LANES):
            block = e_ref[p, HALO + lo : HALO + lo + LANES, :].T
            out[2 * p, :, lo : lo + LANES] = block[HALO : HALO + rows]
            out[2 * p + 1, :, lo : lo + LANES] = block[HALF + HALO : HALF + HALO + rows]
        return carry

    lax.fori_loop(0, pairs, one, 0, unroll=4)
    fixed_out[...] = turned_back(fixed[HALO : HALO + cols, :], rows)
    capacity_out[...] = turned_back(capacity[HALO : HALO + cols, :], rows)


def heating_kernel(
    groups, rows, cols, polar_count, flux, gathered, dens_ref, mat_ref, flux_ref, column_out, fixed_out
):
    tall = dens_ref.shape[0]
    radius, polar = lax.axis_index("radius"), lax.axis_index("polar")
    dens = dens_ref[...]
    row_id = lax.broadcasted_iota(jnp.int32, gathered.shape, 0)
    ahead = (row_id >= radius * polar_count) & (row_id < radius * polar_count + polar)
    carried = jnp.sum(jnp.where(ahead, gathered[...], 0.0), axis=0, keepdims=True)
    lane = lane_of()
    carried = jnp.where(lane < HALF, pltpu.roll(carried, HALF, 1), carried)
    dst = lax.broadcasted_iota(jnp.int32, (tall, tall), 0)
    src = lax.broadcasted_iota(jnp.int32, (tall, tall), 1)
    coeff = jnp.where(
        (src >= HALO) & (src <= dst), 1.0, jnp.where((src < HALO) & (src > dst), -1.0, 0.0)
    )
    within = lax.dot_general(
        coeff, dens, (((1,), (0,)), ((), ())), precision=HIGHEST, preferred_element_type=jnp.float32
    )
    column = 2.0 / (cols * polar_count) * (carried + within)
    vec = flux_ref[0:1, :]
    for i in range(rows):
        vec = jnp.where(lane % HALF == HALO + i, flux[i], vec)
    fixed_out[...] = 16.0 * dens * mat_ref[...] + vec * dens * jnp.exp(-column)
    column_out[...] = turned_back(column[HALO : HALO + cols], rows)


def summed(refs, lead=()):
    total = refs[0][(*lead, ...)]
    for s in refs[1:]:
        total = total + s[(*lead, ...)]
    return total


def next_kernel(groups, rows, count, turn, last, weights, c1_ref, c2_ref, a_ref, b_ref, fr_ref, fp_ref, r_in, q_in, t_in, fixed, cap_in, mat_ref, *rest):
    pairs = groups // 2
    sums = rest[:count]
    rest = rest[count:]
    outs, (delta, mom) = rest[:-2], rest[-2:]
    r_ref, q_ref, out, *outs = outs
    t_ref = None if last else outs.pop(0)
    m_ref = None if last else outs.pop(0)
    tall = fixed.shape[0]
    parts = pieces(tall)
    half = tall // 2
    folded = summed(sums, (0,))
    if turn == 0:
        cap_out = outs.pop(0)
        dens = cap_in[...]
        emits = jnp.concatenate(unfold(summed(sums, (1,))), axis=0)
        cap_out[...] = 16.0 * jnp.where(dens > 0.0, dens, 1.0) + emits
        cap_in = cap_out
    for k, total in enumerate(unfold(folded)):
        here = at(k * half, (k + 1) * half)
        nxt = (fixed[here] + total) / cap_in[here]
        delta[here] = nxt - mat_ref[here]
        if m_ref is not None:
            m_ref[here] = nxt

    def one(p, carry):
        w = weight_of(weights, p)
        c1 = c1_ref[pl.ds(p, 1), :]
        c2 = c2_ref[pl.ds(p, 1), :]
        for lo, hi in parts:
            here = (p, *at(lo, hi))
            r_ref[here] = (
                r_in[here] - c1 * q_in[here] + c2 * t_in[here] + a_ref[here] * (w * delta[lo:hi, :])
            )
        krylov(p, pairs, parts, (0, tall), (HALO, tall - HALO), b_ref, fr_ref, fp_ref, r_ref, q_ref, t_ref, mom)
        return carry

    lax.fori_loop(0, pairs, one, 0, unroll=2)
    send_moments(pairs, rows, mom, out, None)


def material_kernel(fixed, capacity, *rest):
    sums, out = rest[:-1], rest[-1]
    out[...] = (fixed[...] + summed(sums)) / capacity[...]


def spread(part, axis):
    count = lax.axis_size(axis)
    return [part] + [lax.ppermute(part, axis, [(i, i ^ s) for i in range(count)]) for s in range(1, count)]


def pair_up(first, axis):
    return lax.ppermute(first, axis, [(i, i ^ 1) for i in range(lax.axis_size(axis))])


def pair_across(second, axis):
    links = [(i, i + 1) for i in range(1, lax.axis_size(axis) - 1, 2)]
    return lax.ppermute(second, axis, links + [(j, i) for i, j in links])


def per_device(density, opacity, radiation_old, material_old, weights, stellar_flux):
    groups, rows, cols = opacity.shape
    pairs, tall = groups // 2, cols + 2 * HALO
    assert rows + 2 * HALO == HALF
    polar_count = lax.axis_size("polar")
    count = lax.axis_size("group")
    devices = lax.axis_size("radius") * polar_count
    planes = 2 * groups + 3
    big, flat, core = (pairs, tall, LANES), (tall, LANES), (cols, LANES)
    line = (devices, LANES)
    edge = (2 * pairs + 2, HALO, LANES)
    vmem = lambda shape: pltpu.VMEM(shape, jnp.float32)

    strips = [
        pltpu.VMEM((groups, 2 * HALO, cols), jnp.bfloat16),
        vmem((groups, HALO, cols)),
        vmem((HALO, cols)),
        vmem((HALO, cols)),
    ]
    first, second, weights = call(
        functools.partial(pack_rows_kernel, groups, rows),
        [(planes, HALO, cols)] * 2 + [(pairs, LANES)],
        tuple(
            pltpu.with_memory_space_constraint(v, pltpu.HBM)
            for v in (weights, stellar_flux, opacity, radiation_old, density, material_old)
        ),
        [hspec()] * 6,
        scratch=strips * 2
        + [pltpu.SMEM((size,), jnp.float32) for size in (groups, rows)]
        + [pltpu.SemaphoreType.DMA((10,))],
        name="pack_rows",
        limit=20 * 1024 * 1024,
    )
    second = pair_across(second, "radius")
    first = pair_up(first, "radius")
    a, e, dens, mat, flux_lanes, first, second = call(
        functools.partial(turn_kernel, groups, rows, cols),
        [big] * 2 + [flat, flat, (HALO, LANES), edge, edge],
        (opacity, radiation_old, density, material_old, second, first),
        [vspec()] * 6,
        name="turn",
    )
    first, second = pair_up(first, "polar"), pair_across(second, "polar")
    fr, fp, r, q, t, b, mom = call(
        functools.partial(inner_kernel, groups, cols),
        [big] * 6 + [(4 * pairs, LANES)],
        (weights, a, e, dens, mat),
        [vspec()] * 5,
        scratch=[vmem(flat)],
        name="inner",
    )
    a, e, fr, fp, r, q, t, b, dens, mat, out = call(
        functools.partial(frame_kernel, groups, rows, cols),
        [big] * 8 + [flat, flat, line],
        (weights, first, second, mom, a, e, fr, fp, r, q, t, b, dens, mat),
        [vspec()] * 14,
        scratch=[vmem(flat), vmem((4 * pairs, LANES))],
        name="frame",
        aliases={4 + k: k for k in range(10)},
    )
    capacity = dens
    for turn in range(ITERS):
        gathered = lax.all_to_all(out, ("radius", "polar"), 0, 0, tiled=True)
        if turn + 1 == ITERS:
            e, part = call(
                functools.partial(last_update_kernel, pairs, rows, cols),
                [big, (rows, cols)],
                (gathered, a, e, r, q),
                [vspec()] * 5,
                scratch=[vmem(flat)],
                name="last_update",
            )
            sums = spread(part, "group")
            energy, fixed, capacity = call(
                functools.partial(energy_kernel, pairs, rows, cols),
                [(groups, rows, cols), (rows, cols), (rows, cols)],
                (e, fixed, capacity),
                [vspec()] * 3,
                name="energy",
            )
            (mat,) = call(
                material_kernel,
                [(rows, cols)],
                (fixed, capacity, *sums),
                [vspec()] * (2 + count),
                name="material",
            )
            break
        first, last = turn == 0, turn + 2 == ITERS
        e, part, c1, c2 = call(
            functools.partial(update_kernel, pairs, first),
            [big, (2 if first else 1, tall // 2, LANES), (pairs, LANES), (pairs, LANES)],
            (weights, gathered, a, e, r, q),
            [vspec()] * 6,
            scratch=[vmem(flat)] * 2,
            name="update",
        )
        sums = spread(part, "group")
        if first:
            column, fixed = call(
                functools.partial(heating_kernel, groups, rows, cols, polar_count),
                [(rows, cols), flat],
                (stellar_flux, gathered, dens, mat, flux_lanes),
                [sspec()] + [vspec()] * 4,
                name="heating",
            )
        r, q, out, *more = call(
            functools.partial(next_kernel, groups, rows, count, turn, last),
            [big, big, line] + ([] if last else [big, flat]) + ([flat] if first else []),
            (weights, c1, c2, a, b, fr, fp, r, q, t, fixed, capacity, mat, *sums),
            [vspec()] * (13 + count),
            scratch=[vmem(flat), vmem((4 * pairs, LANES))],
            name="next",
        )
        if not last:
            t, mat, *more = more
        if first:
            (capacity,) = more
    return (energy, mat, column)


def solution(mesh):
    return jax.shard_map(
        per_device,
        mesh=mesh,
        in_specs=(
            P("radius", "polar"),
            P("group", "radius", "polar"),
            P("group", "radius", "polar"),
            P("radius", "polar"),
            P("group"),
            P("radius"),
        ),
        out_specs=(P("group", "radius", "polar"), P("radius", "polar"), P("radius", "polar")),
        check_vma=False,
    )
```

```python
import functools
import jax
import jax.numpy as jnp
from jax import lax
from jax.experimental import pallas as pl
from jax.experimental.pallas import tpu as pltpu
from jax.sharding import PartitionSpec as P


ITERS = 3
HALO = 8
LANES = 128
HALF = LANES // 2
STEP = 16
VMEM_LIMIT = 12 * 1024 * 1024
HIGHEST = lax.Precision.HIGHEST
OUTSIDE = 1.6e38


def vspec():
    return pl.BlockSpec(memory_space=pltpu.VMEM)


def sspec():
    return pl.BlockSpec(memory_space=pltpu.SMEM)


def hspec():
    return pl.BlockSpec(memory_space=pltpu.HBM)


def call(kernel, outs, args, specs, scratch=(), flops=1000000, nbytes=1000000, name=None, limit=VMEM_LIMIT, aliases=None):
    return pl.pallas_call(
        kernel,
        out_shape=[jax.ShapeDtypeStruct(s, jnp.float32) for s in outs],
        in_specs=specs,
        out_specs=[vspec() for _ in outs],
        scratch_shapes=list(scratch),
        compiler_params=pltpu.CompilerParams(vmem_limit_bytes=limit),
        cost_estimate=pl.CostEstimate(flops=flops, bytes_accessed=nbytes, transcendentals=0),
        name=name,
        input_output_aliases=aliases or {},
    )(*args)


def lane_of(height=1):
    return lax.broadcasted_iota(jnp.int32, (height, LANES), 1)


def pieces(tall):
    cuts = [0, HALO]
    while cuts[-1] + STEP < tall - HALO:
        cuts.append(cuts[-1] + STEP)
    cuts += [tall - HALO, tall]
    return list(zip(cuts[:-1], cuts[1:]))


def partner(axis, inner, outer):
    even = lax.rem(lax.axis_index(axis), 2) == 0
    return even, jnp.where(even, inner, outer), jnp.where(even, outer, inner)


def pack_rows_kernel(
    groups, rows, weights_in, flux_in, opacity, old, density, material, first, second, weight_lanes, *scratch
):
    even, lo_first, lo_second = partner("radius", rows - HALO, 0)
    weights, flux, sems = scratch[-3:]
    sides = ((first, lo_first, even), (second, lo_second, jnp.logical_not(even)))
    copies = [
        pltpu.make_async_copy(flux_in, flux, sems.at[8]),
        pltpu.make_async_copy(weights_in, weights, sems.at[9]),
    ]
    for side, (_, lo, at_end) in enumerate(sides):
        op_buf, old_buf, dens_buf, mat_buf = scratch[4 * side : 4 * side + 4]
        lo = pl.multiple_of(lo, HALO)
        base = pl.multiple_of(jnp.where(at_end, rows - 2 * HALO, 0), 2 * HALO)
        moves = (
            (opacity.at[:, pl.ds(base, 2 * HALO), :], op_buf),
            (old.at[:, pl.ds(lo, HALO), :], old_buf),
            (density.at[pl.ds(lo, HALO), :], dens_buf),
            (material.at[pl.ds(lo, HALO), :], mat_buf),
        )
        for k, (src, dst) in enumerate(moves):
            copies.append(pltpu.make_async_copy(src, dst, sems.at[4 * side + k]))
    for c in copies:
        c.start()
    for c in copies:
        c.wait()
    half = lane_of() < HALF
    for p in range(groups // 2):
        weight_lanes[p : p + 1, :] = jnp.where(half, weights[2 * p], weights[2 * p + 1])
    lane = lane_of(HALO) % HALF
    for side, (out, lo, at_end) in enumerate(sides):
        op_buf, old_buf, dens_buf, mat_buf = scratch[4 * side : 4 * side + 4]
        dens = dens_buf[...]
        for g in range(groups):
            part = op_buf[g].astype(jnp.float32)
            out[g] = jnp.where(at_end, part[HALO:], part[:HALO]) * dens
            out[groups + g] = old_buf[g]
        out[2 * groups] = dens
        out[2 * groups + 1] = mat_buf[...]
        place = jnp.where(at_end, 0, rows + HALO)
        vec = jnp.zeros((HALO, LANES), jnp.float32)
        for i in range(HALO):
            vec = jnp.where(lane == place + i, flux[lo + i], vec)
        for at_lane in range(0, out.shape[2], LANES):
            out[2 * groups + 2, :, at_lane : at_lane + LANES] = vec


def turn_kernel(
    groups, rows, cols, opacity, old, density, material, got_second, got_first,
    a_ref, e_ref, dens_ref, mat_ref, flux_ref, to_first, to_second,
):
    pairs = groups // 2
    plane_of_flux = 2 * groups + 2
    flux_ref[...] = got_first[plane_of_flux, :, :LANES] + got_second[plane_of_flux, :, :LANES]
    even, _, _ = partner("radius", 0, 0)
    for lo in range(0, cols, LANES):
        hi = lo + LANES

        def tile(plane, own):
            one, two = got_first[plane, :, lo:hi], got_second[plane, :, lo:hi]
            return jnp.concatenate([jnp.where(even, two, one), own, jnp.where(even, one, two)], axis=0)

        d = tile(2 * groups, density[:, lo:hi])
        d = jnp.concatenate([d, d], axis=0).T
        m = tile(2 * groups + 1, material[:, lo:hi])
        m = jnp.concatenate([m, m], axis=0).T
        dens_ref[HALO + lo : HALO + hi, :] = d
        mat_ref[HALO + lo : HALO + hi, :] = m

        def one(p, carry):
            both = []
            for h in range(2):
                g = 2 * p + h
                both.append(tile(g, opacity[g, :, lo:hi].astype(jnp.float32) * density[:, lo:hi]))
            a = jnp.concatenate(both, axis=0).T
            a_ref[p, HALO + lo : HALO + hi, :] = jnp.where(dens_ref[HALO + lo : HALO + hi, :] > 0.0, a, 1.0)
            both = [tile(groups + 2 * p + h, old[2 * p + h, :, lo:hi]) for h in range(2)]
            e_ref[p, HALO + lo : HALO + hi, :] = jnp.concatenate(both, axis=0).T
            return carry

        lax.fori_loop(0, pairs, one, 0, unroll=8)
    _, lo_first, lo_second = partner("polar", cols, HALO)
    for out, lo in ((to_first, lo_first), (to_second, lo_second)):
        edge = pl.ds(pl.multiple_of(lo, HALO), HALO)
        for p in range(pairs):
            out[p] = a_ref[p, edge, :]
            out[pairs + p] = e_ref[p, edge, :]
        out[2 * pairs] = dens_ref[edge, :]
        out[2 * pairs + 1] = mat_ref[edge, :]


def next_row(v):
    return pltpu.roll(v, LANES - 1, 1)


def prev_row(v):
    return pltpu.roll(v, 1, 1)


def after(ref, lead, lo, hi, here, end):
    if hi < end:
        return ref[(*lead, slice(lo + 1, hi + 1), slice(None))]
    return pltpu.roll(here, hi - lo - 1, 0)


def before(ref, lead, lo, hi, here, begin):
    if lo > begin:
        return ref[(*lead, slice(lo - 1, hi - 1), slice(None))]
    return pltpu.roll(here, 1, 0)


def at(lo, hi):
    return (slice(lo, hi), slice(None))


def flux_sum(p, lo, hi, v_ref, v, fr_ref, fp_ref, span):
    begin, end = span
    fp = fp_ref[(p, *at(lo, hi))]
    fp_before = before(fp_ref, (p,), lo, hi, fp, begin)
    polar = fp * (v - after(v_ref, (p,), lo, hi, v, end)) + fp_before * (
        v - before(v_ref, (p,), lo, hi, v, begin)
    )
    fr = fr_ref[(p, *at(lo, hi))] * (v - next_row(v))
    return polar + (fr - prev_row(fr))


def tile_sum(v):
    acc = v[:HALO]
    for lo in range(HALO, v.shape[0], HALO):
        acc = acc + v[lo : lo + HALO]
    return acc


def krylov(p, pairs, parts, span, own, b_ref, fr_ref, fp_ref, r_ref, q_ref, t_ref, mom, old_mom=None):
    sums = [jnp.zeros((HALO, LANES), jnp.float32) for _ in range(4)]
    for lo, hi in parts:
        r = r_ref[(p, *at(lo, hi))]
        q = b_ref[(p, *at(lo, hi))] * r + flux_sum(p, lo, hi, r_ref, r, fr_ref, fp_ref, span)
        q_ref[(p, *at(lo, hi))] = q
        if lo >= own[0] and hi <= own[1]:
            sums[0] = sums[0] + tile_sum(r * r)
            sums[1] = sums[1] + tile_sum(r * q)
            sums[2] = sums[2] + tile_sum(q * q)
    for lo, hi in parts:
        inside = lo >= own[0] and hi <= own[1]
        if not inside and t_ref is None:
            continue
        q = q_ref[(p, *at(lo, hi))]
        t = b_ref[(p, *at(lo, hi))] * q + flux_sum(p, lo, hi, q_ref, q, fr_ref, fp_ref, span)
        if t_ref is not None:
            t_ref[(p, *at(lo, hi))] = t
        if inside:
            sums[3] = sums[3] + tile_sum(q * t)
    for k in range(4):
        total = jnp.sum(sums[k], axis=0, keepdims=True)
        if old_mom is not None:
            total = total + old_mom[pl.ds(k * pairs + p, 1), :]
        mom[pl.ds(k * pairs + p, 1), :] = total


def send_moments(pairs, rows, mom, out, row_sums):
    lane = lane_of(4 * pairs)
    x = mom[...]
    first = jnp.where((lane >= HALO) & (lane < HALO + rows), x, 0.0)
    second = jnp.where((lane >= HALF + HALO) & (lane < HALF + HALO + rows), x, 0.0)
    both = jnp.concatenate([first, second, jnp.zeros((LANES - 8 * pairs, LANES), jnp.float32)], axis=0)
    line = lax.dot_general(
        jnp.ones((HALO, LANES), jnp.float32), both, (((1,), (1,)), ((), ())),
        precision=HIGHEST, preferred_element_type=jnp.float32,
    )
    if row_sums is not None:
        line = jnp.where(lane_of(HALO) < HALF, line, row_sums)
    for lo in range(0, out.shape[0], HALO):
        out[lo : lo + HALO, :] = line


def weight_of(weights, p):
    return weights[pl.ds(p, 1), :]


def fold(s):
    s = s + pltpu.roll(s, HALF, 1)
    middle = s.shape[0] // 2
    return jnp.where(lane_of(middle) < HALF, s[:middle], s[middle:])


def unfold(s):
    other = pltpu.roll(s, HALF, 1)
    low = lane_of(s.shape[0]) < HALF
    return jnp.where(low, s, other), jnp.where(low, other, s)


def first_residual(p, w, inverse_parts, parts, span, dens_ref, mat_ref, a_ref, e_ref, fr_ref, fp_ref, r_ref, inv):
    begin, end = span
    for lo, hi in inverse_parts:
        a, e = a_ref[(p, *at(lo, hi))], e_ref[(p, *at(lo, hi))]
        slope_r = next_row(e) - prev_row(e)
        slope_p = after(e_ref, (p,), lo, hi, e, end) - before(e_ref, (p,), lo, hi, e, begin)
        n2 = slope_r * slope_r + slope_p * slope_p
        u = a * e
        s = 4.0 * u + n2 * lax.rsqrt(n2 + 1e-37)
        inv[lo:hi, :] = jnp.where(dens_ref[lo:hi, :] > 0.0, (n2 + 6.0 * u * s) / (e * s), OUTSIDE)
    for lo, hi in parts:
        d = inv[lo:hi, :]
        fr_ref[(p, *at(lo, hi))] = 4.0 / (d + next_row(d))
        fp_ref[(p, *at(lo, hi))] = 4.0 / (d + after(inv, (), lo, hi, d, end))
    for lo, hi in parts:
        a, e = a_ref[(p, *at(lo, hi))], e_ref[(p, *at(lo, hi))]
        r_ref[(p, *at(lo, hi))] = a * (w * mat_ref[lo:hi, :] - e) - flux_sum(
            p, lo, hi, e_ref, e, fr_ref, fp_ref, span
        )


def inner_kernel(
    groups, cols, weights, a_ref, e_ref, dens_ref, mat_ref,
    fr_ref, fp_ref, r_ref, q_ref, t_ref, b_ref, mom, inv,
):
    pairs = groups // 2
    span = (HALO, HALO + cols)
    parts = [(lo + HALO, hi + HALO) for lo, hi in pieces(cols)]
    own = (2 * HALO, cols)

    def one(p, carry):
        w = weight_of(weights, p)
        for lo, hi in parts:
            b_ref[(p, *at(lo, hi))] = 1.0 + a_ref[(p, *at(lo, hi))]
        first_residual(p, w, parts, parts, span, dens_ref, mat_ref, a_ref, e_ref, fr_ref, fp_ref, r_ref, inv)
        krylov(p, pairs, parts, span, own, b_ref, fr_ref, fp_ref, r_ref, q_ref, t_ref, mom)
        return carry

    lax.fori_loop(0, pairs, one, 0, unroll=2)


def frame_kernel(groups, rows, cols, weights, got_second, got_first, old_mom, *rest):
    a_ref, e_ref, fr_ref, fp_ref, r_ref, q_ref, t_ref, b_ref, dens_ref, mat_ref = rest[10:20]
    out, inv, mom = rest[20:]
    pairs = groups // 2
    tall = cols + 2 * HALO
    span = (0, tall)
    even, _, _ = partner("polar", 0, 0)
    ends = ((0, HALO), (tall - HALO, tall))

    def halo(side, plane):
        one, two = got_first[plane], got_second[plane]
        return jnp.where(even, two, one) if side == 0 else jnp.where(even, one, two)

    for side, (lo, hi) in enumerate(ends):
        dens_ref[lo:hi, :] = halo(side, 2 * pairs)
        mat_ref[lo:hi, :] = halo(side, 2 * pairs + 1)
    parts = [(0, HALO), (HALO, 2 * HALO), (cols, cols + HALO), (cols + HALO, tall)]
    inverse_parts = parts[:2] + [(2 * HALO, 3 * HALO)] + parts[2:]

    def one(p, carry):
        w = weight_of(weights, p)
        for side, (lo, hi) in enumerate(ends):
            a = jnp.where(dens_ref[lo:hi, :] > 0.0, halo(side, p), 1.0)
            a_ref[(p, *at(lo, hi))] = a
            b_ref[(p, *at(lo, hi))] = 1.0 + a
            e_ref[(p, *at(lo, hi))] = halo(side, pairs + p)
        first_residual(
            p, w, inverse_parts, parts, span, dens_ref, mat_ref, a_ref, e_ref, fr_ref, fp_ref, r_ref, inv
        )
        krylov(
            p, pairs, parts, span, (HALO, HALO + cols), b_ref, fr_ref, fp_ref, r_ref, q_ref, t_ref, mom, old_mom
        )
        return carry

    lax.fori_loop(0, pairs, one, 0, unroll=8)
    row_sums = jnp.sum(tile_sum(dens_ref[HALO : HALO + cols, :]), axis=0, keepdims=True)
    send_moments(pairs, rows, mom, out, row_sums)


def steps(pairs, gathered):
    total = jnp.sum(gathered[...], axis=0, keepdims=True)
    lane = lane_of(pairs)
    sub = lax.broadcasted_iota(jnp.int32, (pairs, LANES), 0)

    def moment(k):
        first, second = (
            jnp.sum(jnp.where(lane == sub + (4 * h + k) * pairs, total, 0.0), axis=1, keepdims=True)
            for h in range(2)
        )
        return jnp.where(lane < HALF, first, second)

    m0, m1, m2, m3 = (moment(k) for k in range(4))
    k1, k2, k3 = m1 / m0, m2 / m0, m3 / m0
    first = 1.0 / k1
    det = jnp.maximum(k2 - k1 * k1, 0.0)
    beta = det / (k1 * k1)
    low = k1 * k3 - k2 * k2
    second = jnp.minimum(jnp.where(low > 0.0, k1 * det / low, 0.0), 1.0)
    return first + second * (1.0 + beta), first * second


def absorbed(pairs, c1, c2, a_ref, e_ref, r_ref, q_ref, e_out, s, weights=None, emit=None):
    tall = a_ref.shape[1]
    for lo, hi in pieces(tall):
        total = emitted = jnp.zeros((hi - lo, LANES), jnp.float32)
        for p in range(pairs):
            a = a_ref[(p, *at(lo, hi))]
            e = (
                e_ref[(p, *at(lo, hi))]
                + c1[p : p + 1, :] * r_ref[(p, *at(lo, hi))]
                - c2[p : p + 1, :] * q_ref[(p, *at(lo, hi))]
            )
            e_out[(p, *at(lo, hi))] = e
            total = total + a * e
            if emit is not None:
                emitted = emitted + a * weight_of(weights, p)
        s[lo:hi, :] = total
        if emit is not None:
            emit[lo:hi, :] = emitted


def update_kernel(pairs, first, weights, gathered, a_ref, e_ref, r_ref, q_ref, e_out, s_out, c1_ref, c2_ref, s, emit):
    c1, c2 = steps(pairs, gathered)
    c1_ref[...] = c1
    c2_ref[...] = c2
    if first:
        absorbed(pairs, c1, c2, a_ref, e_ref, r_ref, q_ref, e_out, s, weights, emit)
        s_out[1] = fold(emit[...])
    else:
        absorbed(pairs, c1, c2, a_ref, e_ref, r_ref, q_ref, e_out, s)
    s_out[0] = fold(s[...])


def turned_back(v, rows):
    parts = [v[lo : lo + LANES].T[HALO : HALO + rows] for lo in range(0, v.shape[0], LANES)]
    return jnp.concatenate(parts, axis=1)


def last_update_kernel(pairs, rows, cols, gathered, a_ref, e_ref, r_ref, q_ref, e_out, s_out, s):
    c1, c2 = steps(pairs, gathered)
    absorbed(pairs, c1, c2, a_ref, e_ref, r_ref, q_ref, e_out, s)
    total = s[HALO : HALO + cols, :]
    s_out[...] = turned_back(total + pltpu.roll(total, HALF, 1), rows)


def energy_kernel(pairs, rows, cols, e_ref, fixed, capacity, out, fixed_out, capacity_out):
    def one(p, carry):
        for lo in range(0, cols, LANES):
            block = e_ref[p, HALO + lo : HALO + lo + LANES, :].T
            out[2 * p, :, lo : lo + LANES] = block[HALO : HALO + rows]
            out[2 * p + 1, :, lo : lo + LANES] = block[HALF + HALO : HALF + HALO + rows]
        return carry

    lax.fori_loop(0, pairs, one, 0, unroll=4)
    fixed_out[...] = turned_back(fixed[HALO : HALO + cols, :], rows)
    capacity_out[...] = turned_back(capacity[HALO : HALO + cols, :], rows)


def heating_kernel(
    groups, rows, cols, polar_count, flux, gathered, dens_ref, mat_ref, flux_ref, column_out, fixed_out
):
    tall = dens_ref.shape[0]
    radius, polar = lax.axis_index("radius"), lax.axis_index("polar")
    dens = dens_ref[...]
    row_id = lax.broadcasted_iota(jnp.int32, gathered.shape, 0)
    ahead = (row_id >= radius * polar_count) & (row_id < radius * polar_count + polar)
    carried = jnp.sum(jnp.where(ahead, gathered[...], 0.0), axis=0, keepdims=True)
    lane = lane_of()
    carried = jnp.where(lane < HALF, pltpu.roll(carried, HALF, 1), carried)
    dst = lax.broadcasted_iota(jnp.int32, (tall, tall), 0)
    src = lax.broadcasted_iota(jnp.int32, (tall, tall), 1)
    coeff = jnp.where(
        (src >= HALO) & (src <= dst), 1.0, jnp.where((src < HALO) & (src > dst), -1.0, 0.0)
    )
    within = lax.dot_general(
        coeff, dens, (((1,), (0,)), ((), ())), precision=HIGHEST, preferred_element_type=jnp.float32
    )
    column = 2.0 / (cols * polar_count) * (carried + within)
    vec = flux_ref[0:1, :]
    for i in range(rows):
        vec = jnp.where(lane % HALF == HALO + i, flux[i], vec)
    fixed_out[...] = 16.0 * dens * mat_ref[...] + vec * dens * jnp.exp(-column)
    column_out[...] = turned_back(column[HALO : HALO + cols], rows)


def summed(refs, lead=()):
    total = refs[0][(*lead, ...)]
    for s in refs[1:]:
        total = total + s[(*lead, ...)]
    return total


def next_kernel(groups, rows, count, turn, last, weights, c1_ref, c2_ref, a_ref, b_ref, fr_ref, fp_ref, r_in, q_in, t_in, fixed, cap_in, mat_ref, *rest):
    pairs = groups // 2
    sums = rest[:count]
    rest = rest[count:]
    outs, (delta, mom) = rest[:-2], rest[-2:]
    r_ref, q_ref, out, *outs = outs
    t_ref = None if last else outs.pop(0)
    m_ref = None if last else outs.pop(0)
    tall = fixed.shape[0]
    parts = pieces(tall)
    half = tall // 2
    folded = summed(sums, (0,))
    if turn == 0:
        cap_out = outs.pop(0)
        dens = cap_in[...]
        emits = jnp.concatenate(unfold(summed(sums, (1,))), axis=0)
        cap_out[...] = 16.0 * jnp.where(dens > 0.0, dens, 1.0) + emits
        cap_in = cap_out
    for k, total in enumerate(unfold(folded)):
        here = at(k * half, (k + 1) * half)
        nxt = (fixed[here] + total) / cap_in[here]
        delta[here] = nxt - mat_ref[here]
        if m_ref is not None:
            m_ref[here] = nxt

    def one(p, carry):
        w = weight_of(weights, p)
        c1 = c1_ref[pl.ds(p, 1), :]
        c2 = c2_ref[pl.ds(p, 1), :]
        for lo, hi in parts:
            here = (p, *at(lo, hi))
            r_ref[here] = (
                r_in[here] - c1 * q_in[here] + c2 * t_in[here] + a_ref[here] * (w * delta[lo:hi, :])
            )
        krylov(p, pairs, parts, (0, tall), (HALO, tall - HALO), b_ref, fr_ref, fp_ref, r_ref, q_ref, t_ref, mom)
        return carry

    lax.fori_loop(0, pairs, one, 0, unroll=2)
    send_moments(pairs, rows, mom, out, None)


def material_kernel(fixed, capacity, *rest):
    sums, out = rest[:-1], rest[-1]
    out[...] = (fixed[...] + summed(sums)) / capacity[...]


def spread(part, axis):
    count = lax.axis_size(axis)
    return [part] + [lax.ppermute(part, axis, [(i, i ^ s) for i in range(count)]) for s in range(1, count)]


def pair_up(first, axis):
    return lax.ppermute(first, axis, [(i, i ^ 1) for i in range(lax.axis_size(axis))])


def pair_across(second, axis):
    links = [(i, i + 1) for i in range(1, lax.axis_size(axis) - 1, 2)]
    return lax.ppermute(second, axis, links + [(j, i) for i, j in links])


def per_device(density, opacity, radiation_old, material_old, weights, stellar_flux):
    groups, rows, cols = opacity.shape
    pairs, tall = groups // 2, cols + 2 * HALO
    assert rows + 2 * HALO == HALF
    polar_count = lax.axis_size("polar")
    count = lax.axis_size("group")
    devices = lax.axis_size("radius") * polar_count
    planes = 2 * groups + 3
    big, flat, core = (pairs, tall, LANES), (tall, LANES), (cols, LANES)
    line = (devices, LANES)
    edge = (2 * pairs + 2, HALO, LANES)
    vmem = lambda shape: pltpu.VMEM(shape, jnp.float32)

    strips = [
        pltpu.VMEM((groups, 2 * HALO, cols), jnp.bfloat16),
        vmem((groups, HALO, cols)),
        vmem((HALO, cols)),
        vmem((HALO, cols)),
    ]
    first, second, weights = call(
        functools.partial(pack_rows_kernel, groups, rows),
        [(planes, HALO, cols)] * 2 + [(pairs, LANES)],
        tuple(
            pltpu.with_memory_space_constraint(v, pltpu.HBM)
            for v in (weights, stellar_flux, opacity, radiation_old, density, material_old)
        ),
        [hspec()] * 6,
        scratch=strips * 2
        + [pltpu.SMEM((size,), jnp.float32) for size in (groups, rows)]
        + [pltpu.SemaphoreType.DMA((10,))],
        name="pack_rows",
        limit=20 * 1024 * 1024,
    )
    second = pair_across(second, "radius")
    first = pair_up(first, "radius")
    a, e, dens, mat, flux_lanes, first, second = call(
        functools.partial(turn_kernel, groups, rows, cols),
        [big] * 2 + [flat, flat, (HALO, LANES), edge, edge],
        (opacity, radiation_old, density, material_old, second, first),
        [vspec()] * 6,
        name="turn",
    )
    second = pair_across(second, "polar")
    first = pair_up(first, "polar")
    fr, fp, r, q, t, b, mom = call(
        functools.partial(inner_kernel, groups, cols),
        [big] * 6 + [(4 * pairs, LANES)],
        (weights, a, e, dens, mat),
        [vspec()] * 5,
        scratch=[vmem(flat)],
        name="inner",
    )
    a, e, fr, fp, r, q, t, b, dens, mat, out = call(
        functools.partial(frame_kernel, groups, rows, cols),
        [big] * 8 + [flat, flat, line],
        (weights, second, first, mom, a, e, fr, fp, r, q, t, b, dens, mat),
        [vspec()] * 14,
        scratch=[vmem(flat), vmem((4 * pairs, LANES))],
        name="frame",
        aliases={4 + k: k for k in range(10)},
    )
    capacity = dens
    for turn in range(ITERS):
        gathered = lax.all_to_all(out, ("radius", "polar"), 0, 0, tiled=True)
        if turn + 1 == ITERS:
            e, part = call(
                functools.partial(last_update_kernel, pairs, rows, cols),
                [big, (rows, cols)],
                (gathered, a, e, r, q),
                [vspec()] * 5,
                scratch=[vmem(flat)],
                name="last_update",
            )
            sums = spread(part, "group")
            energy, fixed, capacity = call(
                functools.partial(energy_kernel, pairs, rows, cols),
                [(groups, rows, cols), (rows, cols), (rows, cols)],
                (e, fixed, capacity),
                [vspec()] * 3,
                name="energy",
            )
            (mat,) = call(
                material_kernel,
                [(rows, cols)],
                (fixed, capacity, *sums),
                [vspec()] * (2 + count),
                name="material",
            )
            break
        first, last = turn == 0, turn + 2 == ITERS
        e, part, c1, c2 = call(
            functools.partial(update_kernel, pairs, first),
            [big, (2 if first else 1, tall // 2, LANES), (pairs, LANES), (pairs, LANES)],
            (weights, gathered, a, e, r, q),
            [vspec()] * 6,
            scratch=[vmem(flat)] * 2,
            name="update",
        )
        sums = spread(part, "group")
        if first:
            column, fixed = call(
                functools.partial(heating_kernel, groups, rows, cols, polar_count),
                [(rows, cols), flat],
                (stellar_flux, gathered, dens, mat, flux_lanes),
                [sspec()] + [vspec()] * 4,
                name="heating",
            )
        r, q, out, *more = call(
            functools.partial(next_kernel, groups, rows, count, turn, last),
            [big, big, line] + ([] if last else [big, flat]) + ([flat] if first else []),
            (weights, c1, c2, a, b, fr, fp, r, q, t, fixed, capacity, mat, *sums),
            [vspec()] * (13 + count),
            scratch=[vmem(flat), vmem((4 * pairs, LANES))],
            name="next",
        )
        if not last:
            t, mat, *more = more
        if first:
            (capacity,) = more
    return (energy, mat, column)


def solution(mesh):
    return jax.shard_map(
        per_device,
        mesh=mesh,
        in_specs=(
            P("radius", "polar"),
            P("group", "radius", "polar"),
            P("group", "radius", "polar"),
            P("radius", "polar"),
            P("group"),
            P("radius"),
        ),
        out_specs=(P("group", "radius", "polar"), P("radius", "polar"), P("radius", "polar")),
        check_vma=False,
    )
```

```python
import functools
import jax
import jax.numpy as jnp
from jax import lax
from jax.experimental import pallas as pl
from jax.experimental.pallas import tpu as pltpu
from jax.sharding import PartitionSpec as P


ITERS = 3
HALO = 8
LANES = 128
HALF = LANES // 2
STEP = 16
VMEM_LIMIT = 12 * 1024 * 1024
HIGHEST = lax.Precision.HIGHEST
OUTSIDE = 1.6e38


def vspec():
    return pl.BlockSpec(memory_space=pltpu.VMEM)


def sspec():
    return pl.BlockSpec(memory_space=pltpu.SMEM)


def hspec():
    return pl.BlockSpec(memory_space=pltpu.HBM)


def call(kernel, outs, args, specs, scratch=(), flops=1000000, nbytes=1000000, name=None, limit=VMEM_LIMIT, aliases=None):
    return pl.pallas_call(
        kernel,
        out_shape=[jax.ShapeDtypeStruct(s, jnp.float32) for s in outs],
        in_specs=specs,
        out_specs=[vspec() for _ in outs],
        scratch_shapes=list(scratch),
        compiler_params=pltpu.CompilerParams(
            vmem_limit_bytes=limit
        ),
        cost_estimate=pl.CostEstimate(flops=flops, bytes_accessed=nbytes, transcendentals=0),
        name=name,
        input_output_aliases=aliases or {},
    )(*args)


def lane_of(height=1):
    return lax.broadcasted_iota(jnp.int32, (height, LANES), 1)


def pieces(tall):
    cuts = [0, HALO]
    while cuts[-1] + STEP < tall - HALO:
        cuts.append(cuts[-1] + STEP)
    cuts += [tall - HALO, tall]
    return list(zip(cuts[:-1], cuts[1:]))


def partner(axis, inner, outer):
    even = lax.rem(lax.axis_index(axis), 2) == 0
    return even, jnp.where(even, inner, outer), jnp.where(even, outer, inner)


def pack_rows_kernel(
    groups, rows, weights_in, flux_in, opacity, old, density, material, first, second, weight_lanes, *scratch
):
    even, lo_first, lo_second = partner("radius", rows - HALO, 0)
    weights, flux, sems = scratch[-3:]
    sides = ((first, lo_first, even), (second, lo_second, jnp.logical_not(even)))
    copies = [
        pltpu.make_async_copy(flux_in, flux, sems.at[8]),
        pltpu.make_async_copy(weights_in, weights, sems.at[9]),
    ]
    for side, (_, lo, at_end) in enumerate(sides):
        op_buf, old_buf, dens_buf, mat_buf = scratch[4 * side : 4 * side + 4]
        lo = pl.multiple_of(lo, HALO)
        base = pl.multiple_of(jnp.where(at_end, rows - 2 * HALO, 0), 2 * HALO)
        moves = (
            (opacity.at[:, pl.ds(base, 2 * HALO), :], op_buf),
            (old.at[:, pl.ds(lo, HALO), :], old_buf),
            (density.at[pl.ds(lo, HALO), :], dens_buf),
            (material.at[pl.ds(lo, HALO), :], mat_buf),
        )
        for k, (src, dst) in enumerate(moves):
            copies.append(pltpu.make_async_copy(src, dst, sems.at[4 * side + k]))
    for c in copies:
        c.start()
    for c in copies:
        c.wait()
    half = lane_of() < HALF
    for p in range(groups // 2):
        weight_lanes[p : p + 1, :] = jnp.where(half, weights[2 * p], weights[2 * p + 1])
    lane = lane_of(HALO) % HALF
    for side, (out, lo, at_end) in enumerate(sides):
        op_buf, old_buf, dens_buf, mat_buf = scratch[4 * side : 4 * side + 4]
        dens = dens_buf[...]
        for g in range(groups):
            part = op_buf[g].astype(jnp.float32)
            out[g] = jnp.where(at_end, part[HALO:], part[:HALO]) * dens
            out[groups + g] = old_buf[g]
        out[2 * groups] = dens
        out[2 * groups + 1] = mat_buf[...]
        place = jnp.where(at_end, 0, rows + HALO)
        vec = jnp.zeros((HALO, LANES), jnp.float32)
        for i in range(HALO):
            vec = jnp.where(lane == place + i, flux[lo + i], vec)
        for at_lane in range(0, out.shape[2], LANES):
            out[2 * groups + 2, :, at_lane : at_lane + LANES] = vec


def turn_kernel(
    groups, rows, cols, opacity, old, density, material, got_second, got_first,
    a_ref, e_ref, dens_ref, mat_ref, flux_ref, to_first, to_second,
):
    pairs = groups // 2
    plane_of_flux = 2 * groups + 2
    flux_ref[...] = got_first[plane_of_flux, :, :LANES] + got_second[plane_of_flux, :, :LANES]
    even, _, _ = partner("radius", 0, 0)
    for lo in range(0, cols, LANES):
        hi = lo + LANES

        def tile(plane, own):
            one, two = got_first[plane, :, lo:hi], got_second[plane, :, lo:hi]
            return jnp.concatenate([jnp.where(even, two, one), own, jnp.where(even, one, two)], axis=0)

        d = tile(2 * groups, density[:, lo:hi])
        d = jnp.concatenate([d, d], axis=0).T
        m = tile(2 * groups + 1, material[:, lo:hi])
        m = jnp.concatenate([m, m], axis=0).T
        dens_ref[HALO + lo : HALO + hi, :] = d
        mat_ref[HALO + lo : HALO + hi, :] = m

        def one(p, carry):
            both = []
            for h in range(2):
                g = 2 * p + h
                both.append(tile(g, opacity[g, :, lo:hi].astype(jnp.float32) * density[:, lo:hi]))
            a = jnp.concatenate(both, axis=0).T
            a_ref[p, HALO + lo : HALO + hi, :] = jnp.where(dens_ref[HALO + lo : HALO + hi, :] > 0.0, a, 1.0)
            both = [tile(groups + 2 * p + h, old[2 * p + h, :, lo:hi]) for h in range(2)]
            e_ref[p, HALO + lo : HALO + hi, :] = jnp.concatenate(both, axis=0).T
            return carry

        lax.fori_loop(0, pairs, one, 0, unroll=8)
    _, lo_first, lo_second = partner("polar", cols, HALO)
    for out, lo in ((to_first, lo_first), (to_second, lo_second)):
        edge = pl.ds(pl.multiple_of(lo, HALO), HALO)
        for p in range(pairs):
            out[p] = a_ref[p, edge, :]
            out[pairs + p] = e_ref[p, edge, :]
        out[2 * pairs] = dens_ref[edge, :]
        out[2 * pairs + 1] = mat_ref[edge, :]


def next_row(v):
    return pltpu.roll(v, LANES - 1, 1)


def prev_row(v):
    return pltpu.roll(v, 1, 1)


def after(ref, lead, lo, hi, here, end):
    if hi < end:
        return ref[(*lead, slice(lo + 1, hi + 1), slice(None))]
    return pltpu.roll(here, hi - lo - 1, 0)


def before(ref, lead, lo, hi, here, begin):
    if lo > begin:
        return ref[(*lead, slice(lo - 1, hi - 1), slice(None))]
    return pltpu.roll(here, 1, 0)


def at(lo, hi):
    return (slice(lo, hi), slice(None))


def flux_sum(p, lo, hi, v_ref, v, fr_ref, fp_ref, span):
    begin, end = span
    fp = fp_ref[(p, *at(lo, hi))]
    fp_before = before(fp_ref, (p,), lo, hi, fp, begin)
    polar = fp * (v - after(v_ref, (p,), lo, hi, v, end)) + fp_before * (
        v - before(v_ref, (p,), lo, hi, v, begin)
    )
    fr = fr_ref[(p, *at(lo, hi))] * (v - next_row(v))
    return polar + (fr - prev_row(fr))


def tile_sum(v):
    acc = v[:HALO]
    for lo in range(HALO, v.shape[0], HALO):
        acc = acc + v[lo : lo + HALO]
    return acc


def krylov(p, pairs, parts, span, own, b_ref, fr_ref, fp_ref, r_ref, q_ref, t_ref, mom, old_mom=None):
    sums = [jnp.zeros((HALO, LANES), jnp.float32) for _ in range(4)]
    for lo, hi in parts:
        r = r_ref[(p, *at(lo, hi))]
        q = b_ref[(p, *at(lo, hi))] * r + flux_sum(p, lo, hi, r_ref, r, fr_ref, fp_ref, span)
        q_ref[(p, *at(lo, hi))] = q
        if lo >= own[0] and hi <= own[1]:
            sums[0] = sums[0] + tile_sum(r * r)
            sums[1] = sums[1] + tile_sum(r * q)
            sums[2] = sums[2] + tile_sum(q * q)
    for lo, hi in parts:
        inside = lo >= own[0] and hi <= own[1]
        if not inside and t_ref is None:
            continue
        q = q_ref[(p, *at(lo, hi))]
        t = b_ref[(p, *at(lo, hi))] * q + flux_sum(p, lo, hi, q_ref, q, fr_ref, fp_ref, span)
        if t_ref is not None:
            t_ref[(p, *at(lo, hi))] = t
        if inside:
            sums[3] = sums[3] + tile_sum(q * t)
    for k in range(4):
        total = jnp.sum(sums[k], axis=0, keepdims=True)
        if old_mom is not None:
            total = total + old_mom[pl.ds(k * pairs + p, 1), :]
        mom[pl.ds(k * pairs + p, 1), :] = total


def send_moments(pairs, rows, mom, out, row_sums):
    lane = lane_of(4 * pairs)
    x = mom[...]
    first = jnp.where((lane >= HALO) & (lane < HALO + rows), x, 0.0)
    second = jnp.where((lane >= HALF + HALO) & (lane < HALF + HALO + rows), x, 0.0)
    both = jnp.concatenate([first, second, jnp.zeros((LANES - 8 * pairs, LANES), jnp.float32)], axis=0)
    line = lax.dot_general(
        jnp.ones((HALO, LANES), jnp.float32), both, (((1,), (1,)), ((), ())),
        precision=HIGHEST, preferred_element_type=jnp.float32,
    )
    if row_sums is not None:
        line = jnp.where(lane_of(HALO) < HALF, line, row_sums)
    for lo in range(0, out.shape[0], HALO):
        out[lo : lo + HALO, :] = line


def weight_of(weights, p):
    return weights[pl.ds(p, 1), :]


def fold(s):
    s = s + pltpu.roll(s, HALF, 1)
    middle = s.shape[0] // 2
    return jnp.where(lane_of(middle) < HALF, s[:middle], s[middle:])


def unfold(s):
    other = pltpu.roll(s, HALF, 1)
    low = lane_of(s.shape[0]) < HALF
    return jnp.where(low, s, other), jnp.where(low, other, s)


def first_residual(p, w, inverse_parts, parts, span, dens_ref, mat_ref, a_ref, e_ref, fr_ref, fp_ref, r_ref, inv):
    begin, end = span
    for lo, hi in inverse_parts:
        a, e = a_ref[(p, *at(lo, hi))], e_ref[(p, *at(lo, hi))]
        slope_r = next_row(e) - prev_row(e)
        slope_p = after(e_ref, (p,), lo, hi, e, end) - before(e_ref, (p,), lo, hi, e, begin)
        n2 = slope_r * slope_r + slope_p * slope_p
        u = a * e
        s = 4.0 * u + n2 * lax.rsqrt(n2 + 1e-37)
        inv[lo:hi, :] = jnp.where(dens_ref[lo:hi, :] > 0.0, (n2 + 6.0 * u * s) / (e * s), OUTSIDE)
    for lo, hi in parts:
        d = inv[lo:hi, :]
        fr_ref[(p, *at(lo, hi))] = 4.0 / (d + next_row(d))
        fp_ref[(p, *at(lo, hi))] = 4.0 / (d + after(inv, (), lo, hi, d, end))
    for lo, hi in parts:
        a, e = a_ref[(p, *at(lo, hi))], e_ref[(p, *at(lo, hi))]
        r_ref[(p, *at(lo, hi))] = a * (w * mat_ref[lo:hi, :] - e) - flux_sum(
            p, lo, hi, e_ref, e, fr_ref, fp_ref, span
        )


def inner_kernel(
    groups, cols, weights, a_ref, e_ref, dens_ref, mat_ref,
    fr_ref, fp_ref, r_ref, q_ref, t_ref, b_ref, mom, inv,
):
    pairs = groups // 2
    span = (HALO, HALO + cols)
    parts = [(lo + HALO, hi + HALO) for lo, hi in pieces(cols)]
    own = (2 * HALO, cols)

    def one(p, carry):
        w = weight_of(weights, p)
        for lo, hi in parts:
            b_ref[(p, *at(lo, hi))] = 1.0 + a_ref[(p, *at(lo, hi))]
        first_residual(p, w, parts, parts, span, dens_ref, mat_ref, a_ref, e_ref, fr_ref, fp_ref, r_ref, inv)
        krylov(p, pairs, parts, span, own, b_ref, fr_ref, fp_ref, r_ref, q_ref, t_ref, mom)
        return carry

    lax.fori_loop(0, pairs, one, 0, unroll=2)


def frame_kernel(groups, rows, cols, weights, got_second, got_first, old_mom, *rest):
    a_ref, e_ref, fr_ref, fp_ref, r_ref, q_ref, t_ref, b_ref, dens_ref, mat_ref = rest[10:20]
    out, inv, mom = rest[20:]
    pairs = groups // 2
    tall = cols + 2 * HALO
    span = (0, tall)
    even, _, _ = partner("polar", 0, 0)
    ends = ((0, HALO), (tall - HALO, tall))

    def halo(side, plane):
        one, two = got_first[plane], got_second[plane]
        return jnp.where(even, two, one) if side == 0 else jnp.where(even, one, two)

    for side, (lo, hi) in enumerate(ends):
        dens_ref[lo:hi, :] = halo(side, 2 * pairs)
        mat_ref[lo:hi, :] = halo(side, 2 * pairs + 1)
    parts = [(0, HALO), (HALO, 2 * HALO), (cols, cols + HALO), (cols + HALO, tall)]
    inverse_parts = parts[:2] + [(2 * HALO, 3 * HALO)] + parts[2:]

    def one(p, carry):
        w = weight_of(weights, p)
        for side, (lo, hi) in enumerate(ends):
            a = jnp.where(dens_ref[lo:hi, :] > 0.0, halo(side, p), 1.0)
            a_ref[(p, *at(lo, hi))] = a
            b_ref[(p, *at(lo, hi))] = 1.0 + a
            e_ref[(p, *at(lo, hi))] = halo(side, pairs + p)
        first_residual(
            p, w, inverse_parts, parts, span, dens_ref, mat_ref, a_ref, e_ref, fr_ref, fp_ref, r_ref, inv
        )
        krylov(
            p, pairs, parts, span, (HALO, HALO + cols), b_ref, fr_ref, fp_ref, r_ref, q_ref, t_ref, mom, old_mom
        )
        return carry

    lax.fori_loop(0, pairs, one, 0, unroll=8)
    row_sums = jnp.sum(tile_sum(dens_ref[HALO : HALO + cols, :]), axis=0, keepdims=True)
    send_moments(pairs, rows, mom, out, row_sums)


def steps(pairs, gathered):
    total = jnp.sum(gathered[...], axis=0, keepdims=True)
    lane = lane_of(pairs)
    sub = lax.broadcasted_iota(jnp.int32, (pairs, LANES), 0)

    def moment(k):
        first, second = (
            jnp.sum(jnp.where(lane == sub + (4 * h + k) * pairs, total, 0.0), axis=1, keepdims=True)
            for h in range(2)
        )
        return jnp.where(lane < HALF, first, second)

    m0, m1, m2, m3 = (moment(k) for k in range(4))
    k1, k2, k3 = m1 / m0, m2 / m0, m3 / m0
    first = 1.0 / k1
    det = jnp.maximum(k2 - k1 * k1, 0.0)
    beta = det / (k1 * k1)
    low = k1 * k3 - k2 * k2
    second = jnp.minimum(jnp.where(low > 0.0, k1 * det / low, 0.0), 1.0)
    return first + second * (1.0 + beta), first * second


def absorbed(pairs, c1, c2, a_ref, e_ref, r_ref, q_ref, e_out, s, weights=None, emit=None, skip=0):
    for lo, hi in pieces(a_ref.shape[1])[skip : len(pieces(a_ref.shape[1])) - skip]:
        total = emitted = jnp.zeros((hi - lo, LANES), jnp.float32)
        for p in range(pairs):
            a = a_ref[(p, *at(lo, hi))]
            e = (
                e_ref[(p, *at(lo, hi))]
                + c1[p : p + 1, :] * r_ref[(p, *at(lo, hi))]
                - c2[p : p + 1, :] * q_ref[(p, *at(lo, hi))]
            )
            e_out[(p, *at(lo, hi))] = e
            total = total + a * e
            if emit is not None:
                emitted = emitted + a * weight_of(weights, p)
        s[lo:hi, :] = total
        if emit is not None:
            emit[lo:hi, :] = emitted


def update_kernel(pairs, first, weights, gathered, a_ref, e_ref, r_ref, q_ref, e_out, s_out, c1_ref, c2_ref, s, emit):
    c1, c2 = steps(pairs, gathered)
    c1_ref[...] = c1
    c2_ref[...] = c2
    if first:
        absorbed(pairs, c1, c2, a_ref, e_ref, r_ref, q_ref, e_out, s, weights, emit)
        s_out[1] = fold(emit[...])
    else:
        absorbed(pairs, c1, c2, a_ref, e_ref, r_ref, q_ref, e_out, s)
    s_out[0] = fold(s[...])


def turned_back(v, rows):
    parts = [v[lo : lo + LANES].T[HALO : HALO + rows] for lo in range(0, v.shape[0], LANES)]
    return jnp.concatenate(parts, axis=1)


def last_update_kernel(pairs, rows, cols, gathered, a_ref, e_ref, r_ref, q_ref, e_out, s_out, s):
    c1, c2 = steps(pairs, gathered)
    absorbed(pairs, c1, c2, a_ref, e_ref, r_ref, q_ref, e_out, s, skip=1)
    total = s[HALO : HALO + cols, :]
    s_out[...] = turned_back(total + pltpu.roll(total, HALF, 1), rows)


def energy_kernel(pairs, rows, cols, e_ref, fixed, capacity, out, fixed_out, capacity_out):
    def one(p, carry):
        for lo in range(0, cols, LANES):
            block = e_ref[p, HALO + lo : HALO + lo + LANES, :].T
            out[2 * p, :, lo : lo + LANES] = block[HALO : HALO + rows]
            out[2 * p + 1, :, lo : lo + LANES] = block[HALF + HALO : HALF + HALO + rows]
        return carry

    lax.fori_loop(0, pairs, one, 0, unroll=4)
    fixed_out[...] = turned_back(fixed[HALO : HALO + cols, :], rows)
    capacity_out[...] = turned_back(capacity[HALO : HALO + cols, :], rows)


def heating_kernel(
    groups, rows, cols, polar_count, flux, gathered, dens_ref, mat_ref, flux_ref, column_out, fixed_out
):
    tall = dens_ref.shape[0]
    radius, polar = lax.axis_index("radius"), lax.axis_index("polar")
    dens = dens_ref[...]
    row_id = lax.broadcasted_iota(jnp.int32, gathered.shape, 0)
    ahead = (row_id >= radius * polar_count) & (row_id < radius * polar_count + polar)
    carried = jnp.sum(jnp.where(ahead, gathered[...], 0.0), axis=0, keepdims=True)
    lane = lane_of()
    carried = jnp.where(lane < HALF, pltpu.roll(carried, HALF, 1), carried)
    dst = lax.broadcasted_iota(jnp.int32, (tall, tall), 0)
    src = lax.broadcasted_iota(jnp.int32, (tall, tall), 1)
    coeff = jnp.where(
        (src >= HALO) & (src <= dst), 1.0, jnp.where((src < HALO) & (src > dst), -1.0, 0.0)
    )
    within = lax.dot_general(
        coeff, dens, (((1,), (0,)), ((), ())), precision=HIGHEST, preferred_element_type=jnp.float32
    )
    column = 2.0 / (cols * polar_count) * (carried + within)
    vec = flux_ref[0:1, :]
    for i in range(rows):
        vec = jnp.where(lane % HALF == HALO + i, flux[i], vec)
    fixed_out[...] = 16.0 * dens * mat_ref[...] + vec * dens * jnp.exp(-column)
    column_out[...] = turned_back(column[HALO : HALO + cols], rows)


def summed(refs, lead=()):
    total = refs[0][(*lead, ...)]
    for s in refs[1:]:
        total = total + s[(*lead, ...)]
    return total


def next_kernel(groups, rows, count, turn, last, weights, c1_ref, c2_ref, a_ref, b_ref, fr_ref, fp_ref, r_in, q_in, t_in, fixed, cap_in, mat_ref, *rest):
    pairs = groups // 2
    sums = rest[:count]
    rest = rest[count:]
    outs, (delta, mom) = rest[:-2], rest[-2:]
    r_ref, q_ref, out, *outs = outs
    t_ref = None if last else outs.pop(0)
    m_ref = None if last else outs.pop(0)
    tall = fixed.shape[0]
    parts = pieces(tall)
    half = tall // 2
    folded = summed(sums, (0,))
    if turn == 0:
        cap_out = outs.pop(0)
        dens = cap_in[...]
        emits = jnp.concatenate(unfold(summed(sums, (1,))), axis=0)
        cap_out[...] = 16.0 * jnp.where(dens > 0.0, dens, 1.0) + emits
        cap_in = cap_out
    for k, total in enumerate(unfold(folded)):
        here = at(k * half, (k + 1) * half)
        nxt = (fixed[here] + total) / cap_in[here]
        delta[here] = nxt - mat_ref[here]
        if m_ref is not None:
            m_ref[here] = nxt

    def one(p, carry):
        w = weight_of(weights, p)
        c1 = c1_ref[pl.ds(p, 1), :]
        c2 = c2_ref[pl.ds(p, 1), :]
        for lo, hi in parts:
            here = (p, *at(lo, hi))
            r_ref[here] = (
                r_in[here] - c1 * q_in[here] + c2 * t_in[here] + a_ref[here] * (w * delta[lo:hi, :])
            )
        krylov(p, pairs, parts, (0, tall), (HALO, tall - HALO), b_ref, fr_ref, fp_ref, r_ref, q_ref, t_ref, mom)
        return carry

    lax.fori_loop(0, pairs, one, 0, unroll=2)
    send_moments(pairs, rows, mom, out, None)


def material_kernel(fixed, capacity, *rest):
    sums, out = rest[:-1], rest[-1]
    out[...] = (fixed[...] + summed(sums)) / capacity[...]


def spread(part, axis):
    count = lax.axis_size(axis)
    return [part] + [lax.ppermute(part, axis, [(i, i ^ s) for i in range(count)]) for s in range(1, count)]


def pair_up(first, axis):
    return lax.ppermute(first, axis, [(i, i ^ 1) for i in range(lax.axis_size(axis))])


def pair_across(second, axis):
    links = [(i, i + 1) for i in range(1, lax.axis_size(axis) - 1, 2)]
    return lax.ppermute(second, axis, links + [(j, i) for i, j in links])


def per_device(density, opacity, radiation_old, material_old, weights, stellar_flux):
    groups, rows, cols = opacity.shape
    pairs, tall = groups // 2, cols + 2 * HALO
    assert rows + 2 * HALO == HALF
    polar_count = lax.axis_size("polar")
    count = lax.axis_size("group")
    devices = lax.axis_size("radius") * polar_count
    planes = 2 * groups + 3
    big, flat, core = (pairs, tall, LANES), (tall, LANES), (cols, LANES)
    line = (devices, LANES)
    edge = (2 * pairs + 2, HALO, LANES)
    vmem = lambda shape: pltpu.VMEM(shape, jnp.float32)

    strips = [
        pltpu.VMEM((groups, 2 * HALO, cols), jnp.bfloat16),
        vmem((groups, HALO, cols)),
        vmem((HALO, cols)),
        vmem((HALO, cols)),
    ]
    first, second, weights = call(
        functools.partial(pack_rows_kernel, groups, rows),
        [(planes, HALO, cols)] * 2 + [(pairs, LANES)],
        tuple(
            pltpu.with_memory_space_constraint(v, pltpu.HBM)
            for v in (weights, stellar_flux, opacity, radiation_old, density, material_old)
        ),
        [hspec()] * 6,
        scratch=strips * 2
        + [pltpu.SMEM((size,), jnp.float32) for size in (groups, rows)]
        + [pltpu.SemaphoreType.DMA((10,))],
        name="pack_rows",
        limit=20 * 1024 * 1024,
    )
    second = pair_across(second, "radius")
    first = pair_up(first, "radius")
    a, e, dens, mat, flux_lanes, first, second = call(
        functools.partial(turn_kernel, groups, rows, cols),
        [big] * 2 + [flat, flat, (HALO, LANES), edge, edge],
        (opacity, radiation_old, density, material_old, second, first),
        [vspec()] * 6,
        name="turn",
    )
    second = pair_across(second, "polar")
    first = pair_up(first, "polar")
    fr, fp, r, q, t, b, mom = call(
        functools.partial(inner_kernel, groups, cols),
        [big] * 6 + [(4 * pairs, LANES)],
        (weights, a, e, dens, mat),
        [vspec()] * 5,
        scratch=[vmem(flat)],
        name="inner",
    )
    a, e, fr, fp, r, q, t, b, dens, mat, out = call(
        functools.partial(frame_kernel, groups, rows, cols),
        [big] * 8 + [flat, flat, line],
        (weights, second, first, mom, a, e, fr, fp, r, q, t, b, dens, mat),
        [vspec()] * 14,
        scratch=[vmem(flat), vmem((4 * pairs, LANES))],
        name="frame",
        aliases={4 + k: k for k in range(10)},
    )
    capacity = dens
    for turn in range(ITERS):
        gathered = lax.all_to_all(out, ("radius", "polar"), 0, 0, tiled=True)
        if turn + 1 == ITERS:
            e, part = call(
                functools.partial(last_update_kernel, pairs, rows, cols),
                [big, (rows, cols)],
                (gathered, a, e, r, q),
                [vspec()] * 5,
                scratch=[vmem(flat)],
                name="last_update",
            )
            sums = spread(part, "group")
            energy, fixed, capacity = call(
                functools.partial(energy_kernel, pairs, rows, cols),
                [(groups, rows, cols), (rows, cols), (rows, cols)],
                (e, fixed, capacity),
                [vspec()] * 3,
                name="energy",
            )
            (mat,) = call(
                material_kernel,
                [(rows, cols)],
                (fixed, capacity, *sums),
                [vspec()] * (2 + count),
                name="material",
            )
            break
        first, last = turn == 0, turn + 2 == ITERS
        e, part, c1, c2 = call(
            functools.partial(update_kernel, pairs, first),
            [big, (2 if first else 1, tall // 2, LANES), (pairs, LANES), (pairs, LANES)],
            (weights, gathered, a, e, r, q),
            [vspec()] * 6,
            scratch=[vmem(flat)] * 2,
            name="update",
        )
        sums = spread(part, "group")
        if first:
            column, fixed = call(
                functools.partial(heating_kernel, groups, rows, cols, polar_count),
                [(rows, cols), flat],
                (stellar_flux, gathered, dens, mat, flux_lanes),
                [sspec()] + [vspec()] * 4,
                name="heating",
            )
        r, q, out, *more = call(
            functools.partial(next_kernel, groups, rows, count, turn, last),
            [big, big, line] + ([] if last else [big, flat]) + ([flat] if first else []),
            (weights, c1, c2, a, b, fr, fp, r, q, t, fixed, capacity, mat, *sums),
            [vspec()] * (13 + count),
            scratch=[vmem(flat), vmem((4 * pairs, LANES))],
            name="next",
        )
        if not last:
            t, mat, *more = more
        if first:
            (capacity,) = more
    return (energy, mat, column)


def solution(mesh):
    return jax.shard_map(
        per_device,
        mesh=mesh,
        in_specs=(
            P("radius", "polar"),
            P("group", "radius", "polar"),
            P("group", "radius", "polar"),
            P("radius", "polar"),
            P("group"),
            P("radius"),
        ),
        out_specs=(P("group", "radius", "polar"), P("radius", "polar"), P("radius", "polar")),
        check_vma=False,
    )
```
